32 devices in a mesh: dp: 8 (over y, x, core), fsdp: 4 (over z).
Axes of the slice: x: 2, y: 2, z: 4, core: 2. Of those that a mesh axis runs over, the one named last changes fastest.
Arguments:
- tokens: bfloat16 [16384, 1024], P(('dp', 'fsdp')), may hold values from -6 to 6
- segment_ids: int32 [32, 512], P(('dp', 'fsdp')), may hold values from 0 to 3, never falling along the last dimension, each value on 1 to 256 neighbouring positions
- decay_rate: float32 [16], replicated, may hold values from 0.0005 to 0.03
- cotangent: bfloat16 [16384, 1024], P(('dp', 'fsdp')), may hold values from -6 to 6
- attn_master: float32 [5, 1024, 1024], P(None, ('dp', 'fsdp')), may hold values from -0.1875 to 0.1875
- ffn_master: float32 [3, 2816, 1024], P(None, ('dp', 'fsdp')), may hold values from -0.1875 to 0.1875
- gains: float32 [3, 1024], P(None, ('dp', 'fsdp')), may hold values from 0.5 to 1.5
- attn_moment: float32 [5, 1024, 1024], P(None, ('dp', 'fsdp')), may hold values from -24 to 24
- ffn_moment: float32 [3, 2816, 1024], P(None, ('dp', 'fsdp')), may hold values from -24 to 24
- gain_first: float32 [3, 1024], P(None, ('dp', 'fsdp')), may hold values from -96 to 96
- gain_second: float32 [3, 1024], P(None, ('dp', 'fsdp')), may hold values from 16 to 4096
Outputs:
- out: bfloat16 [16384, 1024], P(('dp', 'fsdp'))
- x_grad: float32 [16384, 1024], P(('dp', 'fsdp'))
- attn_grad: float32 [5, 1024, 1024], P(None, ('dp', 'fsdp'))
- ffn_grad: float32 [3, 2816, 1024], P(None, ('dp', 'fsdp'))
- gain_grad: float32 [3, 1024], P(None, ('dp', 'fsdp'))
- attn_moment_new: float32 [5, 1024, 1024], P(None, ('dp', 'fsdp'))
- ffn_moment_new: float32 [3, 2816, 1024], P(None, ('dp', 'fsdp'))
- attn_master_new: float32 [5, 1024, 1024], P(None, ('dp', 'fsdp'))
- ffn_master_new: float32 [3, 2816, 1024], P(None, ('dp', 'fsdp'))
- attn_copy: bfloat16 [5, 1024, 1024], P(None, ('dp', 'fsdp'))
- ffn_copy: bfloat16 [3, 2816, 1024], P(None, ('dp', 'fsdp'))
- gains_new: float32 [3, 1024], P(None, ('dp', 'fsdp'))
- gain_first_new: float32 [3, 1024], P(None, ('dp', 'fsdp'))
- gain_second_new: float32 [3, 1024], P(None, ('dp', 'fsdp'))
The draws below stay inside these ranges and needn't reach their ends.
Inputs may be any that keep to these rules, and one draw needn't show every extreme that they name: `segment_ids`: within a pack the ids never fall; each pack holds 4 documents of 1 to 256 tokens, one of exactly 256.
All inputs are finite; a program needn't handle non-finite values.
Results may differ from the reference program's by a relative error of at most 0.012.
The reference program's roundings to bfloat16 on the way count: a program that leaves them out, or rounds other values in their place, can miss the bound.
Values may be sent and summed in bfloat16 or wider, within the bound.
No kernel may reach another device: no remote copies, remote signals or barrier semaphores. Data moves between devices by JAX's collectives and lax.ppermute only.
A program may use at most 256 MiB of HBM per device.

```python
import math
import jax
import jax.numpy as jnp
import numpy as np
from jax import lax

D = 1024
H = 16
FF = 2816
TOK_DEV = 512
DOCS = 4
NS_STEPS = 5
PACKS = 32
TOKENS = 16384


def block_levels(stream_key, shape, cuts, low, top_value):
    level = 1.0
    for axis_at, shards_of in cuts:
        steps = jax.random.uniform(jax.random.fold_in(jax.random.fold_in(stream_key, 6), axis_at), (shards_of,), jnp.float32, low / len(cuts), top_value / len(cuts))
        level = level * jnp.repeat(jnp.exp(steps), shape[axis_at] // shards_of).reshape((-1,) + (1,) * (len(shape) - 1 - axis_at))
    return level


def profile(count, total, reach, slope):
    portions = [(1 << 20) // math.isqrt(standing ** slope) + 1 for standing in range(2, count + 1)]
    spare, holding = total - reach - (count - 1), [1] * (count - 1)
    while spare > 0:
        free = [i for i in range(count - 1) if holding[i] < reach]
        pool, left = sum([portions[i] for i in free]), spare
        for i in free:
            extra = min(reach - holding[i], max(1, left * portions[i] // pool), spare)
            holding[i] = holding[i] + extra
            spare = spare - extra
    return np.array([reach] + holding)


def ragged(stream_key, count, total, limit, slope):
    if count == 2:
        one = jax.random.randint(stream_key, (), max(1, total - limit), min(limit, total - 1) + 1)
        return jnp.stack([one, total - one])
    lengths = jnp.asarray(profile(count, total, limit, slope), jnp.int32)
    couples = (count - 1) // 2
    giver, receiver = lengths[1:1 + 2 * couples:2], lengths[2:2 + 2 * couples:2]
    margin = jnp.minimum(giver - 1, limit - receiver)
    moved = jax.random.randint(jax.random.fold_in(stream_key, 1), (couples,), 0, 1 << 20) % (margin + 1)
    lengths = lengths.at[1:1 + 2 * couples:2].set(giver - moved).at[2:2 + 2 * couples:2].set(receiver + moved)
    return lengths[jax.random.permutation(jax.random.fold_in(stream_key, 2), count)]


def centred(rng, extent, deviation, limit, split=(), kind=jnp.bfloat16):
    array = jax.random.normal(rng, extent, jnp.float32) * deviation
    if len(split) > 0:
        array = block_levels(rng, extent, split, -0.22, 0.18) * array
    return jnp.clip(array, min=-limit, max=limit).astype(kind)


def setup_inputs(seed: int = 0) -> dict:
    arg_keys = jax.random.split(jax.random.key(seed), 12)
    tokens = centred(arg_keys[0], (TOKENS, D), 1.0, 6.0, ((0, 32),))
    segment_ids = jax.vmap(lambda own: jnp.searchsorted(jnp.cumsum(ragged(own, DOCS, TOK_DEV, TOK_DEV // 2, 1)), jnp.arange(TOK_DEV), side="right"))(jax.random.split(arg_keys[1], PACKS)).reshape((PACKS, TOK_DEV)).astype(jnp.int32)
    decay_rate = jnp.clip(jnp.exp(jax.random.uniform(arg_keys[2], (H,), jnp.float32, math.log(0.0005), math.log(0.03))), 0.0005, 0.03)
    cotangent = centred(arg_keys[3], (TOKENS, D), 1.0, 6.0, ((0, 32),))
    attn_master = centred(arg_keys[4], (5, D, D), D ** -0.5, 0.1875, ((1, 32),), jnp.float32)
    ffn_master = centred(arg_keys[5], (3, FF, D), D ** -0.5, 0.1875, ((1, 32),), jnp.float32)
    gains = jnp.clip(1.0 + 0.1 * jax.random.normal(arg_keys[6], (3, D), jnp.float32), 0.5, 1.5)
    attn_moment = centred(arg_keys[7], (5, D, D), 4.0, 24.0, ((1, 32),), jnp.float32)
    ffn_moment = centred(arg_keys[8], (3, FF, D), 4.0, 24.0, ((1, 32),), jnp.float32)
    gain_first = centred(arg_keys[9], (3, D), 16.0, 96.0, ((1, 32),), jnp.float32)
    gain_second = jnp.clip(jnp.exp(math.log(4096.0) - 5.5451774 * jax.random.uniform(arg_keys[10], (3, D), jnp.float32) ** block_levels(arg_keys[10], (3, D), ((1, 32),), -0.2, 0.2)), 16.0, 4096.0)
    return {"tokens": tokens, "segment_ids": segment_ids, "decay_rate": decay_rate, "cotangent": cotangent, "attn_master": attn_master, "ffn_master": ffn_master, "gains": gains, "attn_moment": attn_moment, "ffn_moment": ffn_moment, "gain_first": gain_first, "gain_second": gain_second}


HIGH = lax.Precision.HIGHEST
EPS = 1e-06
NS_EPS = 1e-07
NS_A = 3.4445
NS_B = -4.775
NS_C = 2.0315
LR_MUON = 0.3
LR_GAIN = 0.1
MOMENT_DECAY = 0.5
BETA_ONE = 0.9
BETA_TWO = 0.95
ADAM_EPS = 1e-08

@jax.custom_vjp
def low(v):
    return lax.optimization_barrier(v.astype(jnp.bfloat16)).astype(jnp.float32)

@jax.custom_vjp
def low_back(v):
    return v

def low_keep(v):
    return (low(v), None)

def low_pass(kept, grad):
    return (grad,)

def back_keep(v):
    return (v, None)

def back_low(kept, grad):
    return (low(grad),)
low.defvjp(low_keep, low_pass)
low_back.defvjp(back_keep, back_low)

def rms_scale(series):
    return lax.rsqrt(lax.optimization_barrier(jnp.mean(series * series, axis=-1, keepdims=True)) + EPS)

def layer(inputs, segments, attn_full, ffn_full, gain_full, decay_rate):
    packs, length, model_width = inputs.shape
    head_count = decay_rate.shape[0]
    head_size = model_width // head_count
    normed = low(inputs * rms_scale(inputs) * gain_full[0])

    def project(matrix):
        return jnp.einsum('ptd,ed->pte', normed, matrix, precision=HIGH)
    query_act = low(jax.nn.relu(low_back(project(attn_full[0])))).reshape(packs, length, head_count, head_size)
    key_act = low(jax.nn.relu(low_back(project(attn_full[1])))).reshape(packs, length, head_count, head_size)
    value_act = low(low_back(project(attn_full[2]))).reshape(packs, length, head_count, head_size)
    gate_pre = low_back(project(attn_full[3]))
    scores = low_back(jnp.einsum('pthe,pshe->phts', query_act, key_act, precision=HIGH))
    places = jnp.arange(length, dtype=jnp.int32)
    distance = places[:, None] - places[None, :]
    allowed = (segments[:, :, None] == segments[:, None, :]) & (distance >= 0)[None]
    fading = jnp.exp(-decay_rate[:, None, None] * jnp.maximum(distance, 0).astype(jnp.float32)[None])
    fading_mask = jnp.where(allowed[:, None], fading[None], 0.0)
    weights_low = low(scores * fading_mask)
    attended = low_back(jnp.einsum('phts,pshe->pthe', weights_low, value_act, precision=HIGH).reshape(packs, length, model_width))
    gated_out = low(attended * rms_scale(attended) * gain_full[2] * jax.nn.sigmoid(gate_pre))
    middle = inputs + low_back(jnp.einsum('pte,de->ptd', gated_out, attn_full[4], precision=HIGH))
    normed_two = low(middle * rms_scale(middle) * gain_full[1])
    up_one = low_back(jnp.einsum('ptd,fd->ptf', normed_two, ffn_full[0], precision=HIGH))
    up_two = low_back(jnp.einsum('ptd,fd->ptf', normed_two, ffn_full[1], precision=HIGH))
    product = low(up_one * up_two)
    return middle + low_back(jnp.einsum('ptf,fd->ptd', product, ffn_full[2], precision=HIGH))

def orthogonalize(moment):
    current = moment / (jnp.sqrt(jnp.sum(moment * moment)) + NS_EPS)
    for iteration in range(NS_STEPS):
        gram_sum = jnp.dot(current.T, current, precision=HIGH)
        partial_prod = jnp.dot(current, gram_sum, precision=HIGH)
        current = NS_A * current + NS_B * partial_prod + NS_C * jnp.dot(partial_prod, gram_sum, precision=HIGH)
    return current

def reference(tokens, segment_ids, decay_rate, cotangent, attn_master, ffn_master, gains, attn_moment, ffn_moment, gain_first, gain_second):
    attn_full = low(attn_master)
    ffn_full = low(ffn_master)
    gain_full = low(gains)
    group = math.gcd(PACKS, max(1, 4096 // TOK_DEV))
    inputs = tokens.astype(jnp.float32).reshape(PACKS // group, group, TOK_DEV, D)
    segments = segment_ids.reshape(PACKS // group, group, TOK_DEV)
    checked = jax.checkpoint(layer)

    def whole(values_in, attn_in, ffn_in, gain_in):
        return lax.map(lambda couple: checked(couple[0], couple[1], attn_in, ffn_in, gain_in, decay_rate), (values_in, segments))
    result, pull = jax.vjp(whole, inputs, attn_full, ffn_full, gain_full)
    grad_in, attn_grad, ffn_grad, gain_grad = pull(cotangent.astype(jnp.float32).reshape(inputs.shape))
    out = result.reshape(TOKENS, D).astype(jnp.bfloat16)
    x_grad = grad_in.reshape(TOKENS, D)
    attn_state = MOMENT_DECAY * attn_moment + (1.0 - MOMENT_DECAY) * attn_grad
    ffn_state = MOMENT_DECAY * ffn_moment + (1.0 - MOMENT_DECAY) * ffn_grad
    attn_new = attn_master - LR_MUON * lax.map(orthogonalize, attn_state)
    ffn_new = ffn_master - LR_MUON * math.sqrt(FF / D) * lax.map(orthogonalize, ffn_state)
    first_new = BETA_ONE * gain_first + (1.0 - BETA_ONE) * gain_grad
    second_new = BETA_TWO * gain_second + (1.0 - BETA_TWO) * gain_grad * gain_grad
    gains_new = gains - LR_GAIN * first_new / (jnp.sqrt(second_new) + ADAM_EPS)
    return (out, x_grad, attn_grad, ffn_grad, gain_grad, attn_state, ffn_state, attn_new, ffn_new, attn_new.astype(jnp.bfloat16), ffn_new.astype(jnp.bfloat16), gains_new, first_new, second_new)
```

```python
import math

import jax
import jax.numpy as jnp
from jax import lax
from jax.sharding import PartitionSpec as P

D = 1024
FF = 2816
NS_STEPS = 5


EPS = 1e-06
NS_EPS = 1e-07
NS_A = 3.4445
NS_B = -4.775
NS_C = 2.0315
LR_MUON = 0.3
LR_GAIN = 0.1
MOMENT_DECAY = 0.5
BETA_ONE = 0.9
BETA_TWO = 0.95
ADAM_EPS = 1e-08
F32 = jnp.float32
B16 = jnp.bfloat16
ROWS_BY_ROWS = (((1,), (1,)), ((), ()))
TOKENS_OUT = (((0,), (0,)), ((), ()))


def rms_scale(series):
    return lax.rsqrt(jnp.mean(series * series, axis=-1, keepdims=True) + EPS)


def rms_back(series, factor, upstream):
    return factor * upstream - series * (factor * factor * factor) * jnp.mean(
        upstream * series, axis=-1, keepdims=True
    )


def decay_mask(segments, decay_rate):
    length = segments.shape[0]
    places = jnp.arange(length, dtype=jnp.int32)
    distance = places[:, None] - places[None, :]
    allowed = (segments[:, None] == segments[None, :]) & (distance >= 0)
    fading = jnp.exp(-decay_rate[:, None, None] * jnp.maximum(distance, 0).astype(F32)[None])
    return jnp.where(allowed[None], fading, 0.0)


def forward(tokens, segments, decay_rate, attn_full, ffn_full, gain_low):
    length, model_width = tokens.shape
    head_count = decay_rate.shape[0]
    head_size = model_width // head_count
    hidden = ffn_full.shape[1]
    gain_full = gain_low.astype(F32)
    inputs = tokens.astype(F32)
    first_scale = rms_scale(inputs)
    normed = (inputs * first_scale * gain_full[0]).astype(B16)
    projected = lax.dot_general(
        normed,
        attn_full[:4].reshape(4 * model_width, model_width),
        ROWS_BY_ROWS,
        preferred_element_type=F32,
    )
    query_act = jax.nn.relu(projected[:, :model_width]).astype(B16)
    key_act = jax.nn.relu(projected[:, model_width : 2 * model_width]).astype(B16)
    value_act = projected[:, 2 * model_width : 3 * model_width].astype(B16)
    gate_pre = projected[:, 3 * model_width :]
    fading_mask = decay_mask(segments, decay_rate)
    query_heads = query_act.reshape(length, head_count, head_size)
    key_heads = key_act.reshape(length, head_count, head_size)
    value_heads = value_act.reshape(length, head_count, head_size)
    scores = jnp.einsum("the,she->hts", query_heads, key_heads, preferred_element_type=F32)
    weights_low = (scores * fading_mask).astype(B16)
    attended = jnp.einsum(
        "hts,she->the", weights_low, value_heads, preferred_element_type=F32
    ).reshape(length, model_width)
    out_scale = rms_scale(attended)
    normal_out = attended * out_scale * gain_full[2]
    gate_sig = jax.nn.sigmoid(gate_pre)
    gated_out = (normal_out * gate_sig).astype(B16)
    branch = lax.dot_general(gated_out, attn_full[4], ROWS_BY_ROWS, preferred_element_type=F32)
    middle = inputs + branch
    second_scale = rms_scale(middle)
    normed_two = (middle * second_scale * gain_full[1]).astype(B16)
    up_pair = lax.dot_general(
        normed_two,
        ffn_full[:2].reshape(2 * hidden, model_width),
        ROWS_BY_ROWS,
        preferred_element_type=F32,
    )
    up_one = up_pair[:, :hidden]
    up_two = up_pair[:, hidden:]
    product = (up_one * up_two).astype(B16)
    result = middle + jnp.dot(product, ffn_full[2], preferred_element_type=F32)
    stored = (
        inputs,
        first_scale,
        normed,
        query_act,
        key_act,
        value_act,
        gate_pre,
        fading_mask,
        weights_low,
        attended,
        out_scale,
        normal_out,
        gate_sig,
        gated_out,
        middle,
        second_scale,
        normed_two,
        up_one,
        up_two,
        product,
    )
    return (result.astype(B16), stored)


def backward(stored, cotangent, attn_full, ffn_full, gain_low):
    (
        inputs,
        first_scale,
        normed,
        query_act,
        key_act,
        value_act,
        gate_pre,
        fading_mask,
        weights_low,
        attended,
        out_scale,
        normal_out,
        gate_sig,
        gated_out,
        middle,
        second_scale,
        normed_two,
        up_one,
        up_two,
        product,
    ) = stored
    length, model_width = inputs.shape
    head_count = fading_mask.shape[0]
    head_size = model_width // head_count
    hidden = ffn_full.shape[1]
    gain_full = gain_low.astype(F32)
    grad_out = cotangent.astype(F32)
    grad_product = lax.dot_general(cotangent, ffn_full[2], ROWS_BY_ROWS, preferred_element_type=F32)
    grad_down = lax.dot_general(product, cotangent, TOKENS_OUT, preferred_element_type=F32)
    grad_pair = jnp.concatenate([grad_product * up_two, grad_product * up_one], axis=1).astype(B16)
    grad_normed_two = jnp.dot(
        grad_pair, ffn_full[:2].reshape(2 * hidden, model_width), preferred_element_type=F32
    )
    grad_up = lax.dot_general(
        grad_pair, normed_two, TOKENS_OUT, preferred_element_type=F32
    ).reshape(2, hidden, model_width)
    gain_two = jnp.sum(grad_normed_two * middle * second_scale, axis=0)
    grad_middle = grad_out + rms_back(middle, second_scale, grad_normed_two * gain_full[1])
    middle_low = grad_middle.astype(B16)
    grad_gated = jnp.dot(middle_low, attn_full[4], preferred_element_type=F32)
    grad_outproj = lax.dot_general(middle_low, gated_out, TOKENS_OUT, preferred_element_type=F32)
    grad_normal = grad_gated * gate_sig
    grad_gate = grad_gated * normal_out * gate_sig * (1.0 - gate_sig)
    gain_three = jnp.sum(grad_normal * attended * out_scale, axis=0)
    grad_attended = (
        rms_back(attended, out_scale, grad_normal * gain_full[2])
        .astype(B16)
        .reshape(length, head_count, head_size)
    )
    query_heads = query_act.reshape(length, head_count, head_size)
    key_heads = key_act.reshape(length, head_count, head_size)
    value_heads = value_act.reshape(length, head_count, head_size)
    grad_weights = jnp.einsum(
        "the,she->hts", grad_attended, value_heads, preferred_element_type=F32
    )
    grad_values = jnp.einsum(
        "hts,the->she", weights_low, grad_attended, preferred_element_type=F32
    ).reshape(length, model_width)
    grad_scores = (grad_weights * fading_mask).astype(B16)
    grad_queries = jnp.einsum(
        "hts,she->the", grad_scores, key_heads, preferred_element_type=F32
    ).reshape(length, model_width)
    grad_keys = jnp.einsum(
        "hts,the->she", grad_scores, query_heads, preferred_element_type=F32
    ).reshape(length, model_width)
    grad_mixed = jnp.concatenate(
        [
            jnp.where(query_act > 0, grad_queries, 0.0),
            jnp.where(key_act > 0, grad_keys, 0.0),
            grad_values,
            grad_gate,
        ],
        axis=1,
    ).astype(B16)
    grad_normed = jnp.dot(
        grad_mixed, attn_full[:4].reshape(4 * model_width, model_width), preferred_element_type=F32
    )
    grad_inner = lax.dot_general(
        grad_mixed, normed, TOKENS_OUT, preferred_element_type=F32
    ).reshape(4, model_width, model_width)
    gain_one = jnp.sum(grad_normed * inputs * first_scale, axis=0)
    grad_inputs = grad_middle + rms_back(inputs, first_scale, grad_normed * gain_full[0])
    grad_gain = jnp.stack([gain_one, gain_two, gain_three])
    return (grad_inputs, (grad_inner, grad_outproj, grad_up, grad_down), grad_gain)


def plane_bits():
    return lax.axis_size("dp").bit_length() - 1


def swap_bit(value, bit):
    count = lax.axis_size("dp")
    return lax.ppermute(value, "dp", [(i, i ^ (1 << bit)) for i in range(count)])


def choose(term, dims, bit, other):
    place = (lax.axis_index("dp") >> bit) & 1
    index = 1 - place if other else place
    axis = dims.index(bit)
    return lax.dynamic_index_in_dim(term, index, axis, keepdims=False)


def plane_sum(pieces, order):
    bits = plane_bits()
    terms = [(pieces, list(range(bits))[::-1])]
    for bit in order:
        sent = sum(choose(t, dims, bit, True).astype(F32) for t, dims in terms).astype(B16)
        left = terms[-1][1]
        kept = [(choose(t, dims, bit, False), [b for b in dims if b != bit]) for t, dims in terms]
        received = swap_bit(sent, bit)
        terms = kept + [(received, [b for b in left if b != bit])]
    return sum(t.astype(F32) for t, _ in terms)


def scatter_sum(grad):
    count, rows, columns = grad.shape
    planes, lines = lax.axis_size("dp"), lax.axis_size("fsdp")
    bits = plane_bits()
    own = rows // (planes * lines)
    blocks = grad.astype(B16).reshape((count,) + (2,) * bits + (lines, own, columns))
    blocks = jnp.moveaxis(blocks, 0, bits)
    half = lines // 2
    rest = list(range(1, bits))
    core_first = [0] + rest
    core_back = [0] + rest[::-1]
    one = plane_sum(blocks[..., :half, :, :], core_first)
    two = plane_sum(blocks[..., half:, :, :], core_back)
    mine = jnp.concatenate([one, two], axis=1).astype(B16)
    return lax.psum_scatter(mine, "fsdp", scatter_dimension=1, tiled=True).astype(F32).reshape(count, own, columns)


def gain_sum(grad):
    rows, columns = grad.shape
    total = lax.axis_size("dp") * lax.axis_size("fsdp")
    blocks = jnp.transpose(grad.reshape(rows, total, columns // total), (1, 0, 2))
    return jnp.sum(lax.all_to_all(blocks, ("dp", "fsdp"), 0, 0, tiled=True), axis=0)


def diagonal(size):
    return lax.broadcasted_iota(jnp.int32, (size, size), 0) == lax.broadcasted_iota(jnp.int32, (size, size), 1)


def low_dot(left, right):
    return jnp.dot(left.astype(B16), right.astype(B16), preferred_element_type=F32)


def gram_orthogonalize(rows, gram):
    size = gram.shape[0]
    eye = diagonal(size)
    square = jnp.sum(jnp.where(eye, gram, 0.0))
    norm = jnp.sqrt(square) + NS_EPS
    gram = gram / (norm * norm)
    current = rows.astype(F32) / norm
    for iteration in range(NS_STEPS):
        shift = jnp.sum(jnp.where(eye, gram, 0.0)) / size
        rest = gram - jnp.where(eye, shift, 0.0)
        squared = low_dot(rest, rest) + 2.0 * shift * rest + jnp.where(eye, shift * shift, 0.0)
        factor = NS_A + NS_B * shift + NS_C * shift * shift
        poly = NS_B * gram + NS_C * squared + jnp.where(eye, NS_A - factor, 0.0)
        current = factor * current + low_dot(current, poly)
        if iteration + 1 < NS_STEPS:
            half_way = low_dot(rest, poly) + shift * poly + factor * rest
            gram = (
                low_dot(half_way, poly)
                + (shift * factor) * poly
                + factor * half_way
                + jnp.where(eye, shift * factor * factor, 0.0)
            )
    return current


def one_way(value, bit, lower, both=True):
    count = lax.axis_size("dp")
    start = 1 if lower else 0
    return lax.ppermute(
        value, "dp", [(i, i ^ (1 << bit)) for i in range(count) if (i & 1) == start]
    )


def swap_large(value, bit):
    count = lax.axis_size("dp")
    return lax.ppermute(value, "dp", [(i, i ^ (1 << bit)) for i in range(count) if (i & 1) == 0])


def orthogonal_rows(attn_state, ffn_state):
    lines = lax.axis_size("fsdp")
    attn_count, small, columns = attn_state.shape
    ffn_count, large, _ = ffn_state.shape
    attn_low = attn_state.astype(B16)
    ffn_low = ffn_state.astype(B16)
    at_one = min(lines, attn_count)
    spare = attn_count - at_one
    top = jnp.pad(
        jnp.concatenate([ffn_low, jnp.pad(attn_low[at_one:], ((0, 0), (0, large - small), (0, 0)))]),
        ((0, lines - ffn_count - spare), (0, 0), (0, 0)),
    )
    low_part = jnp.pad(attn_low[:at_one], ((0, lines - at_one), (0, 0), (0, 0)))
    outgoing = jnp.concatenate([top, low_part], axis=1)
    arrived = lax.all_to_all(outgoing, "fsdp", split_axis=0, concat_axis=0, tiled=True)
    big, little = arrived[:, :large], arrived[:, large:]
    big_other = one_way(big, 0, True)
    little_other = one_way(little, 0, False)
    at_core = lax.axis_index("dp") & 1
    block, little_block = lines * large, lines * small
    fill = ((0, block - little_block), (0, 0))
    mine = jnp.stack(
        [
            jnp.where(at_core == 0, big.reshape(block, columns), jnp.pad(little.reshape(little_block, columns), fill)),
            jnp.where(
                at_core == 0,
                big_other.reshape(block, columns),
                jnp.pad(little_other.reshape(little_block, columns), fill),
            ),
        ]
    )
    rest = list(range(1, plane_bits()))
    held = [mine[0:1], mine[1:2]]
    for step in range(len(rest)):
        for color in range(2):
            bit = rest[step] if color == 0 else rest[::-1][step]
            part = held[color]
            came = jnp.concatenate(
                [swap_bit(part[:, :little_block], bit), swap_large(part[:, little_block:], bit)], axis=1
            )
            held[color] = jnp.concatenate([part, came])
    gram = sum(
        lax.dot_general(
            part.reshape(-1, columns), part.reshape(-1, columns), TOKENS_OUT, preferred_element_type=F32
        )
        for part in held
    )
    result = gram_orthogonalize(mine.reshape(2 * block, columns), gram).astype(B16).reshape(2, block, columns)
    own, other = result[0], result[1]
    back_big = one_way(other, 0, False)
    back_little = one_way(other[:little_block], 0, True)
    big_out = jnp.where(at_core == 0, own, back_big).reshape(lines, large, columns)
    little_out = jnp.where(at_core == 0, back_little, own[:little_block]).reshape(lines, small, columns)
    returned = lax.all_to_all(
        jnp.concatenate([big_out, little_out], axis=1), "fsdp", split_axis=0, concat_axis=0, tiled=True
    ).astype(F32)
    attn_out = jnp.concatenate(
        [returned[:at_one, large:], returned[ffn_count : ffn_count + spare, :small]], axis=0
    )
    return attn_out, returned[:ffn_count, :large]


def on_device(
    tokens,
    segment_ids,
    decay_rate,
    cotangent,
    attn_master,
    ffn_master,
    gains,
    attn_moment,
    ffn_moment,
    gain_first,
    gain_second,
):
    attn_low = attn_master.astype(B16)
    ffn_low = ffn_master.astype(B16)
    gain_low = gains.astype(B16)
    attn_full, ffn_full, gain_whole = (
        lax.all_gather(attn_low, ("dp", "fsdp"), axis=1, tiled=True),
        lax.all_gather(ffn_low, ("dp", "fsdp"), axis=1, tiled=True),
        lax.all_gather(gain_low, ("dp", "fsdp"), axis=1, tiled=True),
    )
    out, stored = forward(tokens, segment_ids[0], decay_rate, attn_full, ffn_full, gain_whole)
    x_grad, grads, grad_gain = backward(
        stored, cotangent, attn_full, ffn_full, gain_whole
    )
    grad_inner, grad_outproj, grad_up, grad_down = grads
    down_sum = scatter_sum(grad_down[None])
    up_sum = scatter_sum(grad_up)
    attn_grad = jnp.concatenate([scatter_sum(grad_inner), scatter_sum(grad_outproj[None])], axis=0)
    ffn_grad = jnp.concatenate([up_sum, down_sum], axis=0)
    gain_grad = gain_sum(grad_gain)
    attn_state = MOMENT_DECAY * attn_moment + (1.0 - MOMENT_DECAY) * attn_grad
    ffn_state = MOMENT_DECAY * ffn_moment + (1.0 - MOMENT_DECAY) * ffn_grad
    attn_orth, ffn_orth = orthogonal_rows(attn_state, ffn_state)
    attn_new = attn_master - LR_MUON * attn_orth
    ffn_new = ffn_master - LR_MUON * math.sqrt(FF / D) * ffn_orth
    first_new = BETA_ONE * gain_first + (1.0 - BETA_ONE) * gain_grad
    second_new = BETA_TWO * gain_second + (1.0 - BETA_TWO) * gain_grad * gain_grad
    gains_new = gains - LR_GAIN * first_new / (jnp.sqrt(second_new) + ADAM_EPS)
    return (
        out,
        x_grad,
        attn_grad,
        ffn_grad,
        gain_grad,
        attn_state,
        ffn_state,
        attn_new,
        ffn_new,
        attn_new.astype(B16),
        ffn_new.astype(B16),
        gains_new,
        first_new,
        second_new,
    )


def solution(mesh):
    return jax.shard_map(
        on_device,
        mesh=mesh,
        in_specs=(
            P(("dp", "fsdp"), None),
            P(("dp", "fsdp"), None),
            P(),
            P(("dp", "fsdp"), None),
            P(None, ("dp", "fsdp"), None),
            P(None, ("dp", "fsdp"), None),
            P(None, ("dp", "fsdp")),
            P(None, ("dp", "fsdp"), None),
            P(None, ("dp", "fsdp"), None),
            P(None, ("dp", "fsdp")),
            P(None, ("dp", "fsdp")),
        ),
        out_specs=(
            P(("dp", "fsdp"), None),
            P(("dp", "fsdp"), None),
            P(None, ("dp", "fsdp"), None),
            P(None, ("dp", "fsdp"), None),
            P(None, ("dp", "fsdp")),
            P(None, ("dp", "fsdp"), None),
            P(None, ("dp", "fsdp"), None),
            P(None, ("dp", "fsdp"), None),
            P(None, ("dp", "fsdp"), None),
            P(None, ("dp", "fsdp"), None),
            P(None, ("dp", "fsdp"), None),
            P(None, ("dp", "fsdp")),
            P(None, ("dp", "fsdp")),
            P(None, ("dp", "fsdp")),
        ),
        check_vma=False,
    )
```

```python
import math

import jax
import jax.numpy as jnp
from jax import lax
from jax.experimental import pallas as pl
from jax.experimental.pallas import tpu as pltpu
from jax.sharding import PartitionSpec as P

D = 1024
FF = 2816
NS_STEPS = 5


EPS = 1e-06
NS_EPS = 1e-07
NS_A = 3.4445
NS_B = -4.775
NS_C = 2.0315
LR_MUON = 0.3
LR_GAIN = 0.1
MOMENT_DECAY = 0.5
BETA_ONE = 0.9
BETA_TWO = 0.95
ADAM_EPS = 1e-08
F32 = jnp.float32
B16 = jnp.bfloat16
ROWS_BY_ROWS = (((1,), (1,)), ((), ()))
TOKENS_OUT = (((0,), (0,)), ((), ()))


def rms_scale(series):
    return lax.rsqrt(jnp.mean(series * series, axis=-1, keepdims=True) + EPS)


def rms_back(series, factor, upstream):
    return factor * upstream - series * (factor * factor * factor) * jnp.mean(
        upstream * series, axis=-1, keepdims=True
    )


def decay_mask(segments, decay_rate):
    length = segments.shape[0]
    places = jnp.arange(length, dtype=jnp.int32)
    distance = places[:, None] - places[None, :]
    allowed = (segments[:, None] == segments[None, :]) & (distance >= 0)
    fading = jnp.exp(-decay_rate[:, None, None] * jnp.maximum(distance, 0).astype(F32)[None])
    return jnp.where(allowed[None], fading, 0.0)


def forward(tokens, segments, decay_rate, attn_full, ffn_full, gain_low):
    length, model_width = tokens.shape
    head_count = decay_rate.shape[0]
    head_size = model_width // head_count
    hidden = ffn_full[0].shape[1]
    gain_full = gain_low.astype(F32)
    inputs = tokens.astype(F32)
    first_scale = rms_scale(inputs)
    normed = (inputs * first_scale * gain_full[0]).astype(B16)
    projected = lax.dot_general(
        normed,
        attn_full[0].reshape(4 * model_width, model_width),
        ROWS_BY_ROWS,
        preferred_element_type=F32,
    )
    query_act = jax.nn.relu(projected[:, :model_width]).astype(B16)
    key_act = jax.nn.relu(projected[:, model_width : 2 * model_width]).astype(B16)
    value_act = projected[:, 2 * model_width : 3 * model_width].astype(B16)
    gate_pre = projected[:, 3 * model_width :]
    fading_mask = decay_mask(segments, decay_rate)
    query_heads = query_act.reshape(length, head_count, head_size)
    key_heads = key_act.reshape(length, head_count, head_size)
    value_heads = value_act.reshape(length, head_count, head_size)
    scores = jnp.einsum("the,she->hts", query_heads, key_heads, preferred_element_type=F32)
    weights_low = (scores * fading_mask).astype(B16)
    attended = jnp.einsum(
        "hts,she->the", weights_low, value_heads, preferred_element_type=F32
    ).reshape(length, model_width)
    out_scale = rms_scale(attended)
    normal_out = attended * out_scale * gain_full[2]
    gate_sig = jax.nn.sigmoid(gate_pre)
    gated_out = (normal_out * gate_sig).astype(B16)
    branch = lax.dot_general(gated_out, attn_full[1], ROWS_BY_ROWS, preferred_element_type=F32)
    middle = inputs + branch
    second_scale = rms_scale(middle)
    normed_two = (middle * second_scale * gain_full[1]).astype(B16)
    up_pair = lax.dot_general(
        normed_two,
        ffn_full[0].reshape(2 * hidden, model_width),
        ROWS_BY_ROWS,
        preferred_element_type=F32,
    )
    up_one = up_pair[:, :hidden]
    up_two = up_pair[:, hidden:]
    product = (up_one * up_two).astype(B16)
    stored = (
        inputs,
        first_scale,
        normed,
        query_act,
        key_act,
        value_act,
        gate_pre,
        fading_mask,
        weights_low,
        attended,
        out_scale,
        normal_out,
        gate_sig,
        gated_out,
        middle,
        second_scale,
        normed_two,
        up_one,
        up_two,
        product,
    )
    return stored


def backward(stored, cotangent, attn_full, ffn_full, gain_low):
    (
        inputs,
        first_scale,
        normed,
        query_act,
        key_act,
        value_act,
        gate_pre,
        fading_mask,
        weights_low,
        attended,
        out_scale,
        normal_out,
        gate_sig,
        gated_out,
        middle,
        second_scale,
        normed_two,
        up_one,
        up_two,
        product,
    ) = stored
    length, model_width = inputs.shape
    head_count = fading_mask.shape[0]
    head_size = model_width // head_count
    hidden = ffn_full[0].shape[1]
    gain_full = gain_low.astype(F32)
    grad_out = cotangent.astype(F32)
    grad_down = lax.dot_general(product, cotangent, TOKENS_OUT, preferred_element_type=F32).astype(B16)
    down = Halving(grad_down[None])
    down_out, cotangent = tied([down.payloads()], cotangent)
    down_in = down.swap(down_out)
    grad_product = lax.dot_general(cotangent, ffn_full[1], ROWS_BY_ROWS, preferred_element_type=F32)
    grad_pair = jnp.concatenate([grad_product * up_two, grad_product * up_one], axis=1).astype(B16)
    down_in, grad_pair = tied([down_in], grad_pair)
    down.accept(down_in)
    down_out, grad_pair = tied([down.payloads()], grad_pair)
    down_in = down.swap(down_out)
    grad_up = lax.dot_general(grad_pair, normed_two, TOKENS_OUT, preferred_element_type=F32).astype(B16)
    up = Halving(grad_up.reshape(2, hidden, model_width))
    up_out, grad_pair = tied([up.payloads()], grad_pair)
    up_in = up.swap(up_out)
    grad_normed_two = jnp.dot(
        grad_pair, ffn_full[0].reshape(2 * hidden, model_width), preferred_element_type=F32
    )
    gain_two = jnp.sum(grad_normed_two * middle * second_scale, axis=0)
    grad_middle = grad_out + rms_back(middle, second_scale, grad_normed_two * gain_full[1])
    middle_low = grad_middle.astype(B16)
    down_in, up_in, middle_low = tied([down_in, up_in], middle_low)
    down.accept(down_in)
    up.accept(up_in)
    down_out, up_out, middle_low = tied([down.payloads(), up.payloads()], middle_low)
    down_in, up_in = down.swap(down_out), up.swap(up_out)
    grad_outproj = lax.dot_general(middle_low, gated_out, TOKENS_OUT, preferred_element_type=F32).astype(B16)
    proj = Halving(grad_outproj[None])
    proj_out, middle_low = tied([proj.payloads()], middle_low)
    proj_in = proj.swap(proj_out)
    grad_gated = jnp.dot(middle_low, attn_full[1], preferred_element_type=F32)
    grad_normal = grad_gated * gate_sig
    grad_gate = grad_gated * normal_out * gate_sig * (1.0 - gate_sig)
    gain_three = jnp.sum(grad_normal * attended * out_scale, axis=0)
    grad_attended = (
        rms_back(attended, out_scale, grad_normal * gain_full[2])
        .astype(B16)
        .reshape(length, head_count, head_size)
    )
    query_heads = query_act.reshape(length, head_count, head_size)
    key_heads = key_act.reshape(length, head_count, head_size)
    value_heads = value_act.reshape(length, head_count, head_size)
    grad_weights = jnp.einsum(
        "the,she->hts", grad_attended, value_heads, preferred_element_type=F32
    )
    grad_values = jnp.einsum(
        "hts,the->she", weights_low, grad_attended, preferred_element_type=F32
    ).reshape(length, model_width)
    grad_scores = (grad_weights * fading_mask).astype(B16)
    grad_queries = jnp.einsum(
        "hts,she->the", grad_scores, key_heads, preferred_element_type=F32
    ).reshape(length, model_width)
    grad_keys = jnp.einsum(
        "hts,the->she", grad_scores, query_heads, preferred_element_type=F32
    ).reshape(length, model_width)
    grad_mixed = jnp.concatenate(
        [
            jnp.where(query_act > 0, grad_queries, 0.0),
            jnp.where(key_act > 0, grad_keys, 0.0),
            grad_values,
            grad_gate,
        ],
        axis=1,
    ).astype(B16)
    down_in, up_in, proj_in, grad_mixed = tied([down_in, up_in, proj_in], grad_mixed)
    down.accept(down_in)
    up.accept(up_in)
    proj.accept(proj_in)
    up_out, proj_out, grad_mixed = tied([up.payloads(), proj.payloads()], grad_mixed)
    up_in, proj_in = up.swap(up_out), proj.swap(proj_out)
    grad_inner = lax.dot_general(grad_mixed, normed, TOKENS_OUT, preferred_element_type=F32).astype(B16)
    inner = Halving(grad_inner.reshape(4, model_width, model_width))
    inner_out, grad_mixed = tied([inner.payloads()], grad_mixed)
    inner_in = inner.swap(inner_out)
    grad_normed = jnp.dot(
        grad_mixed, attn_full[0].reshape(4 * model_width, model_width), preferred_element_type=F32
    )
    gain_one = jnp.sum(grad_normed * inputs * first_scale, axis=0)
    grad_inputs = grad_middle + rms_back(inputs, first_scale, grad_normed * gain_full[0])
    grad_gain = jnp.stack([gain_one, gain_two, gain_three])
    up_in, proj_in, inner_in, grad_inputs = tied([up_in, proj_in, inner_in], grad_inputs)
    up.accept(up_in)
    proj.accept(proj_in)
    inner.accept(inner_in)
    return (grad_inputs, (down, up, proj, inner), grad_gain)


def ordered(*values):
    return lax.optimization_barrier(values)


def plane_bits():
    return lax.axis_size("dp").bit_length() - 1


def swap_bit(value, bit):
    count = lax.axis_size("dp")
    return lax.ppermute(value, "dp", [(i, i ^ (1 << bit)) for i in range(count)])


class Halving:
    def __init__(self, grad):
        count, rows, columns = grad.shape
        bits = plane_bits()
        self.chunk = rows // lax.axis_size("dp")
        blocks = grad.reshape((count,) + (2,) * bits + (self.chunk, columns))
        self.parts = [[(blocks, list(range(bits))[::-1])]]
        self.orders = [[0]]

    def choose(self, term, dims, bit, other):
        place = (lax.axis_index("dp") >> bit) & 1
        index = 1 - place if other else place
        return lax.dynamic_index_in_dim(term, index, 1 + dims.index(bit), keepdims=False)

    def payloads(self):
        if self.orders == [[]]:
            rest = list(range(1, plane_bits()))
            half = self.chunk // 2
            self.parts = [
                [(t[..., color * half : (color + 1) * half, :], dims) for t, dims in self.parts[0]]
                for color in range(2)
            ]
            self.orders = [rest, rest[::-1]]
        self.bits = [order[0] for order in self.orders]
        return [
            sum(self.choose(t, dims, bit, True).astype(F32) for t, dims in part).astype(B16)
            for part, bit in zip(self.parts, self.bits)
        ]

    def swap(self, payloads):
        return [swap_bit(value, bit) for value, bit in zip(payloads, self.bits)]

    def accept(self, arrived):
        for color, (part, bit) in enumerate(zip(self.parts, self.bits)):
            left = [b for b in part[0][1] if b != bit]
            self.parts[color] = [(self.choose(t, dims, bit, False), left) for t, dims in part]
            self.parts[color].append((arrived[color], left))
            self.orders[color] = self.orders[color][1:]

    def finish(self):
        while len(self.parts) == 1 or self.orders[0]:
            self.accept(self.swap(self.payloads()))
        return jnp.concatenate([sum(t.astype(F32) for t, _ in part).astype(B16) for part in self.parts], axis=1)


def tied(lists, *values):
    flat = ordered(*[v for part in lists for v in part], *values)
    out, at = [], 0
    for part in lists:
        out.append(list(flat[at : at + len(part)]))
        at += len(part)
    return (*out, *flat[at:])


def gain_sum(grad):
    rows, columns = grad.shape
    total = lax.axis_size("dp") * lax.axis_size("fsdp")
    blocks = jnp.transpose(grad.reshape(rows, total, columns // total), (1, 0, 2))
    return jnp.sum(lax.all_to_all(blocks, ("dp", "fsdp"), 0, 0, tiled=True), axis=0)


NS_ROWS = 256


def polynomial_kernel(gram_ref, rows_ref, out_ref, gram, rest_low, poly, poly_low, current):
    size = gram_ref.shape[0]
    count = rows_ref.shape[0]
    blocks = size // NS_ROWS
    parts = count // 2

    def block(i):
        return pl.ds(pl.multiple_of(i * NS_ROWS, NS_ROWS), NS_ROWS)

    def on_diagonal(i):
        row = lax.broadcasted_iota(jnp.int32, (NS_ROWS, size), 0) + i * NS_ROWS
        return row == lax.broadcasted_iota(jnp.int32, (NS_ROWS, size), 1)

    def trace_of(ref):
        def add(i, total):
            return total + jnp.sum(jnp.where(on_diagonal(i), ref[block(i), :], 0.0))

        return lax.fori_loop(0, blocks, add, jnp.float32(0.0))

    square = jnp.full((1, 1), trace_of(gram_ref), F32)
    norm = jnp.sqrt(square) + NS_EPS
    scale = 1.0 / norm

    def start(i, carry):
        gram[block(i), :] = gram_ref[block(i), :] * (scale * scale)
        return carry

    lax.fori_loop(0, blocks, start, 0)
    current[...] = rows_ref[...].astype(F32) * scale

    def step(iteration, trace):
        shift = trace / size
        factor = NS_A + NS_B * shift + NS_C * shift * shift

        def low_rest(i, carry):
            rest_low[block(i), :] = (gram[block(i), :] - jnp.where(on_diagonal(i), shift, 0.0)).astype(B16)
            return carry

        lax.fori_loop(0, blocks, low_rest, 0)

        def polynomial(i, carry):
            eye = on_diagonal(i)
            own = gram[block(i), :]
            rest = own - jnp.where(eye, shift, 0.0)
            squared = jnp.dot(rest_low[block(i), :], rest_low[...], preferred_element_type=F32)
            squared = squared + 2.0 * shift * rest + jnp.where(eye, shift * shift, 0.0)
            value = NS_B * own + NS_C * squared + jnp.where(eye, NS_A - factor, 0.0)
            poly[block(i), :] = value
            poly_low[block(i), :] = value.astype(B16)
            return carry

        lax.fori_loop(0, blocks, polynomial, 0)

        def apply(i, carry):
            where = pl.ds(pl.multiple_of(i * parts, parts), parts)
            value = current[where, :]
            current[where, :] = factor * value + jnp.dot(
                value.astype(B16), poly_low[...], preferred_element_type=F32
            )
            return carry

        lax.fori_loop(0, 2, apply, 0)

        def next_gram(i, total):
            eye = on_diagonal(i)
            rest = gram[block(i), :] - jnp.where(eye, shift, 0.0)
            own = poly[block(i), :]
            half_way = jnp.dot(rest_low[block(i), :], poly_low[...], preferred_element_type=F32)
            half_way = half_way + shift * own + factor * rest
            value = jnp.dot(half_way.astype(B16), poly_low[...], preferred_element_type=F32)
            value = value + (shift * factor) * own + factor * half_way
            value = value + jnp.where(eye, shift * factor * factor, 0.0)
            gram[block(i), :] = value
            return total + jnp.sum(jnp.where(eye, value, 0.0))

        steps = jnp.where(iteration + 1 < NS_STEPS, blocks, 0)
        return lax.fori_loop(0, steps, next_gram, jnp.float32(0.0))

    lax.fori_loop(0, NS_STEPS, step, trace_of(gram))
    out_ref[...] = current[...].astype(B16)


def gram_orthogonalize(rows, gram):
    size = gram.shape[0]
    whole = pltpu.VMEM((size, size), F32)
    low = pltpu.VMEM((size, size), B16)
    return pl.pallas_call(
        polynomial_kernel,
        out_shape=jax.ShapeDtypeStruct(rows.shape, B16),
        in_specs=[pl.BlockSpec(memory_space=pltpu.VMEM)] * 2,
        out_specs=pl.BlockSpec(memory_space=pltpu.VMEM),
        scratch_shapes=[whole, low, whole, low, pltpu.VMEM(rows.shape, F32)],
        compiler_params=pltpu.CompilerParams(vmem_limit_bytes=48 * 1024 * 1024),
        cost_estimate=pl.CostEstimate(flops=30 * size**3, transcendentals=0, bytes_accessed=8 * size * size),
    )(gram, rows)


def one_way(value, bit, lower):
    count = lax.axis_size("dp")
    start = 1 if lower else 0
    return lax.ppermute(
        value, "dp", [(i, i ^ (1 << bit)) for i in range(count) if (i & 1) == start]
    )


def swap_core(value, bit, core):
    count = lax.axis_size("dp")
    return lax.ppermute(value, "dp", [(i, i ^ (1 << bit)) for i in range(count) if (i & 1) == core])


def gather_plane(own, other, core):
    rest = list(range(1, plane_bits()))
    held = [own[None], other[None]]
    for step in range(len(rest)):
        for color in range(2):
            bit = rest[step] if color == 0 else rest[::-1][step]
            held[color] = jnp.concatenate([held[color], swap_core(held[color], bit, core)])
    return held


def gram_of(held):
    return sum(
        lax.dot_general(
            part.reshape(-1, part.shape[-1]),
            part.reshape(-1, part.shape[-1]),
            TOKENS_OUT,
            preferred_element_type=F32,
        )
        for part in held
    )


def to_owners(attn, ffn):
    lines = lax.axis_size("fsdp")
    attn_count, small, columns = attn.shape
    ffn_count, large, _ = ffn.shape
    at_one = min(lines, attn_count)
    spare = attn_count - at_one
    top = [ffn]
    if spare:
        top.append(jnp.pad(attn[at_one:], ((0, 0), (0, large - small), (0, 0))))
    if lines > ffn_count + spare:
        top.append(jnp.zeros((lines - ffn_count - spare, large, columns), ffn.dtype))
    low = attn[:at_one]
    if lines > at_one:
        low = jnp.pad(low, ((0, lines - at_one), (0, 0), (0, 0)))
    return jnp.concatenate(top), low


def exchange(top, low):
    large = top.shape[1]
    both = lax.all_to_all(
        jnp.concatenate([top, low], axis=1), "fsdp", split_axis=0, concat_axis=0, tiled=True
    )
    return both[:, :large], both[:, large:]


def from_owners(top, low, ffn_count, attn_count):
    at_one = min(top.shape[0], attn_count)
    spare = attn_count - at_one
    attn = low[:at_one]
    if spare:
        attn = jnp.concatenate([attn, top[ffn_count : ffn_count + spare, : low.shape[1]]])
    return attn, top[:ffn_count]


def owner_momentum(moment, grad):
    return (MOMENT_DECAY * moment.astype(F32) + (1.0 - MOMENT_DECAY) * grad.astype(F32)).astype(B16)


def on_device(
    tokens,
    segment_ids,
    decay_rate,
    cotangent,
    attn_master,
    ffn_master,
    gains,
    attn_moment,
    ffn_moment,
    gain_first,
    gain_second,
):
    attn_low = attn_master.astype(B16)
    ffn_low = ffn_master.astype(B16)
    gain_low = gains.astype(B16)
    in_full, proj_full, up_full, down_full, gain_whole = (
        lax.all_gather(value, ("dp", "fsdp"), axis=1, tiled=True)
        for value in (attn_low[:4], attn_low[4:], ffn_low[:2], ffn_low[2:], gain_low)
    )
    ffn_full = (up_full, down_full[0])
    top_moment, low_moment = exchange(*to_owners(attn_moment.astype(B16), ffn_moment.astype(B16)))
    top_moment, low_moment, in_full = ordered(top_moment, low_moment, in_full)
    attn_full = (in_full, proj_full[0])
    stored = forward(tokens, segment_ids[0], decay_rate, attn_full, ffn_full, gain_whole)
    x_grad, grads, grad_gain = backward(
        stored, cotangent, attn_full, ffn_full, gain_whole
    )
    down, up, proj, inner = grads
    lines = lax.axis_size("fsdp")
    attn_count, small, columns = attn_master.shape
    ffn_count, large, _ = ffn_master.shape
    block, little = lines * large, lines * small
    inner_out = inner.payloads()
    inner_out, middle, product = tied([inner_out], stored[-6], stored[-1])
    inner.accept(inner.swap(inner_out))
    down_sum = down.finish()
    up_sum = up.finish()
    proj_sum = proj.finish()
    out = (middle + jnp.dot(product, ffn_full[1], preferred_element_type=F32)).astype(B16)
    at_one = min(lines, attn_count)
    top_grad = [up_sum, down_sum]
    if attn_count > at_one:
        spread = jnp.pad(proj_sum.reshape(1, lines, small, columns), ((0, 0), (0, 0), (0, large - small), (0, 0)))
        top_grad.append(spread.reshape(1, block, columns))
    top_grad = jnp.concatenate(top_grad)
    if lines > top_grad.shape[0]:
        top_grad = jnp.pad(top_grad, ((0, lines - top_grad.shape[0]), (0, 0), (0, 0)))
    top_grad = lax.psum_scatter(top_grad, "fsdp", scatter_dimension=0, tiled=True)[0]
    at_core = lax.axis_index("dp") & 1
    big = owner_momentum(top_moment.reshape(block, columns), top_grad)
    big_other = one_way(big, 0, True)
    top_gram = gram_of(gather_plane(big, big_other, 0))
    low_grad = inner.finish()
    if attn_count == at_one:
        low_grad = jnp.concatenate([low_grad, proj_sum])
    if lines > low_grad.shape[0]:
        low_grad = jnp.pad(low_grad, ((0, lines - low_grad.shape[0]), (0, 0), (0, 0)))
    top_grad, low_grad = ordered(top_grad, low_grad)
    low_grad = lax.psum_scatter(low_grad, "fsdp", scatter_dimension=0, tiled=True)[0]
    low = owner_momentum(low_moment.reshape(little, columns), low_grad)
    low_other = one_way(low, 0, False)
    low_gram = gram_of(gather_plane(low, low_other, 1))
    gram = jnp.where(at_core == 0, top_gram, low_gram)
    fill = ((0, block - little), (0, 0))
    mine = jnp.concatenate(
        [
            jnp.where(at_core == 0, big, jnp.pad(low, fill)),
            jnp.where(at_core == 0, big_other, jnp.pad(low_other, fill)),
        ]
    )
    result = gram_orthogonalize(mine, gram)
    own, other = result[:block], result[block:]
    back_top = one_way(other, 0, False)
    back_low = one_way(other[:little], 0, True)
    top_orth = jnp.where(at_core == 0, own, back_top).reshape(lines, large, columns)
    low_orth = jnp.where(at_core == 0, back_low, own[:little]).reshape(lines, small, columns)
    attn_orth, ffn_orth = from_owners(*exchange(top_orth, low_orth), ffn_count, attn_count)
    attn_orth, ffn_orth = attn_orth.astype(F32), ffn_orth.astype(F32)
    attn_grad, ffn_grad = from_owners(
        *exchange(top_grad.reshape(lines, large, columns), low_grad.reshape(lines, small, columns)),
        ffn_count,
        attn_count,
    )
    attn_grad, ffn_grad = attn_grad.astype(F32), ffn_grad.astype(F32)
    attn_state = MOMENT_DECAY * attn_moment + (1.0 - MOMENT_DECAY) * attn_grad
    ffn_state = MOMENT_DECAY * ffn_moment + (1.0 - MOMENT_DECAY) * ffn_grad
    gain_grad = gain_sum(grad_gain)
    attn_new = attn_master - LR_MUON * attn_orth
    ffn_new = ffn_master - LR_MUON * math.sqrt(FF / D) * ffn_orth
    first_new = BETA_ONE * gain_first + (1.0 - BETA_ONE) * gain_grad
    second_new = BETA_TWO * gain_second + (1.0 - BETA_TWO) * gain_grad * gain_grad
    gains_new = gains - LR_GAIN * first_new / (jnp.sqrt(second_new) + ADAM_EPS)
    return (
        out,
        x_grad,
        attn_grad,
        ffn_grad,
        gain_grad,
        attn_state,
        ffn_state,
        attn_new,
        ffn_new,
        attn_new.astype(B16),
        ffn_new.astype(B16),
        gains_new,
        first_new,
        second_new,
    )


def solution(mesh):
    return jax.shard_map(
        on_device,
        mesh=mesh,
        in_specs=(
            P(("dp", "fsdp"), None),
            P(("dp", "fsdp"), None),
            P(),
            P(("dp", "fsdp"), None),
            P(None, ("dp", "fsdp"), None),
            P(None, ("dp", "fsdp"), None),
            P(None, ("dp", "fsdp")),
            P(None, ("dp", "fsdp"), None),
            P(None, ("dp", "fsdp"), None),
            P(None, ("dp", "fsdp")),
            P(None, ("dp", "fsdp")),
        ),
        out_specs=(
            P(("dp", "fsdp"), None),
            P(("dp", "fsdp"), None),
            P(None, ("dp", "fsdp"), None),
            P(None, ("dp", "fsdp"), None),
            P(None, ("dp", "fsdp")),
            P(None, ("dp", "fsdp"), None),
            P(None, ("dp", "fsdp"), None),
            P(None, ("dp", "fsdp"), None),
            P(None, ("dp", "fsdp"), None),
            P(None, ("dp", "fsdp"), None),
            P(None, ("dp", "fsdp"), None),
            P(None, ("dp", "fsdp")),
            P(None, ("dp", "fsdp")),
            P(None, ("dp", "fsdp")),
        ),
        check_vma=False,
    )
```

```python
import math

import jax
import jax.numpy as jnp
from jax import lax
from jax.experimental import pallas as pl
from jax.experimental.pallas import tpu as pltpu
from jax.sharding import PartitionSpec as P

D = 1024
FF = 2816
NS_STEPS = 5


EPS = 1e-06
NS_EPS = 1e-07
NS_A = 3.4445
NS_B = -4.775
NS_C = 2.0315
LR_MUON = 0.3
LR_GAIN = 0.1
MOMENT_DECAY = 0.5
BETA_ONE = 0.9
BETA_TWO = 0.95
ADAM_EPS = 1e-08
F32 = jnp.float32
B16 = jnp.bfloat16
ROWS_BY_ROWS = (((1,), (1,)), ((), ()))
TOKENS_OUT = (((0,), (0,)), ((), ()))


def rms_scale(series):
    return lax.rsqrt(jnp.mean(series * series, axis=-1, keepdims=True) + EPS)


def rms_back(series, factor, upstream):
    return factor * upstream - series * (factor * factor * factor) * jnp.mean(
        upstream * series, axis=-1, keepdims=True
    )


def decay_mask(segments, decay_rate):
    length = segments.shape[0]
    places = jnp.arange(length, dtype=jnp.int32)
    distance = places[:, None] - places[None, :]
    allowed = (segments[:, None] == segments[None, :]) & (distance >= 0)
    fading = jnp.exp(-decay_rate[:, None, None] * jnp.maximum(distance, 0).astype(F32)[None])
    return jnp.where(allowed[None], fading, 0.0)


def forward(tokens, segments, decay_rate, attn_full, up_gather, down_gather, gain_low):
    length, model_width = tokens.shape
    head_count = decay_rate.shape[0]
    head_size = model_width // head_count
    gain_full = gain_low.astype(F32)
    inputs = tokens.astype(F32)
    first_scale = rms_scale(inputs)
    normed = (inputs * first_scale * gain_full[0]).astype(B16)
    projected = lax.dot_general(
        normed,
        attn_full.reshape(5 * model_width, model_width),
        ROWS_BY_ROWS,
        preferred_element_type=F32,
    )
    query_act = jax.nn.relu(projected[:, :model_width]).astype(B16)
    key_act = jax.nn.relu(projected[:, model_width : 2 * model_width]).astype(B16)
    value_act = projected[:, 2 * model_width : 3 * model_width].astype(B16)
    gate_pre = projected[:, 3 * model_width : 4 * model_width]
    fading_mask = decay_mask(segments, decay_rate)
    query_heads = query_act.reshape(length, head_count, head_size)
    key_heads = key_act.reshape(length, head_count, head_size)
    value_heads = value_act.reshape(length, head_count, head_size)
    scores = jnp.einsum("the,she->hts", query_heads, key_heads, preferred_element_type=F32)
    weights_low = (scores * fading_mask).astype(B16)
    attended = jnp.einsum(
        "hts,she->the", weights_low, value_heads, preferred_element_type=F32
    ).reshape(length, model_width)
    out_scale = rms_scale(attended)
    normal_out = attended * out_scale * gain_full[2]
    gate_sig = jax.nn.sigmoid(gate_pre)
    gated_out = (normal_out * gate_sig).astype(B16)
    down_gather.held, gated_out = tied([down_gather.held], gated_out)
    down_gather.send()
    branch = lax.dot_general(gated_out, attn_full[4], ROWS_BY_ROWS, preferred_element_type=F32)
    middle = inputs + branch
    second_scale = rms_scale(middle)
    normed_two = (middle * second_scale * gain_full[1]).astype(B16)
    up_gather.pieces, normed_two = tied([up_gather.pieces], normed_two)
    ffn_up = up_gather.join()
    up_one, up_two = (
        lax.dot_general(normed_two, matrix, ROWS_BY_ROWS, preferred_element_type=F32) for matrix in ffn_up
    )
    product = (up_one * up_two).astype(B16)
    stored = (
        inputs,
        first_scale,
        normed,
        query_act,
        key_act,
        value_act,
        gate_pre,
        fading_mask,
        weights_low,
        attended,
        out_scale,
        normal_out,
        gate_sig,
        gated_out,
        middle,
        second_scale,
        normed_two,
        up_one,
        up_two,
        product,
    )
    return stored, ffn_up


def backward(stored, cotangent, attn_full, ffn_up, down_gather, gain_low):
    (
        inputs,
        first_scale,
        normed,
        query_act,
        key_act,
        value_act,
        gate_pre,
        fading_mask,
        weights_low,
        attended,
        out_scale,
        normal_out,
        gate_sig,
        gated_out,
        middle,
        second_scale,
        normed_two,
        up_one,
        up_two,
        product,
    ) = stored
    length, model_width = inputs.shape
    head_count = fading_mask.shape[0]
    head_size = model_width // head_count
    hidden = product.shape[1]
    gain_full = gain_low.astype(F32)
    grad_out = cotangent.astype(F32)
    half = hidden // 2
    down = Halving(
        weight_grad(product[:, :half], cotangent), weight_grad(product[:, half:], cotangent)
    )
    down_out, down_gather.pieces, cotangent = tied([down.payloads(), down_gather.pieces], cotangent)
    down_in = down.swap(down_out)
    ffn_down = down_gather.join()[0]
    grad_product = lax.dot_general(cotangent, ffn_down, ROWS_BY_ROWS, preferred_element_type=F32)
    grad_one = (grad_product * up_two).astype(B16)
    grad_two = (grad_product * up_one).astype(B16)
    send_one, send_two = weight_grad(grad_one[:, half:], normed_two), weight_grad(grad_two[:, half:], normed_two)
    down_in, sends, grad_one, grad_two = tied([down_in, [send_one, send_two]], grad_one, grad_two)
    down.accept(down_in)
    one = Halving(weight_grad(grad_one[:, :half], normed_two), sends[0])
    two = Halving(weight_grad(grad_two[:, :half], normed_two), sends[1])
    one_in, two_in = one.swap(one.payloads()), two.swap(two.payloads())
    down_out, grad_one, grad_two = tied([down.payloads()], grad_one, grad_two)
    down_in = down.swap(down_out)
    grad_normed_two = jnp.dot(grad_one, ffn_up[0], preferred_element_type=F32) + jnp.dot(
        grad_two, ffn_up[1], preferred_element_type=F32
    )
    gain_two = jnp.sum(grad_normed_two * middle * second_scale, axis=0)
    grad_middle = grad_out + rms_back(middle, second_scale, grad_normed_two * gain_full[1])
    middle_low = grad_middle.astype(B16)
    down_in, one_in, two_in, middle_low = tied([down_in, one_in, two_in], middle_low)
    down.accept(down_in)
    one.accept(one_in)
    two.accept(two_in)
    down_out, one_out, two_out, middle_low = tied(
        [down.payloads(), one.payloads(), two.payloads()], middle_low
    )
    down_in, one_in, two_in = down.swap(down_out), one.swap(one_out), two.swap(two_out)
    grad_outproj = lax.dot_general(middle_low, gated_out, TOKENS_OUT, preferred_element_type=F32).astype(B16)
    proj = Halving(grad_outproj[None])
    proj_out, middle_low = tied([proj.payloads()], middle_low)
    proj_in = proj.swap(proj_out)
    grad_gated = jnp.dot(middle_low, attn_full[4], preferred_element_type=F32)
    grad_normal = grad_gated * gate_sig
    grad_gate = grad_gated * normal_out * gate_sig * (1.0 - gate_sig)
    gain_three = jnp.sum(grad_normal * attended * out_scale, axis=0)
    grad_attended = (
        rms_back(attended, out_scale, grad_normal * gain_full[2])
        .astype(B16)
        .reshape(length, head_count, head_size)
    )
    query_heads = query_act.reshape(length, head_count, head_size)
    key_heads = key_act.reshape(length, head_count, head_size)
    value_heads = value_act.reshape(length, head_count, head_size)
    grad_weights = jnp.einsum(
        "the,she->hts", grad_attended, value_heads, preferred_element_type=F32
    )
    grad_values = jnp.einsum(
        "hts,the->she", weights_low, grad_attended, preferred_element_type=F32
    ).reshape(length, model_width)
    grad_scores = (grad_weights * fading_mask).astype(B16)
    grad_queries = jnp.einsum(
        "hts,she->the", grad_scores, key_heads, preferred_element_type=F32
    ).reshape(length, model_width)
    grad_keys = jnp.einsum(
        "hts,the->she", grad_scores, query_heads, preferred_element_type=F32
    ).reshape(length, model_width)
    grad_mixed = jnp.concatenate(
        [
            jnp.where(query_act > 0, grad_queries, 0.0),
            jnp.where(key_act > 0, grad_keys, 0.0),
            grad_values,
            grad_gate,
        ],
        axis=1,
    ).astype(B16)
    down_in, one_in, two_in, proj_in, grad_mixed = tied([down_in, one_in, two_in, proj_in], grad_mixed)
    down.accept(down_in)
    one.accept(one_in)
    two.accept(two_in)
    proj.accept(proj_in)
    one_out, two_out, proj_out, grad_mixed = tied(
        [one.payloads(), two.payloads(), proj.payloads()], grad_mixed
    )
    one_in, two_in, proj_in = one.swap(one_out), two.swap(two_out), proj.swap(proj_out)
    grad_inner = lax.dot_general(grad_mixed, normed, TOKENS_OUT, preferred_element_type=F32).astype(B16)
    inner = Halving(grad_inner.reshape(4, model_width, model_width))
    inner_out, grad_mixed = tied([inner.payloads()], grad_mixed)
    inner_in = inner.swap(inner_out)
    grad_normed = jnp.dot(
        jnp.pad(grad_mixed, ((0, 0), (0, model_width))),
        attn_full.reshape(5 * model_width, model_width),
        preferred_element_type=F32,
    )
    gain_one = jnp.sum(grad_normed * inputs * first_scale, axis=0)
    grad_inputs = grad_middle + rms_back(inputs, first_scale, grad_normed * gain_full[0])
    grad_gain = jnp.stack([gain_one, gain_two, gain_three])
    one_in, two_in, proj_in, inner_in, grad_inputs = tied(
        [one_in, two_in, proj_in, inner_in], grad_inputs
    )
    one.accept(one_in)
    two.accept(two_in)
    proj.accept(proj_in)
    inner.accept(inner_in)
    return (grad_inputs, (one, two, down, proj, inner), grad_gain, ffn_down)


def ordered(*values):
    return lax.optimization_barrier(values)


def plane_bits():
    return lax.axis_size("dp").bit_length() - 1


def swap_bit(value, bit):
    count = lax.axis_size("dp")
    return lax.ppermute(value, "dp", [(i, i ^ (1 << bit)) for i in range(count)])


def weight_grad(features, series):
    return lax.dot_general(features, series, TOKENS_OUT, preferred_element_type=F32).astype(B16)


class Halving:
    def __init__(self, grad, sent=None):
        bits = plane_bits()
        self.fixed = sent is not None
        if self.fixed:
            rows, columns = grad.shape
            self.chunk = 2 * rows // lax.axis_size("dp")
            shape = (1,) + (2,) * (bits - 1) + (self.chunk, columns)
            self.first = [sent.reshape(shape)]
            self.parts = [[(grad.reshape(shape), list(range(1, bits))[::-1])]]
        else:
            count, rows, columns = grad.shape
            self.chunk = rows // lax.axis_size("dp")
            self.first = None
            blocks = grad.reshape((count,) + (2,) * bits + (self.chunk, columns))
            self.parts = [[(blocks, list(range(bits))[::-1])]]
        self.orders = [[0]]

    def choose(self, term, dims, bit, other):
        if bit not in dims:
            return term
        if self.fixed:
            index = 1 if other else 0
        else:
            place = (lax.axis_index("dp") >> bit) & 1
            index = 1 - place if other else place
        return lax.dynamic_index_in_dim(term, index, 1 + dims.index(bit), keepdims=False)

    def payloads(self):
        if self.orders == [[]]:
            rest = list(range(1, plane_bits()))
            half = self.chunk // 2
            self.parts = [
                [(t[..., color * half : (color + 1) * half, :], dims) for t, dims in self.parts[0]]
                for color in range(2)
            ]
            self.orders = [rest, rest[::-1]]
        self.bits = [order[0] for order in self.orders]
        if self.first is not None:
            first, self.first = self.first, None
            return first
        return [
            sum(self.choose(t, dims, bit, True).astype(F32) for t, dims in part).astype(B16)
            for part, bit in zip(self.parts, self.bits)
        ]

    def swap(self, payloads):
        return [swap_bit(value, bit) for value, bit in zip(payloads, self.bits)]

    def accept(self, arrived):
        for color, (part, bit) in enumerate(zip(self.parts, self.bits)):
            left = [b for b in part[0][1] if b != bit]
            self.parts[color] = [(self.choose(t, dims, bit, False), left) for t, dims in part]
            self.parts[color].append((arrived[color], left))
            self.orders[color] = self.orders[color][1:]

    def finish(self):
        while len(self.parts) == 1 or self.orders[0]:
            self.accept(self.swap(self.payloads()))
        return jnp.concatenate([sum(t.astype(F32) for t, _ in part).astype(B16) for part in self.parts], axis=1)


def tied(lists, *values):
    flat = ordered(*[v for part in lists for v in part], *values)
    out, at = [], 0
    for part in lists:
        out.append(list(flat[at : at + len(part)]))
        at += len(part)
    return (*out, *flat[at:])


def line_gather(value):
    lines = lax.axis_size("fsdp")
    above, below = [], []
    from_above = from_below = value
    for _ in range(lines - 1):
        from_above = lax.ppermute(from_above, "fsdp", [(i, i - 1) for i in range(1, lines)])
        from_below = lax.ppermute(from_below, "fsdp", [(i, i + 1) for i in range(lines - 1)])
        above.append(from_above)
        below.append(from_below)
    every = jnp.stack(below[::-1] + [value] + above, axis=1)
    return lax.dynamic_slice_in_dim(every, lines - 1 - lax.axis_index("fsdp"), lines, axis=1)


class HiddenGather:
    def __init__(self, line):
        self.count, lines, _, self.columns = line.shape
        rest = list(range(1, plane_bits()))
        self.orders = (rest, rest[::-1])
        self.held, self.have = [], []
        for color, order in enumerate(self.orders):
            held = line[:, : lines // 2] if color == 0 else line[:, lines // 2 :]
            have = []
            for bit in order[:-1]:
                have = sorted(have + [bit], reverse=True)
                held = jnp.stack([held, swap_bit(held, bit)], axis=1 + have.index(bit))
            self.held.append(held)
            self.have.append(have)

    def send(self):
        self.pieces = []
        for held, order in zip(self.held, self.orders):
            came = swap_bit(held, order[-1])
            self.pieces += [held, came, swap_bit(held, 0), swap_bit(came, 0)]

    def join(self):
        out = []
        for matrix in range(self.count):
            sides = [[], []]
            for color, (have, order) in enumerate(zip(self.have, self.orders)):
                axis = sorted(have + order[-1:], reverse=True).index(order[-1])
                held, came, other_held, other_came = (p[matrix] for p in self.pieces[4 * color : 4 * color + 4])
                sides[0].append(jnp.stack([held, came], axis=axis))
                sides[1].append(jnp.stack([other_held, other_came], axis=axis))
            whole = jnp.stack([jnp.concatenate(side, axis=len(self.orders[0])) for side in sides])
            out.append(whole.reshape(-1, self.columns))
        return out


def gain_gather(value):
    rows, own = value.shape
    total = lax.axis_size("dp") * lax.axis_size("fsdp")
    copies = jnp.broadcast_to(value[None], (total, rows, own))
    every = lax.all_to_all(copies, ("dp", "fsdp"), 0, 0, tiled=True)
    return jnp.transpose(every, (1, 0, 2)).reshape(rows, total * own)


def gain_sum(grad):
    rows, columns = grad.shape
    total = lax.axis_size("dp") * lax.axis_size("fsdp")
    blocks = jnp.transpose(grad.reshape(rows, total, columns // total), (1, 0, 2))
    return jnp.sum(lax.all_to_all(blocks, ("dp", "fsdp"), 0, 0, tiled=True), axis=0)


NS_ROWS = 256


def polynomial_kernel(gram_ref, rows_ref, out_ref, gram, rest_low, poly, poly_low, current):
    size = gram_ref.shape[0]
    count = rows_ref.shape[0]
    blocks = size // NS_ROWS
    parts = count // 2

    def block(i):
        return pl.ds(pl.multiple_of(i * NS_ROWS, NS_ROWS), NS_ROWS)

    def on_diagonal(i):
        row = lax.broadcasted_iota(jnp.int32, (NS_ROWS, size), 0) + i * NS_ROWS
        return row == lax.broadcasted_iota(jnp.int32, (NS_ROWS, size), 1)

    def trace_of(ref):
        def add(i, total):
            return total + jnp.sum(jnp.where(on_diagonal(i), ref[block(i), :], 0.0))

        return lax.fori_loop(0, blocks, add, jnp.float32(0.0))

    square = jnp.full((1, 1), trace_of(gram_ref), F32)
    norm = jnp.sqrt(square) + NS_EPS
    scale = 1.0 / norm

    def start(i, carry):
        gram[block(i), :] = gram_ref[block(i), :] * (scale * scale)
        return carry

    lax.fori_loop(0, blocks, start, 0)
    current[...] = rows_ref[...].astype(F32) * scale

    def step(iteration, trace):
        shift = trace / size
        factor = NS_A + NS_B * shift + NS_C * shift * shift

        def low_rest(i, carry):
            rest_low[block(i), :] = (gram[block(i), :] - jnp.where(on_diagonal(i), shift, 0.0)).astype(B16)
            return carry

        lax.fori_loop(0, blocks, low_rest, 0)

        def polynomial(i, carry):
            eye = on_diagonal(i)
            own = gram[block(i), :]
            rest = own - jnp.where(eye, shift, 0.0)
            squared = jnp.dot(rest_low[block(i), :], rest_low[...], preferred_element_type=F32)
            squared = squared + 2.0 * shift * rest + jnp.where(eye, shift * shift, 0.0)
            value = NS_B * own + NS_C * squared + jnp.where(eye, NS_A - factor, 0.0)
            poly[block(i), :] = value
            poly_low[block(i), :] = value.astype(B16)
            return carry

        lax.fori_loop(0, blocks, polynomial, 0)

        def apply(i, carry):
            where = pl.ds(pl.multiple_of(i * parts, parts), parts)
            value = current[where, :]
            current[where, :] = factor * value + jnp.dot(
                value.astype(B16), poly_low[...], preferred_element_type=F32
            )
            return carry

        lax.fori_loop(0, 2, apply, 0)

        def next_gram(i, total):
            eye = on_diagonal(i)
            rest = gram[block(i), :] - jnp.where(eye, shift, 0.0)
            own = poly[block(i), :]
            half_way = jnp.dot(rest_low[block(i), :], poly_low[...], preferred_element_type=F32)
            half_way = half_way + shift * own + factor * rest
            value = jnp.dot(half_way.astype(B16), poly_low[...], preferred_element_type=F32)
            value = value + (shift * factor) * own + factor * half_way
            value = value + jnp.where(eye, shift * factor * factor, 0.0)
            gram[block(i), :] = value
            return total + jnp.sum(jnp.where(eye, value, 0.0))

        steps = jnp.where(iteration + 1 < NS_STEPS, blocks, 0)
        return lax.fori_loop(0, steps, next_gram, jnp.float32(0.0))

    lax.fori_loop(0, NS_STEPS, step, trace_of(gram))
    out_ref[...] = current[...].astype(B16)


def gram_orthogonalize(rows, gram):
    size = gram.shape[0]
    whole = pltpu.VMEM((size, size), F32)
    low = pltpu.VMEM((size, size), B16)
    return pl.pallas_call(
        polynomial_kernel,
        out_shape=jax.ShapeDtypeStruct(rows.shape, B16),
        in_specs=[pl.BlockSpec(memory_space=pltpu.VMEM)] * 2,
        out_specs=pl.BlockSpec(memory_space=pltpu.VMEM),
        scratch_shapes=[whole, low, whole, low, pltpu.VMEM(rows.shape, F32)],
        compiler_params=pltpu.CompilerParams(vmem_limit_bytes=48 * 1024 * 1024),
        cost_estimate=pl.CostEstimate(flops=30 * size**3, transcendentals=0, bytes_accessed=8 * size * size),
    )(gram, rows)


def one_way(value, bit, lower):
    count = lax.axis_size("dp")
    start = 1 if lower else 0
    return lax.ppermute(
        value, "dp", [(i, i ^ (1 << bit)) for i in range(count) if (i & 1) == start]
    )


def swap_core(value, bit, core):
    count = lax.axis_size("dp")
    return lax.ppermute(value, "dp", [(i, i ^ (1 << bit)) for i in range(count) if (i & 1) == core])


def gather_plane(own, other, core):
    rest = list(range(1, plane_bits()))
    held = [own[None], other[None]]
    for step in range(len(rest)):
        for color in range(2):
            bit = rest[step] if color == 0 else rest[::-1][step]
            held[color] = jnp.concatenate([held[color], swap_core(held[color], bit, core)])
    return held


def gram_of(held):
    return sum(
        lax.dot_general(
            part.reshape(-1, part.shape[-1]),
            part.reshape(-1, part.shape[-1]),
            TOKENS_OUT,
            preferred_element_type=F32,
        )
        for part in held
    )


def to_owners(attn, ffn):
    lines = lax.axis_size("fsdp")
    attn_count, small, columns = attn.shape
    ffn_count, large, _ = ffn.shape
    at_one = min(lines, attn_count)
    spare = attn_count - at_one
    top = [ffn]
    if spare:
        top.append(jnp.pad(attn[at_one:], ((0, 0), (0, large - small), (0, 0))))
    if lines > ffn_count + spare:
        top.append(jnp.zeros((lines - ffn_count - spare, large, columns), ffn.dtype))
    low = attn[:at_one]
    if lines > at_one:
        low = jnp.pad(low, ((0, lines - at_one), (0, 0), (0, 0)))
    return jnp.concatenate(top), low


def exchange(top, low):
    large = top.shape[1]
    both = lax.all_to_all(
        jnp.concatenate([top, low], axis=1), "fsdp", split_axis=0, concat_axis=0, tiled=True
    )
    return both[:, :large], both[:, large:]


def from_owners(top, low, ffn_count, attn_count):
    at_one = min(top.shape[0], attn_count)
    spare = attn_count - at_one
    attn = low[:at_one]
    if spare:
        attn = jnp.concatenate([attn, top[ffn_count : ffn_count + spare, : low.shape[1]]])
    return attn, top[:ffn_count]


def owner_momentum(moment, grad):
    return (MOMENT_DECAY * moment.astype(F32) + (1.0 - MOMENT_DECAY) * grad.astype(F32)).astype(B16)


def on_device(
    tokens,
    segment_ids,
    decay_rate,
    cotangent,
    attn_master,
    ffn_master,
    gains,
    attn_moment,
    ffn_moment,
    gain_first,
    gain_second,
):
    attn_low = attn_master.astype(B16)
    ffn_low = ffn_master.astype(B16)
    gain_low = gains.astype(B16)
    attn_full = lax.all_gather(attn_low, ("dp", "fsdp"), axis=1, tiled=True)
    up_line, down_low = ordered(line_gather(ffn_low[:2]), ffn_low[2:])
    up_gather, down_gather = HiddenGather(up_line), HiddenGather(line_gather(down_low))
    gain_whole = gain_gather(gain_low)
    top_moment, low_moment = exchange(*to_owners(attn_moment.astype(B16), ffn_moment.astype(B16)))
    up_gather.held, top_moment, low_moment, attn_full = tied(
        [up_gather.held], top_moment, low_moment, attn_full
    )
    up_gather.send()
    stored, ffn_up = forward(tokens, segment_ids[0], decay_rate, attn_full, up_gather, down_gather, gain_whole)
    x_grad, grads, grad_gain, ffn_down = backward(
        stored, cotangent, attn_full, ffn_up, down_gather, gain_whole
    )
    one, two, down, proj, inner = grads
    lines = lax.axis_size("fsdp")
    attn_count, small, columns = attn_master.shape
    ffn_count, large, _ = ffn_master.shape
    block, little = lines * large, lines * small
    inner_out = inner.payloads()
    inner_out, middle, product = tied([inner_out], stored[-6], stored[-1])
    inner.accept(inner.swap(inner_out))
    ffn_sums = [value.finish() for value in (one, two, down)]
    proj_sum = proj.finish()
    out = (middle + jnp.dot(product, ffn_down, preferred_element_type=F32)).astype(B16)
    at_one = min(lines, attn_count)
    top_grad = ffn_sums
    if attn_count > at_one:
        spread = jnp.pad(proj_sum.reshape(1, lines, small, columns), ((0, 0), (0, 0), (0, large - small), (0, 0)))
        top_grad.append(spread.reshape(1, block, columns))
    top_grad = jnp.concatenate(top_grad)
    if lines > top_grad.shape[0]:
        top_grad = jnp.pad(top_grad, ((0, lines - top_grad.shape[0]), (0, 0), (0, 0)))
    top_grad = lax.psum_scatter(top_grad, "fsdp", scatter_dimension=0, tiled=True)[0]
    at_core = lax.axis_index("dp") & 1
    big = owner_momentum(top_moment.reshape(block, columns), top_grad)
    big_other = one_way(big, 0, True)
    top_gram = gram_of(gather_plane(big, big_other, 0))
    low_grad = inner.finish()
    if attn_count == at_one:
        low_grad = jnp.concatenate([low_grad, proj_sum])
    if lines > low_grad.shape[0]:
        low_grad = jnp.pad(low_grad, ((0, lines - low_grad.shape[0]), (0, 0), (0, 0)))
    top_grad, low_grad = ordered(top_grad, low_grad)
    low_grad = lax.psum_scatter(low_grad, "fsdp", scatter_dimension=0, tiled=True)[0]
    low = owner_momentum(low_moment.reshape(little, columns), low_grad)
    low_other = one_way(low, 0, False)
    low_gram = gram_of(gather_plane(low, low_other, 1))
    gram = jnp.where(at_core == 0, top_gram, low_gram)
    fill = ((0, block - little), (0, 0))
    mine = jnp.concatenate(
        [
            jnp.where(at_core == 0, big, jnp.pad(low, fill)),
            jnp.where(at_core == 0, big_other, jnp.pad(low_other, fill)),
        ]
    )
    result = gram_orthogonalize(mine, gram)
    own, other = result[:block], result[block:]
    back_top = one_way(other, 0, False)
    back_low = one_way(other[:little], 0, True)
    top_orth = jnp.where(at_core == 0, own, back_top).reshape(lines, large, columns)
    low_orth = jnp.where(at_core == 0, back_low, own[:little]).reshape(lines, small, columns)
    attn_orth, ffn_orth = from_owners(*exchange(top_orth, low_orth), ffn_count, attn_count)
    attn_orth, ffn_orth = attn_orth.astype(F32), ffn_orth.astype(F32)
    attn_grad, ffn_grad = from_owners(
        *exchange(top_grad.reshape(lines, large, columns), low_grad.reshape(lines, small, columns)),
        ffn_count,
        attn_count,
    )
    attn_grad, ffn_grad = attn_grad.astype(F32), ffn_grad.astype(F32)
    attn_state = MOMENT_DECAY * attn_moment + (1.0 - MOMENT_DECAY) * attn_grad
    ffn_state = MOMENT_DECAY * ffn_moment + (1.0 - MOMENT_DECAY) * ffn_grad
    gain_grad = gain_sum(grad_gain)
    attn_new = attn_master - LR_MUON * attn_orth
    ffn_new = ffn_master - LR_MUON * math.sqrt(FF / D) * ffn_orth
    first_new = BETA_ONE * gain_first + (1.0 - BETA_ONE) * gain_grad
    second_new = BETA_TWO * gain_second + (1.0 - BETA_TWO) * gain_grad * gain_grad
    gains_new = gains - LR_GAIN * first_new / (jnp.sqrt(second_new) + ADAM_EPS)
    return (
        out,
        x_grad,
        attn_grad,
        ffn_grad,
        gain_grad,
        attn_state,
        ffn_state,
        attn_new,
        ffn_new,
        attn_new.astype(B16),
        ffn_new.astype(B16),
        gains_new,
        first_new,
        second_new,
    )


def solution(mesh):
    return jax.shard_map(
        on_device,
        mesh=mesh,
        in_specs=(
            P(("dp", "fsdp"), None),
            P(("dp", "fsdp"), None),
            P(),
            P(("dp", "fsdp"), None),
            P(None, ("dp", "fsdp"), None),
            P(None, ("dp", "fsdp"), None),
            P(None, ("dp", "fsdp")),
            P(None, ("dp", "fsdp"), None),
            P(None, ("dp", "fsdp"), None),
            P(None, ("dp", "fsdp")),
            P(None, ("dp", "fsdp")),
        ),
        out_specs=(
            P(("dp", "fsdp"), None),
            P(("dp", "fsdp"), None),
            P(None, ("dp", "fsdp"), None),
            P(None, ("dp", "fsdp"), None),
            P(None, ("dp", "fsdp")),
            P(None, ("dp", "fsdp"), None),
            P(None, ("dp", "fsdp"), None),
            P(None, ("dp", "fsdp"), None),
            P(None, ("dp", "fsdp"), None),
            P(None, ("dp", "fsdp"), None),
            P(None, ("dp", "fsdp"), None),
            P(None, ("dp", "fsdp")),
            P(None, ("dp", "fsdp")),
            P(None, ("dp", "fsdp")),
        ),
        check_vma=False,
    )
```

```python
import math

import jax
import jax.numpy as jnp
from jax import lax
from jax.experimental import pallas as pl
from jax.experimental.pallas import tpu as pltpu
from jax.sharding import PartitionSpec as P

D = 1024
FF = 2816
NS_STEPS = 5


EPS = 1e-06
NS_EPS = 1e-07
NS_A = 3.4445
NS_B = -4.775
NS_C = 2.0315
LR_MUON = 0.3
LR_GAIN = 0.1
MOMENT_DECAY = 0.5
BETA_ONE = 0.9
BETA_TWO = 0.95
ADAM_EPS = 1e-08
F32 = jnp.float32
B16 = jnp.bfloat16
ROWS_BY_ROWS = (((1,), (1,)), ((), ()))
TOKENS_OUT = (((0,), (0,)), ((), ()))


def rms_scale(series):
    return lax.rsqrt(jnp.mean(series * series, axis=-1, keepdims=True) + EPS)


def rms_back(series, factor, upstream):
    return factor * upstream - series * (factor * factor * factor) * jnp.mean(
        upstream * series, axis=-1, keepdims=True
    )


def decay_mask(segments, decay_rate):
    length = segments.shape[0]
    places = jnp.arange(length, dtype=jnp.int32)
    distance = places[:, None] - places[None, :]
    allowed = (segments[:, None] == segments[None, :]) & (distance >= 0)
    fading = jnp.exp(-decay_rate[:, None, None] * jnp.maximum(distance, 0).astype(F32)[None])
    return jnp.where(allowed[None], fading, 0.0)


def forward(tokens, segments, decay_rate, attn_full, ffn_up, gain_low):
    length, model_width = tokens.shape
    head_count = decay_rate.shape[0]
    head_size = model_width // head_count
    gain_full = gain_low.astype(F32)
    inputs = tokens.astype(F32)
    first_scale = rms_scale(inputs)
    normed = (inputs * first_scale * gain_full[0]).astype(B16)
    projected = lax.dot_general(
        normed,
        attn_full.reshape(5 * model_width, model_width),
        ROWS_BY_ROWS,
        preferred_element_type=F32,
    )
    query_act = jax.nn.relu(projected[:, :model_width]).astype(B16)
    key_act = jax.nn.relu(projected[:, model_width : 2 * model_width]).astype(B16)
    value_act = projected[:, 2 * model_width : 3 * model_width].astype(B16)
    gate_pre = projected[:, 3 * model_width : 4 * model_width]
    fading_mask = decay_mask(segments, decay_rate)
    query_heads = query_act.reshape(length, head_count, head_size)
    key_heads = key_act.reshape(length, head_count, head_size)
    value_heads = value_act.reshape(length, head_count, head_size)
    scores = jnp.einsum("the,she->hts", query_heads, key_heads, preferred_element_type=F32)
    weights_low = (scores * fading_mask).astype(B16)
    attended = jnp.einsum(
        "hts,she->the", weights_low, value_heads, preferred_element_type=F32
    ).reshape(length, model_width)
    out_scale = rms_scale(attended)
    normal_out = attended * out_scale * gain_full[2]
    gate_sig = jax.nn.sigmoid(gate_pre)
    gated_out = (normal_out * gate_sig).astype(B16)
    branch = lax.dot_general(gated_out, attn_full[4], ROWS_BY_ROWS, preferred_element_type=F32)
    middle = inputs + branch
    second_scale = rms_scale(middle)
    normed_two = (middle * second_scale * gain_full[1]).astype(B16)
    up_one, up_two = (
        lax.dot_general(normed_two, matrix, ROWS_BY_ROWS, preferred_element_type=F32) for matrix in ffn_up
    )
    product = (up_one * up_two).astype(B16)
    stored = (
        inputs,
        first_scale,
        normed,
        query_act,
        key_act,
        value_act,
        gate_pre,
        fading_mask,
        weights_low,
        attended,
        out_scale,
        normal_out,
        gate_sig,
        gated_out,
        middle,
        second_scale,
        normed_two,
        up_one,
        up_two,
        product,
    )
    return stored


def backward(stored, cotangent, attn_full, ffn_up, ffn_down, gain_low):
    (
        inputs,
        first_scale,
        normed,
        query_act,
        key_act,
        value_act,
        gate_pre,
        fading_mask,
        weights_low,
        attended,
        out_scale,
        normal_out,
        gate_sig,
        gated_out,
        middle,
        second_scale,
        normed_two,
        up_one,
        up_two,
        product,
    ) = stored
    length, model_width = inputs.shape
    head_count = fading_mask.shape[0]
    head_size = model_width // head_count
    hidden = product.shape[1]
    gain_full = gain_low.astype(F32)
    grad_out = cotangent.astype(F32)
    half = hidden // 2
    down = Halving(
        weight_grad(product[:, :half], cotangent), weight_grad(product[:, half:], cotangent)
    )
    down_out, cotangent = tied([down.payloads()], cotangent)
    down_in = down.swap(down_out)
    grad_product = lax.dot_general(cotangent, ffn_down, ROWS_BY_ROWS, preferred_element_type=F32)
    grad_one = (grad_product * up_two).astype(B16)
    grad_two = (grad_product * up_one).astype(B16)
    send_one, send_two = weight_grad(grad_one[:, half:], normed_two), weight_grad(grad_two[:, half:], normed_two)
    down_in, sends, grad_one, grad_two = tied([down_in, [send_one, send_two]], grad_one, grad_two)
    down.accept(down_in)
    one = Halving(weight_grad(grad_one[:, :half], normed_two), sends[0])
    two = Halving(weight_grad(grad_two[:, :half], normed_two), sends[1])
    one_in, two_in = one.swap(one.payloads()), two.swap(two.payloads())
    down_out, grad_one, grad_two = tied([down.payloads()], grad_one, grad_two)
    down_in = down.swap(down_out)
    grad_normed_two = jnp.dot(grad_one, ffn_up[0], preferred_element_type=F32) + jnp.dot(
        grad_two, ffn_up[1], preferred_element_type=F32
    )
    gain_two = jnp.sum(grad_normed_two * middle * second_scale, axis=0)
    grad_middle = grad_out + rms_back(middle, second_scale, grad_normed_two * gain_full[1])
    middle_low = grad_middle.astype(B16)
    down_in, one_in, two_in, middle_low = tied([down_in, one_in, two_in], middle_low)
    down.accept(down_in)
    one.accept(one_in)
    two.accept(two_in)
    down_out, one_out, two_out, middle_low = tied(
        [down.payloads(), one.payloads(), two.payloads()], middle_low
    )
    down_in, one_in, two_in = down.swap(down_out), one.swap(one_out), two.swap(two_out)
    grad_outproj = lax.dot_general(middle_low, gated_out, TOKENS_OUT, preferred_element_type=F32).astype(B16)
    proj = Halving(grad_outproj[None])
    proj_out, middle_low = tied([proj.payloads()], middle_low)
    proj_in = proj.swap(proj_out)
    grad_gated = jnp.dot(middle_low, attn_full[4], preferred_element_type=F32)
    grad_normal = grad_gated * gate_sig
    grad_gate = grad_gated * normal_out * gate_sig * (1.0 - gate_sig)
    gain_three = jnp.sum(grad_normal * attended * out_scale, axis=0)
    grad_attended = (
        rms_back(attended, out_scale, grad_normal * gain_full[2])
        .astype(B16)
    )
    down_in, proj_in, grad_attended = tied([down_in, proj_in], grad_attended)
    down.accept(down_in)
    proj.accept(proj_in)
    proj_out, grad_attended = tied([proj.payloads()], grad_attended)
    proj_in = proj.swap(proj_out)
    grad_attended = grad_attended.reshape(length, head_count, head_size)
    query_heads = query_act.reshape(length, head_count, head_size)
    key_heads = key_act.reshape(length, head_count, head_size)
    value_heads = value_act.reshape(length, head_count, head_size)
    grad_weights = jnp.einsum(
        "the,she->hts", grad_attended, value_heads, preferred_element_type=F32
    )
    grad_values = jnp.einsum(
        "hts,the->she", weights_low, grad_attended, preferred_element_type=F32
    ).reshape(length, model_width)
    grad_scores = (grad_weights * fading_mask).astype(B16)
    grad_queries = jnp.einsum(
        "hts,she->the", grad_scores, key_heads, preferred_element_type=F32
    ).reshape(length, model_width)
    grad_keys = jnp.einsum(
        "hts,the->she", grad_scores, query_heads, preferred_element_type=F32
    ).reshape(length, model_width)
    grad_mixed = jnp.concatenate(
        [
            jnp.where(query_act > 0, grad_queries, 0.0),
            jnp.where(key_act > 0, grad_keys, 0.0),
            grad_values,
            grad_gate,
        ],
        axis=1,
    ).astype(B16)
    inner = Halving(weight_grad(grad_mixed, normed).reshape(4, model_width, model_width))
    inner_out, grad_mixed = tied([inner.payloads()], grad_mixed)
    inner_in = inner.swap(inner_out)
    one_in, two_in, proj_in, inner_in, grad_mixed = tied([one_in, two_in, proj_in, inner_in], grad_mixed)
    one.accept(one_in)
    two.accept(two_in)
    proj.accept(proj_in)
    inner.accept(inner_in)
    one_out, two_out, proj_out, inner_out, grad_mixed = tied(
        [one.payloads(), two.payloads(), proj.payloads(), inner.payloads()], grad_mixed
    )
    one_in, two_in, proj_in = one.swap(one_out), two.swap(two_out), proj.swap(proj_out)
    inner_in = inner.swap(inner_out)
    grad_normed = jnp.dot(
        jnp.pad(grad_mixed, ((0, 0), (0, model_width))),
        attn_full.reshape(5 * model_width, model_width),
        preferred_element_type=F32,
    )
    gain_one = jnp.sum(grad_normed * inputs * first_scale, axis=0)
    grad_inputs = grad_middle + rms_back(inputs, first_scale, grad_normed * gain_full[0])
    grad_gain = jnp.stack([gain_one, gain_two, gain_three])
    one_in, two_in, proj_in, grad_inputs = tied([one_in, two_in, proj_in], grad_inputs)
    one.accept(one_in)
    two.accept(two_in)
    proj.accept(proj_in)
    inner.accept(inner_in)
    return (grad_inputs, (one, two, down, proj, inner), grad_gain)


def ordered(*values):
    return lax.optimization_barrier(values)


def plane_bits():
    return lax.axis_size("dp").bit_length() - 1


def swap_bit(value, bit):
    count = lax.axis_size("dp")
    return lax.ppermute(value, "dp", [(i, i ^ (1 << bit)) for i in range(count)])


def weight_grad(features, series):
    return lax.dot_general(features, series, TOKENS_OUT, preferred_element_type=F32).astype(B16)


class Halving:
    def __init__(self, grad, sent=None):
        bits = plane_bits()
        self.fixed = sent is not None
        if self.fixed:
            rows, columns = grad.shape
            self.chunk = 2 * rows // lax.axis_size("dp")
            shape = (1,) + (2,) * (bits - 1) + (self.chunk, columns)
            self.first = [sent.reshape(shape)]
            self.parts = [[(grad.reshape(shape), list(range(1, bits))[::-1])]]
        else:
            count, rows, columns = grad.shape
            self.chunk = rows // lax.axis_size("dp")
            self.first = None
            blocks = grad.reshape((count,) + (2,) * bits + (self.chunk, columns))
            self.parts = [[(blocks, list(range(bits))[::-1])]]
        self.orders = [[0]]

    def choose(self, term, dims, bit, other):
        if bit not in dims:
            return term
        if self.fixed:
            index = 1 if other else 0
        else:
            place = (lax.axis_index("dp") >> bit) & 1
            index = 1 - place if other else place
        return lax.dynamic_index_in_dim(term, index, 1 + dims.index(bit), keepdims=False)

    def payloads(self):
        if self.orders == [[]]:
            rest = list(range(1, plane_bits()))
            half = self.chunk // 2
            self.parts = [
                [(t[..., color * half : (color + 1) * half, :], dims) for t, dims in self.parts[0]]
                for color in range(2)
            ]
            self.orders = [rest, rest[::-1]]
        self.bits = [order[0] for order in self.orders]
        if self.first is not None:
            first, self.first = self.first, None
            return first
        return [
            sum(self.choose(t, dims, bit, True).astype(F32) for t, dims in part).astype(B16)
            for part, bit in zip(self.parts, self.bits)
        ]

    def swap(self, payloads):
        return [swap_bit(value, bit) for value, bit in zip(payloads, self.bits)]

    def accept(self, arrived):
        for color, (part, bit) in enumerate(zip(self.parts, self.bits)):
            left = [b for b in part[0][1] if b != bit]
            self.parts[color] = [(self.choose(t, dims, bit, False), left) for t, dims in part]
            self.parts[color].append((arrived[color], left))
            self.orders[color] = self.orders[color][1:]

    def finish(self):
        while len(self.parts) == 1 or self.orders[0]:
            self.accept(self.swap(self.payloads()))
        return jnp.concatenate([sum(t.astype(F32) for t, _ in part).astype(B16) for part in self.parts], axis=1)


def tied(lists, *values):
    flat = ordered(*[v for part in lists for v in part], *values)
    out, at = [], 0
    for part in lists:
        out.append(list(flat[at : at + len(part)]))
        at += len(part)
    return (*out, *flat[at:])


def line_gather(value):
    copies = jnp.broadcast_to(value[None], (lax.axis_size("fsdp"), *value.shape))
    return lax.all_to_all(copies, "fsdp", 0, 0, tiled=True)


def hidden_gather(line):
    lines, count, _, columns = line.shape
    rest = list(range(1, plane_bits()))
    sides = [[], []]
    for color, order in enumerate((rest, rest[::-1])):
        held = line[: lines // 2] if color == 0 else line[lines // 2 :]
        have = []
        for bit in order:
            came = swap_bit(held, bit)
            have = sorted(have + [bit], reverse=True)
            axis = have.index(bit)
            if bit == order[-1]:
                sides[0].append((held, came, axis))
                sides[1].append((swap_bit(held, 0), swap_bit(came, 0), axis))
            else:
                held = jnp.stack([held, came], axis=axis)
    out = []
    for matrix in range(count):
        halves = [
            jnp.concatenate(
                [jnp.stack([a[..., matrix, :, :], b[..., matrix, :, :]], axis=axis) for a, b, axis in side],
                axis=len(rest),
            )
            for side in sides
        ]
        out.append(jnp.stack(halves).reshape(-1, columns))
    return out


def gain_gather(value):
    rows, own = value.shape
    total = lax.axis_size("dp") * lax.axis_size("fsdp")
    copies = jnp.broadcast_to(value[None], (total, rows, own))
    every = lax.all_to_all(copies, ("dp", "fsdp"), 0, 0, tiled=True)
    return jnp.transpose(every, (1, 0, 2)).reshape(rows, total * own)


def gain_sum(grad):
    rows, columns = grad.shape
    total = lax.axis_size("dp") * lax.axis_size("fsdp")
    blocks = jnp.transpose(grad.reshape(rows, total, columns // total), (1, 0, 2))
    return jnp.sum(lax.all_to_all(blocks, ("dp", "fsdp"), 0, 0, tiled=True), axis=0)


NS_ROWS = 256


def polynomial_kernel(gram_ref, rows_ref, out_ref, gram, rest_low, poly, poly_low, current):
    size = gram_ref.shape[0]
    count = rows_ref.shape[0]
    blocks = size // NS_ROWS
    parts = count // 2

    def block(i):
        return pl.ds(pl.multiple_of(i * NS_ROWS, NS_ROWS), NS_ROWS)

    def on_diagonal(i):
        row = lax.broadcasted_iota(jnp.int32, (NS_ROWS, size), 0) + i * NS_ROWS
        return row == lax.broadcasted_iota(jnp.int32, (NS_ROWS, size), 1)

    def trace_of(ref):
        def add(i, total):
            return total + jnp.sum(jnp.where(on_diagonal(i), ref[block(i), :], 0.0))

        return lax.fori_loop(0, blocks, add, jnp.float32(0.0))

    square = jnp.full((1, 1), trace_of(gram_ref), F32)
    norm = jnp.sqrt(square) + NS_EPS
    scale = 1.0 / norm

    def start(i, carry):
        gram[block(i), :] = gram_ref[block(i), :] * (scale * scale)
        return carry

    lax.fori_loop(0, blocks, start, 0)
    current[...] = rows_ref[...].astype(F32) * scale

    def step(iteration, trace):
        shift = trace / size
        factor = NS_A + NS_B * shift + NS_C * shift * shift

        def low_rest(i, carry):
            rest_low[block(i), :] = (gram[block(i), :] - jnp.where(on_diagonal(i), shift, 0.0)).astype(B16)
            return carry

        lax.fori_loop(0, blocks, low_rest, 0)

        def polynomial(i, carry):
            eye = on_diagonal(i)
            own = gram[block(i), :]
            rest = own - jnp.where(eye, shift, 0.0)
            squared = jnp.dot(rest_low[block(i), :], rest_low[...], preferred_element_type=F32)
            squared = squared + 2.0 * shift * rest + jnp.where(eye, shift * shift, 0.0)
            value = NS_B * own + NS_C * squared + jnp.where(eye, NS_A - factor, 0.0)
            poly[block(i), :] = value
            poly_low[block(i), :] = value.astype(B16)
            return carry

        lax.fori_loop(0, blocks, polynomial, 0)

        def apply(i, carry):
            where = pl.ds(pl.multiple_of(i * parts, parts), parts)
            value = current[where, :]
            current[where, :] = factor * value + jnp.dot(
                value.astype(B16), poly_low[...], preferred_element_type=F32
            )
            return carry

        lax.fori_loop(0, 2, apply, 0)

        def next_gram(i, total):
            eye = on_diagonal(i)
            rest = gram[block(i), :] - jnp.where(eye, shift, 0.0)
            own = poly[block(i), :]
            half_way = jnp.dot(rest_low[block(i), :], poly_low[...], preferred_element_type=F32)
            half_way = half_way + shift * own + factor * rest
            value = jnp.dot(half_way.astype(B16), poly_low[...], preferred_element_type=F32)
            value = value + (shift * factor) * own + factor * half_way
            value = value + jnp.where(eye, shift * factor * factor, 0.0)
            gram[block(i), :] = value
            return total + jnp.sum(jnp.where(eye, value, 0.0))

        steps = jnp.where(iteration + 1 < NS_STEPS, blocks, 0)
        return lax.fori_loop(0, steps, next_gram, jnp.float32(0.0))

    lax.fori_loop(0, NS_STEPS, step, trace_of(gram))
    out_ref[...] = current[...].astype(B16)


def gram_orthogonalize(rows, gram):
    size = gram.shape[0]
    whole = pltpu.VMEM((size, size), F32)
    low = pltpu.VMEM((size, size), B16)
    return pl.pallas_call(
        polynomial_kernel,
        out_shape=jax.ShapeDtypeStruct(rows.shape, B16),
        in_specs=[pl.BlockSpec(memory_space=pltpu.VMEM)] * 2,
        out_specs=pl.BlockSpec(memory_space=pltpu.VMEM),
        scratch_shapes=[whole, low, whole, low, pltpu.VMEM(rows.shape, F32)],
        compiler_params=pltpu.CompilerParams(vmem_limit_bytes=48 * 1024 * 1024),
        cost_estimate=pl.CostEstimate(flops=30 * size**3, transcendentals=0, bytes_accessed=8 * size * size),
    )(gram, rows)


def one_way(value, bit, lower):
    count = lax.axis_size("dp")
    start = 1 if lower else 0
    return lax.ppermute(
        value, "dp", [(i, i ^ (1 << bit)) for i in range(count) if (i & 1) == start]
    )


def swap_core(value, bit, core):
    count = lax.axis_size("dp")
    return lax.ppermute(value, "dp", [(i, i ^ (1 << bit)) for i in range(count) if (i & 1) == core])


def gather_plane(own, other, core, late=None):
    rest = list(range(1, plane_bits()))
    held = [own[None], other[None]]
    for step in range(len(rest)):
        if late is not None and step + 1 == len(rest):
            held, late = tied([held], late)
        for color in range(2):
            bit = rest[step] if color == 0 else rest[::-1][step]
            held[color] = jnp.concatenate([held[color], swap_core(held[color], bit, core)])
    return held, late


def gram_of(held):
    return sum(
        lax.dot_general(
            part.reshape(-1, part.shape[-1]),
            part.reshape(-1, part.shape[-1]),
            TOKENS_OUT,
            preferred_element_type=F32,
        )
        for part in held
    )


def to_owners(attn, ffn):
    lines = lax.axis_size("fsdp")
    attn_count, small, columns = attn.shape
    ffn_count, large, _ = ffn.shape
    at_one = min(lines, attn_count)
    spare = attn_count - at_one
    top = [ffn]
    if spare:
        top.append(jnp.pad(attn[at_one:], ((0, 0), (0, large - small), (0, 0))))
    if lines > ffn_count + spare:
        top.append(jnp.zeros((lines - ffn_count - spare, large, columns), ffn.dtype))
    low = attn[:at_one]
    if lines > at_one:
        low = jnp.pad(low, ((0, lines - at_one), (0, 0), (0, 0)))
    return jnp.concatenate(top), low


def exchange(top, low):
    large = top.shape[1]
    both = lax.all_to_all(
        jnp.concatenate([top, low], axis=1), "fsdp", split_axis=0, concat_axis=0, tiled=True
    )
    return both[:, :large], both[:, large:]


def from_owners(top, low, ffn_count, attn_count):
    at_one = min(top.shape[0], attn_count)
    spare = attn_count - at_one
    attn = low[:at_one]
    if spare:
        attn = jnp.concatenate([attn, top[ffn_count : ffn_count + spare, : low.shape[1]]])
    return attn, top[:ffn_count]


def owner_momentum(moment, grad):
    return (MOMENT_DECAY * moment.astype(F32) + (1.0 - MOMENT_DECAY) * grad.astype(F32)).astype(B16)


def on_device(
    tokens,
    segment_ids,
    decay_rate,
    cotangent,
    attn_master,
    ffn_master,
    gains,
    attn_moment,
    ffn_moment,
    gain_first,
    gain_second,
):
    attn_low = attn_master.astype(B16)
    ffn_low = ffn_master.astype(B16)
    gain_low = gains.astype(B16)
    attn_full = lax.all_gather(attn_low, ("dp", "fsdp"), axis=1, tiled=True)
    up_line, down_low = ordered(line_gather(ffn_low[:2]), ffn_low[2:])
    ffn_up, (ffn_down,) = hidden_gather(up_line), hidden_gather(line_gather(down_low))
    gain_whole = gain_gather(gain_low)
    top_moment, low_moment = exchange(*to_owners(attn_moment.astype(B16), ffn_moment.astype(B16)))
    top_moment, low_moment, attn_full = ordered(top_moment, low_moment, attn_full)
    stored = forward(tokens, segment_ids[0], decay_rate, attn_full, ffn_up, gain_whole)
    x_grad, grads, grad_gain = backward(stored, cotangent, attn_full, ffn_up, ffn_down, gain_whole)
    one, two, down, proj, inner = grads
    lines = lax.axis_size("fsdp")
    attn_count, small, columns = attn_master.shape
    ffn_count, large, _ = ffn_master.shape
    block, little = lines * large, lines * small
    middle, product = stored[-6], stored[-1]
    ffn_sums = [value.finish() for value in (one, two, down)]
    proj_sum = proj.finish()
    out = (middle + jnp.dot(product, ffn_down, preferred_element_type=F32)).astype(B16)
    at_one = min(lines, attn_count)
    top_grad = ffn_sums
    if attn_count > at_one:
        spread = jnp.pad(proj_sum.reshape(1, lines, small, columns), ((0, 0), (0, 0), (0, large - small), (0, 0)))
        top_grad.append(spread.reshape(1, block, columns))
    top_grad = jnp.concatenate(top_grad)
    if lines > top_grad.shape[0]:
        top_grad = jnp.pad(top_grad, ((0, lines - top_grad.shape[0]), (0, 0), (0, 0)))
    top_grad = lax.psum_scatter(top_grad, "fsdp", scatter_dimension=0, tiled=True)[0]
    low_grad = inner.finish()
    if attn_count == at_one:
        low_grad = jnp.concatenate([low_grad, proj_sum])
    if lines > low_grad.shape[0]:
        low_grad = jnp.pad(low_grad, ((0, lines - low_grad.shape[0]), (0, 0), (0, 0)))
    top_grad, low_grad = ordered(top_grad, low_grad)
    low_grad = lax.psum_scatter(low_grad, "fsdp", scatter_dimension=0, tiled=True)[0]
    at_core = lax.axis_index("dp") & 1
    big = owner_momentum(top_moment.reshape(block, columns), top_grad)
    big_other = one_way(big, 0, True)
    top_held, low_grad = gather_plane(big, big_other, 0, low_grad)
    top_gram = gram_of(top_held)
    low = owner_momentum(low_moment.reshape(little, columns), low_grad)
    low_other = one_way(low, 0, False)
    low_gram = gram_of(gather_plane(low, low_other, 1)[0])
    gram = jnp.where(at_core == 0, top_gram, low_gram)
    fill = ((0, block - little), (0, 0))
    mine = jnp.concatenate(
        [
            jnp.where(at_core == 0, big, jnp.pad(low, fill)),
            jnp.where(at_core == 0, big_other, jnp.pad(low_other, fill)),
        ]
    )
    result = gram_orthogonalize(mine, gram)
    own, other = result[:block], result[block:]
    back_top = one_way(other, 0, False)
    back_low = one_way(other[:little], 0, True)
    top_orth = jnp.where(at_core == 0, own, back_top).reshape(lines, large, columns)
    low_orth = jnp.where(at_core == 0, back_low, own[:little]).reshape(lines, small, columns)
    attn_orth, ffn_orth = from_owners(*exchange(top_orth, low_orth), ffn_count, attn_count)
    attn_orth, ffn_orth = attn_orth.astype(F32), ffn_orth.astype(F32)
    attn_grad, ffn_grad = from_owners(
        *exchange(top_grad.reshape(lines, large, columns), low_grad.reshape(lines, small, columns)),
        ffn_count,
        attn_count,
    )
    attn_grad, ffn_grad = attn_grad.astype(F32), ffn_grad.astype(F32)
    attn_state = MOMENT_DECAY * attn_moment + (1.0 - MOMENT_DECAY) * attn_grad
    ffn_state = MOMENT_DECAY * ffn_moment + (1.0 - MOMENT_DECAY) * ffn_grad
    gain_grad = gain_sum(grad_gain)
    attn_new = attn_master - LR_MUON * attn_orth
    ffn_new = ffn_master - LR_MUON * math.sqrt(FF / D) * ffn_orth
    first_new = BETA_ONE * gain_first + (1.0 - BETA_ONE) * gain_grad
    second_new = BETA_TWO * gain_second + (1.0 - BETA_TWO) * gain_grad * gain_grad
    gains_new = gains - LR_GAIN * first_new / (jnp.sqrt(second_new) + ADAM_EPS)
    return (
        out,
        x_grad,
        attn_grad,
        ffn_grad,
        gain_grad,
        attn_state,
        ffn_state,
        attn_new,
        ffn_new,
        attn_new.astype(B16),
        ffn_new.astype(B16),
        gains_new,
        first_new,
        second_new,
    )


def solution(mesh):
    return jax.shard_map(
        on_device,
        mesh=mesh,
        in_specs=(
            P(("dp", "fsdp"), None),
            P(("dp", "fsdp"), None),
            P(),
            P(("dp", "fsdp"), None),
            P(None, ("dp", "fsdp"), None),
            P(None, ("dp", "fsdp"), None),
            P(None, ("dp", "fsdp")),
            P(None, ("dp", "fsdp"), None),
            P(None, ("dp", "fsdp"), None),
            P(None, ("dp", "fsdp")),
            P(None, ("dp", "fsdp")),
        ),
        out_specs=(
            P(("dp", "fsdp"), None),
            P(("dp", "fsdp"), None),
            P(None, ("dp", "fsdp"), None),
            P(None, ("dp", "fsdp"), None),
            P(None, ("dp", "fsdp")),
            P(None, ("dp", "fsdp"), None),
            P(None, ("dp", "fsdp"), None),
            P(None, ("dp", "fsdp"), None),
            P(None, ("dp", "fsdp"), None),
            P(None, ("dp", "fsdp"), None),
            P(None, ("dp", "fsdp"), None),
            P(None, ("dp", "fsdp")),
            P(None, ("dp", "fsdp")),
            P(None, ("dp", "fsdp")),
        ),
        check_vma=False,
    )
```

```python
import math

import jax
import jax.numpy as jnp
from jax import lax
from jax.experimental import pallas as pl
from jax.experimental.pallas import tpu as pltpu
from jax.sharding import PartitionSpec as P

D = 1024
FF = 2816
NS_STEPS = 5


EPS = 1e-06
NS_EPS = 1e-07
NS_A = 3.4445
NS_B = -4.775
NS_C = 2.0315
LR_MUON = 0.3
LR_GAIN = 0.1
MOMENT_DECAY = 0.5
BETA_ONE = 0.9
BETA_TWO = 0.95
ADAM_EPS = 1e-08
F32 = jnp.float32
B16 = jnp.bfloat16
ROWS_BY_ROWS = (((1,), (1,)), ((), ()))
TOKENS_OUT = (((0,), (0,)), ((), ()))


def rms_scale(series):
    return lax.rsqrt(jnp.mean(series * series, axis=-1, keepdims=True) + EPS)


def rms_back(series, factor, upstream):
    return factor * upstream - series * (factor * factor * factor) * jnp.mean(
        upstream * series, axis=-1, keepdims=True
    )


def decay_mask(segments, decay_rate):
    length = segments.shape[0]
    places = jnp.arange(length, dtype=jnp.int32)
    distance = places[:, None] - places[None, :]
    allowed = (segments[:, None] == segments[None, :]) & (distance >= 0)
    fading = jnp.exp(-decay_rate[:, None, None] * jnp.maximum(distance, 0).astype(F32)[None])
    return jnp.where(allowed[None], fading, 0.0)


def forward(tokens, segments, decay_rate, attn_full, ffn_up, gain_low, moments):
    length, model_width = tokens.shape
    head_count = decay_rate.shape[0]
    head_size = model_width // head_count
    gain_full = gain_low.astype(F32)
    inputs = tokens.astype(F32)
    first_scale = rms_scale(inputs)
    normed = (inputs * first_scale * gain_full[0]).astype(B16)
    projected = lax.dot_general(
        normed,
        attn_full.reshape(5 * model_width, model_width),
        ROWS_BY_ROWS,
        preferred_element_type=F32,
    )
    query_act = jax.nn.relu(projected[:, :model_width]).astype(B16)
    key_act = jax.nn.relu(projected[:, model_width : 2 * model_width]).astype(B16)
    value_act = projected[:, 2 * model_width : 3 * model_width].astype(B16)
    gate_pre = projected[:, 3 * model_width : 4 * model_width]
    fading_mask = decay_mask(segments, decay_rate)
    query_heads = query_act.reshape(length, head_count, head_size)
    key_heads = key_act.reshape(length, head_count, head_size)
    value_heads = value_act.reshape(length, head_count, head_size)
    scores = jnp.einsum("the,she->hts", query_heads, key_heads, preferred_element_type=F32)
    weights_low = (scores * fading_mask).astype(B16)
    attended = jnp.einsum(
        "hts,she->the", weights_low, value_heads, preferred_element_type=F32
    ).reshape(length, model_width)
    out_scale = rms_scale(attended)
    normal_out = attended * out_scale * gain_full[2]
    gate_sig = jax.nn.sigmoid(gate_pre)
    gated_out = (normal_out * gate_sig).astype(B16)
    branch = lax.dot_general(gated_out, attn_full[4], ROWS_BY_ROWS, preferred_element_type=F32)
    middle = inputs + branch
    second_scale = rms_scale(middle)
    normed_two = (middle * second_scale * gain_full[1]).astype(B16)
    moments, normed_two = tied([moments], normed_two)
    up_one, up_two = (
        lax.dot_general(normed_two, matrix, ROWS_BY_ROWS, preferred_element_type=F32) for matrix in ffn_up
    )
    product = (up_one * up_two).astype(B16)
    stored = (
        inputs,
        first_scale,
        normed,
        query_act,
        key_act,
        value_act,
        gate_pre,
        fading_mask,
        weights_low,
        attended,
        out_scale,
        normal_out,
        gate_sig,
        gated_out,
        middle,
        second_scale,
        normed_two,
        up_one,
        up_two,
        product,
    )
    return stored, moments


def backward(stored, cotangent, attn_full, ffn_up, down_gather, gain_low):
    (
        inputs,
        first_scale,
        normed,
        query_act,
        key_act,
        value_act,
        gate_pre,
        fading_mask,
        weights_low,
        attended,
        out_scale,
        normal_out,
        gate_sig,
        gated_out,
        middle,
        second_scale,
        normed_two,
        up_one,
        up_two,
        product,
    ) = stored
    length, model_width = inputs.shape
    head_count = fading_mask.shape[0]
    head_size = model_width // head_count
    hidden = product.shape[1]
    gain_full = gain_low.astype(F32)
    grad_out = cotangent.astype(F32)
    half = hidden // 2
    down = Halving(
        weight_grad(product[:, :half], cotangent), weight_grad(product[:, half:], cotangent)
    )
    down_out, down_gather.pieces, cotangent = tied([down.payloads(), down_gather.pieces], cotangent)
    down_in = down.swap(down_out)
    (ffn_down,) = down_gather.join()
    grad_product = lax.dot_general(cotangent, ffn_down, ROWS_BY_ROWS, preferred_element_type=F32)
    grad_one = (grad_product * up_two).astype(B16)
    grad_two = (grad_product * up_one).astype(B16)
    send_one, send_two = weight_grad(grad_one[:, half:], normed_two), weight_grad(grad_two[:, half:], normed_two)
    down_in, sends, grad_one, grad_two = tied([down_in, [send_one, send_two]], grad_one, grad_two)
    down.accept(down_in)
    one = Halving(weight_grad(grad_one[:, :half], normed_two), sends[0])
    two = Halving(weight_grad(grad_two[:, :half], normed_two), sends[1])
    one_in, two_in = one.swap(one.payloads()), two.swap(two.payloads())
    down_out, grad_one, grad_two = tied([down.payloads()], grad_one, grad_two)
    down_in = down.swap(down_out)
    grad_normed_two = jnp.dot(grad_one, ffn_up[0], preferred_element_type=F32) + jnp.dot(
        grad_two, ffn_up[1], preferred_element_type=F32
    )
    gain_two = jnp.sum(grad_normed_two * middle * second_scale, axis=0)
    grad_middle = grad_out + rms_back(middle, second_scale, grad_normed_two * gain_full[1])
    middle_low = grad_middle.astype(B16)
    down_in, one_in, two_in, middle_low = tied([down_in, one_in, two_in], middle_low)
    down.accept(down_in)
    one.accept(one_in)
    two.accept(two_in)
    down_out, one_out, two_out, middle_low = tied(
        [down.payloads(), one.payloads(), two.payloads()], middle_low
    )
    down_in, one_in, two_in = down.swap(down_out), one.swap(one_out), two.swap(two_out)
    grad_outproj = lax.dot_general(middle_low, gated_out, TOKENS_OUT, preferred_element_type=F32).astype(B16)
    proj = Halving(grad_outproj[None])
    proj_out, middle_low = tied([proj.payloads()], middle_low)
    proj_in = proj.swap(proj_out)
    grad_gated = jnp.dot(middle_low, attn_full[4], preferred_element_type=F32)
    grad_normal = grad_gated * gate_sig
    grad_gate = grad_gated * normal_out * gate_sig * (1.0 - gate_sig)
    gain_three = jnp.sum(grad_normal * attended * out_scale, axis=0)
    grad_attended = (
        rms_back(attended, out_scale, grad_normal * gain_full[2])
        .astype(B16)
    )
    down_in, proj_in, grad_attended = tied([down_in, proj_in], grad_attended)
    down.accept(down_in)
    proj.accept(proj_in)
    proj_out, grad_attended = tied([proj.payloads()], grad_attended)
    proj_in = proj.swap(proj_out)
    grad_attended = grad_attended.reshape(length, head_count, head_size)
    query_heads = query_act.reshape(length, head_count, head_size)
    key_heads = key_act.reshape(length, head_count, head_size)
    value_heads = value_act.reshape(length, head_count, head_size)
    grad_weights = jnp.einsum(
        "the,she->hts", grad_attended, value_heads, preferred_element_type=F32
    )
    grad_values = jnp.einsum(
        "hts,the->she", weights_low, grad_attended, preferred_element_type=F32
    ).reshape(length, model_width)
    grad_scores = (grad_weights * fading_mask).astype(B16)
    grad_queries = jnp.einsum(
        "hts,she->the", grad_scores, key_heads, preferred_element_type=F32
    ).reshape(length, model_width)
    grad_keys = jnp.einsum(
        "hts,the->she", grad_scores, query_heads, preferred_element_type=F32
    ).reshape(length, model_width)
    grad_mixed = jnp.concatenate(
        [
            jnp.where(query_act > 0, grad_queries, 0.0),
            jnp.where(key_act > 0, grad_keys, 0.0),
            grad_values,
            grad_gate,
        ],
        axis=1,
    ).astype(B16)
    inner = Halving(weight_grad(grad_mixed, normed).reshape(4, model_width, model_width))
    inner_out, grad_mixed = tied([inner.payloads()], grad_mixed)
    inner_in = inner.swap(inner_out)
    one_in, two_in, proj_in, inner_in, grad_mixed = tied([one_in, two_in, proj_in, inner_in], grad_mixed)
    one.accept(one_in)
    two.accept(two_in)
    proj.accept(proj_in)
    inner.accept(inner_in)
    one_out, two_out, proj_out, inner_out, grad_mixed = tied(
        [one.payloads(), two.payloads(), proj.payloads(), inner.payloads()], grad_mixed
    )
    one_in, two_in, proj_in = one.swap(one_out), two.swap(two_out), proj.swap(proj_out)
    inner_in = inner.swap(inner_out)
    grad_normed = jnp.dot(
        jnp.pad(grad_mixed, ((0, 0), (0, model_width))),
        attn_full.reshape(5 * model_width, model_width),
        preferred_element_type=F32,
    )
    gain_one = jnp.sum(grad_normed * inputs * first_scale, axis=0)
    grad_inputs = grad_middle + rms_back(inputs, first_scale, grad_normed * gain_full[0])
    grad_gain = jnp.stack([gain_one, gain_two, gain_three])
    one_in, two_in, proj_in, grad_inputs = tied([one_in, two_in, proj_in], grad_inputs)
    one.accept(one_in)
    two.accept(two_in)
    proj.accept(proj_in)
    inner.accept(inner_in)
    return (grad_inputs, (one, two, down, proj, inner), grad_gain, ffn_down)


def ordered(*values):
    return lax.optimization_barrier(values)


def plane_bits():
    return lax.axis_size("dp").bit_length() - 1


def swap_bit(value, bit):
    count = lax.axis_size("dp")
    return lax.ppermute(value, "dp", [(i, i ^ (1 << bit)) for i in range(count)])


def weight_grad(features, series):
    return lax.dot_general(features, series, TOKENS_OUT, preferred_element_type=F32).astype(B16)


class Halving:
    def __init__(self, grad, sent=None):
        bits = plane_bits()
        self.fixed = sent is not None
        if self.fixed:
            rows, columns = grad.shape
            self.chunk = 2 * rows // lax.axis_size("dp")
            shape = (1,) + (2,) * (bits - 1) + (self.chunk, columns)
            self.first = [sent.reshape(shape)]
            self.parts = [[(grad.reshape(shape), list(range(1, bits))[::-1])]]
        else:
            count, rows, columns = grad.shape
            self.chunk = rows // lax.axis_size("dp")
            self.first = None
            blocks = grad.reshape((count,) + (2,) * bits + (self.chunk, columns))
            self.parts = [[(blocks, list(range(bits))[::-1])]]
        self.orders = [[0]]

    def choose(self, term, dims, bit, other):
        if bit not in dims:
            return term
        if self.fixed:
            index = 1 if other else 0
        else:
            place = (lax.axis_index("dp") >> bit) & 1
            index = 1 - place if other else place
        return lax.dynamic_index_in_dim(term, index, 1 + dims.index(bit), keepdims=False)

    def payloads(self):
        if self.orders == [[]]:
            rest = list(range(1, plane_bits()))
            half = self.chunk // 2
            self.parts = [
                [(t[..., color * half : (color + 1) * half, :], dims) for t, dims in self.parts[0]]
                for color in range(2)
            ]
            self.orders = [rest, rest[::-1]]
        self.bits = [order[0] for order in self.orders]
        if self.first is not None:
            first, self.first = self.first, None
            return first
        return [
            sum(self.choose(t, dims, bit, True).astype(F32) for t, dims in part).astype(B16)
            for part, bit in zip(self.parts, self.bits)
        ]

    def swap(self, payloads):
        return [swap_bit(value, bit) for value, bit in zip(payloads, self.bits)]

    def accept(self, arrived):
        for color, (part, bit) in enumerate(zip(self.parts, self.bits)):
            left = [b for b in part[0][1] if b != bit]
            self.parts[color] = [(self.choose(t, dims, bit, False), left) for t, dims in part]
            self.parts[color].append((arrived[color], left))
            self.orders[color] = self.orders[color][1:]

    def finish(self):
        while len(self.parts) == 1 or self.orders[0]:
            self.accept(self.swap(self.payloads()))
        return jnp.concatenate([sum(t.astype(F32) for t, _ in part).astype(B16) for part in self.parts], axis=1)


def tied(lists, *values):
    flat = ordered(*[v for part in lists for v in part], *values)
    out, at = [], 0
    for part in lists:
        out.append(list(flat[at : at + len(part)]))
        at += len(part)
    return (*out, *flat[at:])


def line_gather(value):
    copies = jnp.broadcast_to(value[None], (lax.axis_size("fsdp"), *value.shape))
    return lax.all_to_all(copies, "fsdp", 0, 0, tiled=True)


class HiddenGather:
    def __init__(self, line):
        lines, self.count, _, self.columns = line.shape
        rest = list(range(1, plane_bits()))
        self.orders = (rest, rest[::-1])
        self.held, self.axes = [], []
        for color, order in enumerate(self.orders):
            held = line[: lines // 2] if color == 0 else line[lines // 2 :]
            for step, bit in enumerate(order):
                axis = sorted(order[: step + 1], reverse=True).index(bit)
                if step + 1 < len(order):
                    held = jnp.stack([held, swap_bit(held, bit)], axis=axis)
            self.held.append(held)
            self.axes.append(axis)

    def send(self):
        self.pieces = []
        for held, order in zip(self.held, self.orders):
            came = swap_bit(held, order[-1])
            self.pieces += [held, came, swap_bit(held, 0), swap_bit(came, 0)]

    def join(self):
        out = []
        for matrix in range(self.count):
            sides = []
            for side in range(2):
                halves = []
                for color, axis in enumerate(self.axes):
                    first = 4 * color + 2 * side
                    pair = [p[..., matrix, :, :] for p in self.pieces[first : first + 2]]
                    halves.append(jnp.stack(pair, axis=axis))
                sides.append(jnp.concatenate(halves, axis=len(self.orders[0])))
            out.append(jnp.stack(sides).reshape(-1, self.columns))
        return out


def gain_gather(value):
    rows, own = value.shape
    total = lax.axis_size("dp") * lax.axis_size("fsdp")
    copies = jnp.broadcast_to(value[None], (total, rows, own))
    every = lax.all_to_all(copies, ("dp", "fsdp"), 0, 0, tiled=True)
    return jnp.transpose(every, (1, 0, 2)).reshape(rows, total * own)


def gain_sum(grad):
    rows, columns = grad.shape
    total = lax.axis_size("dp") * lax.axis_size("fsdp")
    blocks = jnp.transpose(grad.reshape(rows, total, columns // total), (1, 0, 2))
    return jnp.sum(lax.all_to_all(blocks, ("dp", "fsdp"), 0, 0, tiled=True), axis=0)


NS_ROWS = 256


def polynomial_kernel(gram_ref, rows_ref, out_ref, gram, rest_low, poly, poly_low, current):
    size = gram_ref.shape[0]
    count = rows_ref.shape[0]
    blocks = size // NS_ROWS
    parts = count // 2

    def block(i):
        return pl.ds(pl.multiple_of(i * NS_ROWS, NS_ROWS), NS_ROWS)

    def on_diagonal(i):
        row = lax.broadcasted_iota(jnp.int32, (NS_ROWS, size), 0) + i * NS_ROWS
        return row == lax.broadcasted_iota(jnp.int32, (NS_ROWS, size), 1)

    def trace_of(ref):
        def add(i, total):
            return total + jnp.sum(jnp.where(on_diagonal(i), ref[block(i), :], 0.0))

        return lax.fori_loop(0, blocks, add, jnp.float32(0.0))

    square = jnp.full((1, 1), trace_of(gram_ref), F32)
    norm = jnp.sqrt(square) + NS_EPS
    scale = 1.0 / norm

    def start(i, carry):
        gram[block(i), :] = gram_ref[block(i), :] * (scale * scale)
        return carry

    lax.fori_loop(0, blocks, start, 0)
    current[...] = rows_ref[...].astype(F32) * scale

    def step(iteration, trace):
        shift = trace / size
        factor = NS_A + NS_B * shift + NS_C * shift * shift

        def low_rest(i, carry):
            rest_low[block(i), :] = (gram[block(i), :] - jnp.where(on_diagonal(i), shift, 0.0)).astype(B16)
            return carry

        lax.fori_loop(0, blocks, low_rest, 0)

        def polynomial(i, carry):
            eye = on_diagonal(i)
            own = gram[block(i), :]
            rest = own - jnp.where(eye, shift, 0.0)
            squared = jnp.dot(rest_low[block(i), :], rest_low[...], preferred_element_type=F32)
            squared = squared + 2.0 * shift * rest + jnp.where(eye, shift * shift, 0.0)
            value = NS_B * own + NS_C * squared + jnp.where(eye, NS_A - factor, 0.0)
            poly[block(i), :] = value
            poly_low[block(i), :] = value.astype(B16)
            return carry

        lax.fori_loop(0, blocks, polynomial, 0)

        def apply(i, carry):
            where = pl.ds(pl.multiple_of(i * parts, parts), parts)
            value = current[where, :]
            current[where, :] = factor * value + jnp.dot(
                value.astype(B16), poly_low[...], preferred_element_type=F32
            )
            return carry

        lax.fori_loop(0, 2, apply, 0)

        def next_gram(i, total):
            eye = on_diagonal(i)
            rest = gram[block(i), :] - jnp.where(eye, shift, 0.0)
            own = poly[block(i), :]
            half_way = jnp.dot(rest_low[block(i), :], poly_low[...], preferred_element_type=F32)
            half_way = half_way + shift * own + factor * rest
            value = jnp.dot(half_way.astype(B16), poly_low[...], preferred_element_type=F32)
            value = value + (shift * factor) * own + factor * half_way
            value = value + jnp.where(eye, shift * factor * factor, 0.0)
            gram[block(i), :] = value
            return total + jnp.sum(jnp.where(eye, value, 0.0))

        steps = jnp.where(iteration + 1 < NS_STEPS, blocks, 0)
        return lax.fori_loop(0, steps, next_gram, jnp.float32(0.0))

    lax.fori_loop(0, NS_STEPS, step, trace_of(gram))
    out_ref[...] = current[...].astype(B16)


def gram_orthogonalize(rows, gram):
    size = gram.shape[0]
    whole = pltpu.VMEM((size, size), F32)
    low = pltpu.VMEM((size, size), B16)
    return pl.pallas_call(
        polynomial_kernel,
        out_shape=jax.ShapeDtypeStruct(rows.shape, B16),
        in_specs=[pl.BlockSpec(memory_space=pltpu.VMEM)] * 2,
        out_specs=pl.BlockSpec(memory_space=pltpu.VMEM),
        scratch_shapes=[whole, low, whole, low, pltpu.VMEM(rows.shape, F32)],
        compiler_params=pltpu.CompilerParams(vmem_limit_bytes=48 * 1024 * 1024),
        cost_estimate=pl.CostEstimate(flops=30 * size**3, transcendentals=0, bytes_accessed=8 * size * size),
    )(gram, rows)


def one_way(value, bit, lower):
    count = lax.axis_size("dp")
    start = 1 if lower else 0
    return lax.ppermute(
        value, "dp", [(i, i ^ (1 << bit)) for i in range(count) if (i & 1) == start]
    )


def swap_core(value, bit, core):
    count = lax.axis_size("dp")
    return lax.ppermute(value, "dp", [(i, i ^ (1 << bit)) for i in range(count) if (i & 1) == core])


def gather_plane(own, other, core, late=None):
    rest = list(range(1, plane_bits()))
    held = [own[None], other[None]]
    for step in range(len(rest)):
        if late is not None and step + 1 == len(rest):
            held, late = tied([held], late)
        for color in range(2):
            bit = rest[step] if color == 0 else rest[::-1][step]
            held[color] = jnp.concatenate([held[color], swap_core(held[color], bit, core)])
    return held, late


def gram_of(held):
    return sum(
        lax.dot_general(
            part.reshape(-1, part.shape[-1]),
            part.reshape(-1, part.shape[-1]),
            TOKENS_OUT,
            preferred_element_type=F32,
        )
        for part in held
    )


def to_owners(attn, ffn):
    lines = lax.axis_size("fsdp")
    attn_count, small, columns = attn.shape
    ffn_count, large, _ = ffn.shape
    at_one = min(lines, attn_count)
    spare = attn_count - at_one
    top = [ffn]
    if spare:
        top.append(jnp.pad(attn[at_one:], ((0, 0), (0, large - small), (0, 0))))
    if lines > ffn_count + spare:
        top.append(jnp.zeros((lines - ffn_count - spare, large, columns), ffn.dtype))
    low = attn[:at_one]
    if lines > at_one:
        low = jnp.pad(low, ((0, lines - at_one), (0, 0), (0, 0)))
    return jnp.concatenate(top), low


def exchange(top, low):
    large = top.shape[1]
    both = lax.all_to_all(
        jnp.concatenate([top, low], axis=1), "fsdp", split_axis=0, concat_axis=0, tiled=True
    )
    return both[:, :large], both[:, large:]


def from_owners(top, low, ffn_count, attn_count):
    at_one = min(top.shape[0], attn_count)
    spare = attn_count - at_one
    attn = low[:at_one]
    if spare:
        attn = jnp.concatenate([attn, top[ffn_count : ffn_count + spare, : low.shape[1]]])
    return attn, top[:ffn_count]


def owner_momentum(moment, grad):
    return (MOMENT_DECAY * moment.astype(F32) + (1.0 - MOMENT_DECAY) * grad.astype(F32)).astype(B16)


def on_device(
    tokens,
    segment_ids,
    decay_rate,
    cotangent,
    attn_master,
    ffn_master,
    gains,
    attn_moment,
    ffn_moment,
    gain_first,
    gain_second,
):
    attn_low = attn_master.astype(B16)
    ffn_low = ffn_master.astype(B16)
    gain_low = gains.astype(B16)
    attn_full = lax.all_gather(attn_low, ("dp", "fsdp"), axis=1, tiled=True)
    gain_whole, up_low = ordered(gain_gather(gain_low), ffn_low[:2])
    up_gather = HiddenGather(line_gather(up_low))
    up_gather.held, down_low = tied([up_gather.held], ffn_low[2:])
    up_gather.send()
    down_gather = HiddenGather(line_gather(down_low))
    down_gather.send()
    ffn_up = up_gather.join()
    *moments, attn_full = ordered(*to_owners(attn_moment.astype(B16), ffn_moment.astype(B16)), attn_full)
    moments = exchange(*moments)
    stored, moments = forward(tokens, segment_ids[0], decay_rate, attn_full, ffn_up, gain_whole, moments)
    top_moment, low_moment = moments
    x_grad, grads, grad_gain, ffn_down = backward(
        stored, cotangent, attn_full, ffn_up, down_gather, gain_whole
    )
    one, two, down, proj, inner = grads
    lines = lax.axis_size("fsdp")
    attn_count, small, columns = attn_master.shape
    ffn_count, large, _ = ffn_master.shape
    block, little = lines * large, lines * small
    middle, product = stored[-6], stored[-1]
    ffn_sums = [value.finish() for value in (one, two, down)]
    proj_sum = proj.finish()
    out = (middle + jnp.dot(product, ffn_down, preferred_element_type=F32)).astype(B16)
    at_one = min(lines, attn_count)
    top_grad = ffn_sums
    if attn_count > at_one:
        spread = jnp.pad(proj_sum.reshape(1, lines, small, columns), ((0, 0), (0, 0), (0, large - small), (0, 0)))
        top_grad.append(spread.reshape(1, block, columns))
    top_grad = jnp.concatenate(top_grad)
    if lines > top_grad.shape[0]:
        top_grad = jnp.pad(top_grad, ((0, lines - top_grad.shape[0]), (0, 0), (0, 0)))
    top_grad = lax.psum_scatter(top_grad, "fsdp", scatter_dimension=0, tiled=True)[0]
    low_grad = inner.finish()
    if attn_count == at_one:
        low_grad = jnp.concatenate([low_grad, proj_sum])
    if lines > low_grad.shape[0]:
        low_grad = jnp.pad(low_grad, ((0, lines - low_grad.shape[0]), (0, 0), (0, 0)))
    top_grad, low_grad = ordered(top_grad, low_grad)
    low_grad = lax.psum_scatter(low_grad, "fsdp", scatter_dimension=0, tiled=True)[0]
    at_core = lax.axis_index("dp") & 1
    big = owner_momentum(top_moment.reshape(block, columns), top_grad)
    big_other = one_way(big, 0, True)
    top_held, low_grad = gather_plane(big, big_other, 0, low_grad)
    top_gram = gram_of(top_held)
    low = owner_momentum(low_moment.reshape(little, columns), low_grad)
    low_other = one_way(low, 0, False)
    low_gram = gram_of(gather_plane(low, low_other, 1)[0])
    gram = jnp.where(at_core == 0, top_gram, low_gram)
    fill = ((0, block - little), (0, 0))
    mine = jnp.concatenate(
        [
            jnp.where(at_core == 0, big, jnp.pad(low, fill)),
            jnp.where(at_core == 0, big_other, jnp.pad(low_other, fill)),
        ]
    )
    result = gram_orthogonalize(mine, gram)
    own, other = result[:block], result[block:]
    back_top = one_way(other, 0, False)
    back_low = one_way(other[:little], 0, True)
    top_orth = jnp.where(at_core == 0, own, back_top).reshape(lines, large, columns)
    low_orth = jnp.where(at_core == 0, back_low, own[:little]).reshape(lines, small, columns)
    attn_orth, ffn_orth = from_owners(*exchange(top_orth, low_orth), ffn_count, attn_count)
    attn_orth, ffn_orth = attn_orth.astype(F32), ffn_orth.astype(F32)
    attn_grad, ffn_grad = from_owners(
        *exchange(top_grad.reshape(lines, large, columns), low_grad.reshape(lines, small, columns)),
        ffn_count,
        attn_count,
    )
    attn_grad, ffn_grad = attn_grad.astype(F32), ffn_grad.astype(F32)
    attn_state = MOMENT_DECAY * attn_moment + (1.0 - MOMENT_DECAY) * attn_grad
    ffn_state = MOMENT_DECAY * ffn_moment + (1.0 - MOMENT_DECAY) * ffn_grad
    gain_grad = gain_sum(grad_gain)
    attn_new = attn_master - LR_MUON * attn_orth
    ffn_new = ffn_master - LR_MUON * math.sqrt(FF / D) * ffn_orth
    first_new = BETA_ONE * gain_first + (1.0 - BETA_ONE) * gain_grad
    second_new = BETA_TWO * gain_second + (1.0 - BETA_TWO) * gain_grad * gain_grad
    gains_new = gains - LR_GAIN * first_new / (jnp.sqrt(second_new) + ADAM_EPS)
    return (
        out,
        x_grad,
        attn_grad,
        ffn_grad,
        gain_grad,
        attn_state,
        ffn_state,
        attn_new,
        ffn_new,
        attn_new.astype(B16),
        ffn_new.astype(B16),
        gains_new,
        first_new,
        second_new,
    )


def solution(mesh):
    return jax.shard_map(
        on_device,
        mesh=mesh,
        in_specs=(
            P(("dp", "fsdp"), None),
            P(("dp", "fsdp"), None),
            P(),
            P(("dp", "fsdp"), None),
            P(None, ("dp", "fsdp"), None),
            P(None, ("dp", "fsdp"), None),
            P(None, ("dp", "fsdp")),
            P(None, ("dp", "fsdp"), None),
            P(None, ("dp", "fsdp"), None),
            P(None, ("dp", "fsdp")),
            P(None, ("dp", "fsdp")),
        ),
        out_specs=(
            P(("dp", "fsdp"), None),
            P(("dp", "fsdp"), None),
            P(None, ("dp", "fsdp"), None),
            P(None, ("dp", "fsdp"), None),
            P(None, ("dp", "fsdp")),
            P(None, ("dp", "fsdp"), None),
            P(None, ("dp", "fsdp"), None),
            P(None, ("dp", "fsdp"), None),
            P(None, ("dp", "fsdp"), None),
            P(None, ("dp", "fsdp"), None),
            P(None, ("dp", "fsdp"), None),
            P(None, ("dp", "fsdp")),
            P(None, ("dp", "fsdp")),
            P(None, ("dp", "fsdp")),
        ),
        check_vma=False,
    )
```

```python
import itertools
import math

import jax
import jax.numpy as jnp
from jax import lax
from jax.experimental import pallas as pl
from jax.experimental.pallas import tpu as pltpu
from jax.sharding import PartitionSpec as P

D = 1024
FF = 2816
NS_STEPS = 5


EPS = 1e-06
NS_EPS = 1e-07
NS_A = 3.4445
NS_B = -4.775
NS_C = 2.0315
LR_MUON = 0.3
LR_GAIN = 0.1
MOMENT_DECAY = 0.5
BETA_ONE = 0.9
BETA_TWO = 0.95
ADAM_EPS = 1e-08
F32 = jnp.float32
B16 = jnp.bfloat16
ROWS_BY_ROWS = (((1,), (1,)), ((), ()))
TOKENS_OUT = (((0,), (0,)), ((), ()))


def rms_scale(series):
    return lax.rsqrt(jnp.mean(series * series, axis=-1, keepdims=True) + EPS)


def rms_back(series, factor, upstream):
    return factor * upstream - series * (factor * factor * factor) * jnp.mean(
        upstream * series, axis=-1, keepdims=True
    )


def decay_mask(segments, decay_rate):
    length = segments.shape[0]
    places = jnp.arange(length, dtype=jnp.int32)
    distance = places[:, None] - places[None, :]
    allowed = (segments[:, None] == segments[None, :]) & (distance >= 0)
    fading = jnp.exp(-decay_rate[:, None, None] * jnp.maximum(distance, 0).astype(F32)[None])
    return jnp.where(allowed[None], fading, 0.0)


def forward(tokens, segments, decay_rate, attn_full, up_gather, down_line, gain_low, moments):
    length, model_width = tokens.shape
    head_count = decay_rate.shape[0]
    head_size = model_width // head_count
    gain_full = gain_low.astype(F32)
    inputs = tokens.astype(F32)
    first_scale = rms_scale(inputs)
    normed = (inputs * first_scale * gain_full[0]).astype(B16)
    projected = lax.dot_general(
        normed,
        attn_full.reshape(5 * model_width, model_width),
        ROWS_BY_ROWS,
        preferred_element_type=F32,
    )
    query_act = jax.nn.relu(projected[:, :model_width]).astype(B16)
    key_act = jax.nn.relu(projected[:, model_width : 2 * model_width]).astype(B16)
    value_act = projected[:, 2 * model_width : 3 * model_width].astype(B16)
    gate_pre = projected[:, 3 * model_width : 4 * model_width]
    fading_mask = decay_mask(segments, decay_rate)
    query_heads = query_act.reshape(length, head_count, head_size)
    key_heads = key_act.reshape(length, head_count, head_size)
    value_heads = value_act.reshape(length, head_count, head_size)
    scores = jnp.einsum("the,she->hts", query_heads, key_heads, preferred_element_type=F32)
    weights_low = (scores * fading_mask).astype(B16)
    attended = jnp.einsum(
        "hts,she->the", weights_low, value_heads, preferred_element_type=F32
    ).reshape(length, model_width)
    out_scale = rms_scale(attended)
    normal_out = attended * out_scale * gain_full[2]
    gate_sig = jax.nn.sigmoid(gate_pre)
    gated_out = (normal_out * gate_sig).astype(B16)
    up_gather.came, moments, down_line, gated_out = tied([up_gather.came, moments], down_line, gated_out)
    up_gather.cores()
    down_gather = Gather(down_line)
    moments = exchange(*moments)
    branch = lax.dot_general(gated_out, attn_full[4], ROWS_BY_ROWS, preferred_element_type=F32)
    middle = inputs + branch
    second_scale = rms_scale(middle)
    normed_two = (middle * second_scale * gain_full[1]).astype(B16)
    up_gather.pieces, down_gather.held, normed_two = tied([up_gather.pieces, down_gather.held], normed_two)
    ffn_up = up_gather.join()
    down_gather.cross()
    down_gather.cores()
    up_one, up_two = (
        lax.dot_general(normed_two, matrix, ROWS_BY_ROWS, preferred_element_type=F32) for matrix in ffn_up
    )
    product = (up_one * up_two).astype(B16)
    stored = (
        inputs,
        first_scale,
        normed,
        query_act,
        key_act,
        value_act,
        gate_pre,
        fading_mask,
        weights_low,
        attended,
        out_scale,
        normal_out,
        gate_sig,
        gated_out,
        middle,
        second_scale,
        normed_two,
        up_one,
        up_two,
        product,
    )
    return stored, down_gather, moments, ffn_up


def backward(stored, cotangent, attn_full, ffn_up, down_gather, moments, gain_low):
    (
        inputs,
        first_scale,
        normed,
        query_act,
        key_act,
        value_act,
        gate_pre,
        fading_mask,
        weights_low,
        attended,
        out_scale,
        normal_out,
        gate_sig,
        gated_out,
        middle,
        second_scale,
        normed_two,
        up_one,
        up_two,
        product,
    ) = stored
    length, model_width = inputs.shape
    head_count = fading_mask.shape[0]
    head_size = model_width // head_count
    hidden = product.shape[1]
    gain_full = gain_low.astype(F32)
    grad_out = cotangent.astype(F32)
    half = hidden // 2
    down = Halving(
        weight_grad(product[:, :half], cotangent), weight_grad(product[:, half:], cotangent)
    )
    down_out, down_gather.pieces, moments, cotangent = tied(
        [down.payloads(), down_gather.pieces, moments], cotangent
    )
    down_in = down.swap(down_out)
    (ffn_down,) = down_gather.join()
    grad_product = lax.dot_general(cotangent, ffn_down, ROWS_BY_ROWS, preferred_element_type=F32)
    grad_one = (grad_product * up_two).astype(B16)
    grad_two = (grad_product * up_one).astype(B16)
    send_one, send_two = weight_grad(grad_one[:, half:], normed_two), weight_grad(grad_two[:, half:], normed_two)
    down_in, sends, grad_one, grad_two = tied([down_in, [send_one, send_two]], grad_one, grad_two)
    down.accept(down_in)
    one = Halving(weight_grad(grad_one[:, :half], normed_two), sends[0])
    two = Halving(weight_grad(grad_two[:, :half], normed_two), sends[1])
    one_in, two_in = one.swap(one.payloads()), two.swap(two.payloads())
    down_out, grad_one, grad_two = tied([down.payloads()], grad_one, grad_two)
    down_in = down.swap(down_out)
    grad_normed_two = jnp.dot(grad_one, ffn_up[0], preferred_element_type=F32) + jnp.dot(
        grad_two, ffn_up[1], preferred_element_type=F32
    )
    gain_two = jnp.sum(grad_normed_two * middle * second_scale, axis=0)
    grad_middle = grad_out + rms_back(middle, second_scale, grad_normed_two * gain_full[1])
    middle_low = grad_middle.astype(B16)
    down_in, one_in, two_in, middle_low = tied([down_in, one_in, two_in], middle_low)
    down.accept(down_in)
    one.accept(one_in)
    two.accept(two_in)
    down_out, one_out, two_out, middle_low = tied(
        [down.payloads(), one.payloads(), two.payloads()], middle_low
    )
    down_in, one_in, two_in = down.swap(down_out), one.swap(one_out), two.swap(two_out)
    grad_outproj = lax.dot_general(middle_low, gated_out, TOKENS_OUT, preferred_element_type=F32).astype(B16)
    proj = Halving(grad_outproj[None])
    proj_out, middle_low = tied([proj.payloads()], middle_low)
    proj_in = proj.swap(proj_out)
    grad_gated = jnp.dot(middle_low, attn_full[4], preferred_element_type=F32)
    grad_normal = grad_gated * gate_sig
    grad_gate = grad_gated * normal_out * gate_sig * (1.0 - gate_sig)
    gain_three = jnp.sum(grad_normal * attended * out_scale, axis=0)
    grad_attended = (
        rms_back(attended, out_scale, grad_normal * gain_full[2])
        .astype(B16)
    )
    down_in, proj_in, grad_attended = tied([down_in, proj_in], grad_attended)
    down.accept(down_in)
    proj.accept(proj_in)
    proj_out, grad_attended = tied([proj.payloads()], grad_attended)
    proj_in = proj.swap(proj_out)
    grad_attended = grad_attended.reshape(length, head_count, head_size)
    query_heads = query_act.reshape(length, head_count, head_size)
    key_heads = key_act.reshape(length, head_count, head_size)
    value_heads = value_act.reshape(length, head_count, head_size)
    grad_weights = jnp.einsum(
        "the,she->hts", grad_attended, value_heads, preferred_element_type=F32
    )
    grad_values = jnp.einsum(
        "hts,the->she", weights_low, grad_attended, preferred_element_type=F32
    ).reshape(length, model_width)
    grad_scores = (grad_weights * fading_mask).astype(B16)
    grad_queries = jnp.einsum(
        "hts,she->the", grad_scores, key_heads, preferred_element_type=F32
    ).reshape(length, model_width)
    grad_keys = jnp.einsum(
        "hts,the->she", grad_scores, query_heads, preferred_element_type=F32
    ).reshape(length, model_width)
    grad_mixed = jnp.concatenate(
        [
            jnp.where(query_act > 0, grad_queries, 0.0),
            jnp.where(key_act > 0, grad_keys, 0.0),
            grad_values,
            grad_gate,
        ],
        axis=1,
    ).astype(B16)
    inner = Halving(weight_grad(grad_mixed, normed).reshape(4, model_width, model_width))
    inner_out, grad_mixed = tied([inner.payloads()], grad_mixed)
    inner_in = inner.swap(inner_out)
    one_in, two_in, proj_in, inner_in, grad_mixed = tied([one_in, two_in, proj_in, inner_in], grad_mixed)
    one.accept(one_in)
    two.accept(two_in)
    proj.accept(proj_in)
    inner.accept(inner_in)
    one_out, two_out, proj_out, inner_out, grad_mixed = tied(
        [one.payloads(), two.payloads(), proj.payloads(), inner.payloads()], grad_mixed
    )
    one_in, two_in, proj_in = one.swap(one_out), two.swap(two_out), proj.swap(proj_out)
    inner_in = inner.swap(inner_out)
    grad_normed = jnp.dot(
        jnp.pad(grad_mixed, ((0, 0), (0, model_width))),
        attn_full.reshape(5 * model_width, model_width),
        preferred_element_type=F32,
    )
    gain_one = jnp.sum(grad_normed * inputs * first_scale, axis=0)
    grad_inputs = grad_middle + rms_back(inputs, first_scale, grad_normed * gain_full[0])
    grad_gain = jnp.stack([gain_one, gain_two, gain_three])
    one_in, two_in, proj_in, grad_inputs = tied([one_in, two_in, proj_in], grad_inputs)
    one.accept(one_in)
    two.accept(two_in)
    proj.accept(proj_in)
    inner.accept(inner_in)
    return (grad_inputs, (one, two, down, proj, inner), grad_gain, ffn_down, moments)


def ordered(*values):
    return lax.optimization_barrier(values)


def plane_bits():
    return lax.axis_size("dp").bit_length() - 1


def swap_bit(value, bit):
    count = lax.axis_size("dp")
    return lax.ppermute(value, "dp", [(i, i ^ (1 << bit)) for i in range(count)])


def weight_grad(features, series):
    return lax.dot_general(features, series, TOKENS_OUT, preferred_element_type=F32).astype(B16)


class Halving:
    def __init__(self, grad, sent=None):
        bits = plane_bits()
        self.fixed = sent is not None
        if self.fixed:
            rows, columns = grad.shape
            self.chunk = 2 * rows // lax.axis_size("dp")
            shape = (1,) + (2,) * (bits - 1) + (self.chunk, columns)
            self.first = [sent.reshape(shape)]
            self.parts = [[(grad.reshape(shape), list(range(1, bits))[::-1])]]
        else:
            count, rows, columns = grad.shape
            self.chunk = rows // lax.axis_size("dp")
            self.first = None
            blocks = grad.reshape((count,) + (2,) * bits + (self.chunk, columns))
            self.parts = [[(blocks, list(range(bits))[::-1])]]
        self.orders = [[0]]

    def choose(self, term, dims, bit, other):
        if bit not in dims:
            return term
        if self.fixed:
            index = 1 if other else 0
        else:
            place = (lax.axis_index("dp") >> bit) & 1
            index = 1 - place if other else place
        return lax.dynamic_index_in_dim(term, index, 1 + dims.index(bit), keepdims=False)

    def payloads(self):
        if self.orders == [[]]:
            rest = list(range(1, plane_bits()))
            half = self.chunk // 2
            self.parts = [
                [(t[..., color * half : (color + 1) * half, :], dims) for t, dims in self.parts[0]]
                for color in range(2)
            ]
            self.orders = [rest, rest[::-1]]
        self.bits = [order[0] for order in self.orders]
        if self.first is not None:
            first, self.first = self.first, None
            return first
        return [
            sum(self.choose(t, dims, bit, True).astype(F32) for t, dims in part).astype(B16)
            for part, bit in zip(self.parts, self.bits)
        ]

    def swap(self, payloads):
        return [swap_bit(value, bit) for value, bit in zip(payloads, self.bits)]

    def accept(self, arrived):
        for color, (part, bit) in enumerate(zip(self.parts, self.bits)):
            left = [b for b in part[0][1] if b != bit]
            self.parts[color] = [(self.choose(t, dims, bit, False), left) for t, dims in part]
            self.parts[color].append((arrived[color], left))
            self.orders[color] = self.orders[color][1:]

    def finish(self):
        while len(self.parts) == 1 or self.orders[0]:
            self.accept(self.swap(self.payloads()))
        return jnp.concatenate([sum(t.astype(F32) for t, _ in part).astype(B16) for part in self.parts], axis=1)


def tied(lists, *values):
    flat = ordered(*[v for part in lists for v in part], *values)
    out, at = [], 0
    for part in lists:
        out.append(list(flat[at : at + len(part)]))
        at += len(part)
    return (*out, *flat[at:])


def line_gather(value):
    copies = jnp.broadcast_to(value[None], (lax.axis_size("fsdp"), *value.shape))
    return lax.all_to_all(copies, "fsdp", 0, 0, tiled=True)


class Gather:
    def __init__(self, line):
        lines, self.count, _, self.columns = line.shape
        rest = list(range(1, plane_bits()))
        self.orders = (rest, rest[::-1])
        self.held, self.axes = [], []
        for color, order in enumerate(self.orders):
            held = line[: lines // 2] if color == 0 else line[lines // 2 :]
            for step, bit in enumerate(order):
                axis = sorted(order[: step + 1], reverse=True).index(bit)
                if step + 1 < len(order):
                    held = jnp.stack([held, swap_bit(held, bit)], axis=axis)
            self.held.append(held)
            self.axes.append(axis)

    def cross(self):
        self.came = [swap_bit(held, order[-1]) for held, order in zip(self.held, self.orders)]

    def cores(self):
        self.pieces = []
        for held, came in zip(self.held, self.came):
            self.pieces += [held, came, swap_bit(held, 0), swap_bit(came, 0)]

    def natural(self):
        half, _, own, _ = self.held[0].shape[-4:]
        planes = lax.axis_size("dp")
        whole = jnp.zeros((self.count, planes, 2 * half, own, self.columns), self.held[0].dtype)
        for number in range(4):
            for color, order in enumerate(self.orders):
                piece = self.pieces[4 * color + number]
                bits = sorted(order[:-1], reverse=True)
                base = (1 << order[-1]) * (number % 2) + number // 2
                for index in itertools.product(range(2), repeat=len(bits)):
                    place = base + sum(value << bit for value, bit in zip(index, bits))
                    block = jnp.swapaxes(piece[index], 0, 1)[:, None]
                    where = (0, lax.axis_index("dp") ^ place, color * half, 0, 0)
                    whole = lax.dynamic_update_slice(whole, block, where)
        return whole.reshape(self.count, -1, self.columns)

    def join(self):
        out = []
        for matrix in range(self.count):
            sides = []
            for side in range(2):
                halves = []
                for color, axis in enumerate(self.axes):
                    first = 4 * color + 2 * side
                    pair = [p[..., matrix, :, :] for p in self.pieces[first : first + 2]]
                    halves.append(jnp.stack(pair, axis=axis))
                sides.append(jnp.concatenate(halves, axis=len(self.orders[0])))
            out.append(jnp.stack(sides).reshape(-1, self.columns))
        return out


def gain_gather(value):
    rows, own = value.shape
    total = lax.axis_size("dp") * lax.axis_size("fsdp")
    copies = jnp.broadcast_to(value[None], (total, rows, own))
    every = lax.all_to_all(copies, ("dp", "fsdp"), 0, 0, tiled=True)
    return jnp.transpose(every, (1, 0, 2)).reshape(rows, total * own)


def gain_sum(grad):
    rows, columns = grad.shape
    total = lax.axis_size("dp") * lax.axis_size("fsdp")
    blocks = jnp.transpose(grad.reshape(rows, total, columns // total), (1, 0, 2))
    return jnp.sum(lax.all_to_all(blocks, ("dp", "fsdp"), 0, 0, tiled=True), axis=0)


NS_ROWS = 256


def polynomial_kernel(gram_ref, rows_ref, out_ref, gram, rest_low, poly, poly_low, current):
    size = gram_ref.shape[0]
    count = rows_ref.shape[0]
    blocks = size // NS_ROWS
    parts = count // 2

    def block(i):
        return pl.ds(pl.multiple_of(i * NS_ROWS, NS_ROWS), NS_ROWS)

    def on_diagonal(i):
        row = lax.broadcasted_iota(jnp.int32, (NS_ROWS, size), 0) + i * NS_ROWS
        return row == lax.broadcasted_iota(jnp.int32, (NS_ROWS, size), 1)

    def trace_of(ref):
        def add(i, total):
            return total + jnp.sum(jnp.where(on_diagonal(i), ref[block(i), :], 0.0))

        return lax.fori_loop(0, blocks, add, jnp.float32(0.0))

    square = jnp.full((1, 1), trace_of(gram_ref), F32)
    norm = jnp.sqrt(square) + NS_EPS
    scale = 1.0 / norm

    def start(i, carry):
        gram[block(i), :] = gram_ref[block(i), :] * (scale * scale)
        return carry

    lax.fori_loop(0, blocks, start, 0)
    current[...] = rows_ref[...].astype(F32) * scale

    def step(iteration, trace):
        shift = trace / size
        factor = NS_A + NS_B * shift + NS_C * shift * shift

        def low_rest(i, carry):
            rest_low[block(i), :] = (gram[block(i), :] - jnp.where(on_diagonal(i), shift, 0.0)).astype(B16)
            return carry

        lax.fori_loop(0, blocks, low_rest, 0)

        def polynomial(i, carry):
            eye = on_diagonal(i)
            own = gram[block(i), :]
            rest = own - jnp.where(eye, shift, 0.0)
            squared = jnp.dot(rest_low[block(i), :], rest_low[...], preferred_element_type=F32)
            squared = squared + 2.0 * shift * rest + jnp.where(eye, shift * shift, 0.0)
            value = NS_B * own + NS_C * squared + jnp.where(eye, NS_A - factor, 0.0)
            poly[block(i), :] = value
            poly_low[block(i), :] = value.astype(B16)
            return carry

        lax.fori_loop(0, blocks, polynomial, 0)

        def apply(i, carry):
            where = pl.ds(pl.multiple_of(i * parts, parts), parts)
            value = current[where, :]
            current[where, :] = factor * value + jnp.dot(
                value.astype(B16), poly_low[...], preferred_element_type=F32
            )
            return carry

        lax.fori_loop(0, 2, apply, 0)

        def next_gram(i, total):
            eye = on_diagonal(i)
            rest = gram[block(i), :] - jnp.where(eye, shift, 0.0)
            own = poly[block(i), :]
            half_way = jnp.dot(rest_low[block(i), :], poly_low[...], preferred_element_type=F32)
            half_way = half_way + shift * own + factor * rest
            value = jnp.dot(half_way.astype(B16), poly_low[...], preferred_element_type=F32)
            value = value + (shift * factor) * own + factor * half_way
            value = value + jnp.where(eye, shift * factor * factor, 0.0)
            gram[block(i), :] = value
            return total + jnp.sum(jnp.where(eye, value, 0.0))

        steps = jnp.where(iteration + 1 < NS_STEPS, blocks, 0)
        return lax.fori_loop(0, steps, next_gram, jnp.float32(0.0))

    lax.fori_loop(0, NS_STEPS, step, trace_of(gram))
    out_ref[...] = current[...].astype(B16)


def gram_orthogonalize(rows, gram):
    size = gram.shape[0]
    whole = pltpu.VMEM((size, size), F32)
    low = pltpu.VMEM((size, size), B16)
    return pl.pallas_call(
        polynomial_kernel,
        out_shape=jax.ShapeDtypeStruct(rows.shape, B16),
        in_specs=[pl.BlockSpec(memory_space=pltpu.VMEM)] * 2,
        out_specs=pl.BlockSpec(memory_space=pltpu.VMEM),
        scratch_shapes=[whole, low, whole, low, pltpu.VMEM(rows.shape, F32)],
        compiler_params=pltpu.CompilerParams(vmem_limit_bytes=48 * 1024 * 1024),
        cost_estimate=pl.CostEstimate(flops=30 * size**3, transcendentals=0, bytes_accessed=8 * size * size),
    )(gram, rows)


def one_way(value, bit, lower):
    count = lax.axis_size("dp")
    start = 1 if lower else 0
    return lax.ppermute(
        value, "dp", [(i, i ^ (1 << bit)) for i in range(count) if (i & 1) == start]
    )


def swap_core(value, bit, core):
    count = lax.axis_size("dp")
    return lax.ppermute(value, "dp", [(i, i ^ (1 << bit)) for i in range(count) if (i & 1) == core])


def gather_plane(own, other, core, late=None):
    rest = list(range(1, plane_bits()))
    held = [own[None], other[None]]
    for step in range(len(rest)):
        if late is not None and step + 1 == len(rest):
            held, late = tied([held], late)
        for color in range(2):
            bit = rest[step] if color == 0 else rest[::-1][step]
            held[color] = jnp.concatenate([held[color], swap_core(held[color], bit, core)])
    return held, late


def gram_of(held):
    return sum(
        lax.dot_general(
            part.reshape(-1, part.shape[-1]),
            part.reshape(-1, part.shape[-1]),
            TOKENS_OUT,
            preferred_element_type=F32,
        )
        for part in held
    )


def to_owners(attn, ffn):
    lines = lax.axis_size("fsdp")
    attn_count, small, columns = attn.shape
    ffn_count, large, _ = ffn.shape
    at_one = min(lines, attn_count)
    spare = attn_count - at_one
    top = [ffn]
    if spare:
        top.append(jnp.pad(attn[at_one:], ((0, 0), (0, large - small), (0, 0))))
    if lines > ffn_count + spare:
        top.append(jnp.zeros((lines - ffn_count - spare, large, columns), ffn.dtype))
    low = attn[:at_one]
    if lines > at_one:
        low = jnp.pad(low, ((0, lines - at_one), (0, 0), (0, 0)))
    return jnp.concatenate(top), low


def exchange(top, low):
    large = top.shape[1]
    both = lax.all_to_all(
        jnp.concatenate([top, low], axis=1), "fsdp", split_axis=0, concat_axis=0, tiled=True
    )
    return both[:, :large], both[:, large:]


def from_owners(top, low, ffn_count, attn_count):
    at_one = min(top.shape[0], attn_count)
    spare = attn_count - at_one
    attn = low[:at_one]
    if spare:
        attn = jnp.concatenate([attn, top[ffn_count : ffn_count + spare, : low.shape[1]]])
    return attn, top[:ffn_count]


def owner_momentum(moment, grad):
    return (MOMENT_DECAY * moment.astype(F32) + (1.0 - MOMENT_DECAY) * grad.astype(F32)).astype(B16)


def on_device(
    tokens,
    segment_ids,
    decay_rate,
    cotangent,
    attn_master,
    ffn_master,
    gains,
    attn_moment,
    ffn_moment,
    gain_first,
    gain_second,
):
    attn_low = attn_master.astype(B16)
    ffn_low = ffn_master.astype(B16)
    gain_low = gains.astype(B16)
    gain_whole, attn_low = ordered(gain_gather(gain_low), attn_low)
    attn_gather = Gather(line_gather(attn_low))
    attn_gather.held, up_low = tied([attn_gather.held], ffn_low[:2])
    attn_gather.cross()
    attn_gather.cores()
    up_gather = Gather(line_gather(up_low))
    attn_full = attn_gather.natural()
    moments = to_owners(attn_moment.astype(B16), ffn_moment.astype(B16))
    up_gather.held, moments, down_low, attn_full = tied([up_gather.held, moments], ffn_low[2:], attn_full)
    up_gather.cross()
    stored, down_gather, moments, ffn_up = forward(
        tokens, segment_ids[0], decay_rate, attn_full, up_gather, line_gather(down_low), gain_whole, moments
    )
    x_grad, grads, grad_gain, ffn_down, (top_moment, low_moment) = backward(
        stored, cotangent, attn_full, ffn_up, down_gather, moments, gain_whole
    )
    one, two, down, proj, inner = grads
    lines = lax.axis_size("fsdp")
    attn_count, small, columns = attn_master.shape
    ffn_count, large, _ = ffn_master.shape
    block, little = lines * large, lines * small
    middle, product = stored[-6], stored[-1]
    ffn_sums = [value.finish() for value in (one, two, down)]
    proj_sum = proj.finish()
    out = (middle + jnp.dot(product, ffn_down, preferred_element_type=F32)).astype(B16)
    at_one = min(lines, attn_count)
    top_grad = ffn_sums
    if attn_count > at_one:
        spread = jnp.pad(proj_sum.reshape(1, lines, small, columns), ((0, 0), (0, 0), (0, large - small), (0, 0)))
        top_grad.append(spread.reshape(1, block, columns))
    top_grad = jnp.concatenate(top_grad)
    if lines > top_grad.shape[0]:
        top_grad = jnp.pad(top_grad, ((0, lines - top_grad.shape[0]), (0, 0), (0, 0)))
    top_grad = lax.psum_scatter(top_grad, "fsdp", scatter_dimension=0, tiled=True)[0]
    low_grad = inner.finish()
    if attn_count == at_one:
        low_grad = jnp.concatenate([low_grad, proj_sum])
    if lines > low_grad.shape[0]:
        low_grad = jnp.pad(low_grad, ((0, lines - low_grad.shape[0]), (0, 0), (0, 0)))
    top_grad, low_grad = ordered(top_grad, low_grad)
    low_grad = lax.psum_scatter(low_grad, "fsdp", scatter_dimension=0, tiled=True)[0]
    at_core = lax.axis_index("dp") & 1
    big = owner_momentum(top_moment.reshape(block, columns), top_grad)
    big_other = one_way(big, 0, True)
    top_held, low_grad = gather_plane(big, big_other, 0, low_grad)
    top_gram = gram_of(top_held)
    low = owner_momentum(low_moment.reshape(little, columns), low_grad)
    low_other = one_way(low, 0, False)
    low_gram = gram_of(gather_plane(low, low_other, 1)[0])
    gram = jnp.where(at_core == 0, top_gram, low_gram)
    fill = ((0, block - little), (0, 0))
    mine = jnp.concatenate(
        [
            jnp.where(at_core == 0, big, jnp.pad(low, fill)),
            jnp.where(at_core == 0, big_other, jnp.pad(low_other, fill)),
        ]
    )
    result = gram_orthogonalize(mine, gram)
    own, other = result[:block], result[block:]
    back_top = one_way(other, 0, False)
    back_low = one_way(other[:little], 0, True)
    top_orth = jnp.where(at_core == 0, own, back_top).reshape(lines, large, columns)
    low_orth = jnp.where(at_core == 0, back_low, own[:little]).reshape(lines, small, columns)
    attn_orth, ffn_orth = from_owners(*exchange(top_orth, low_orth), ffn_count, attn_count)
    attn_orth, ffn_orth = attn_orth.astype(F32), ffn_orth.astype(F32)
    attn_grad, ffn_grad = from_owners(
        *exchange(top_grad.reshape(lines, large, columns), low_grad.reshape(lines, small, columns)),
        ffn_count,
        attn_count,
    )
    attn_grad, ffn_grad = attn_grad.astype(F32), ffn_grad.astype(F32)
    attn_state = MOMENT_DECAY * attn_moment + (1.0 - MOMENT_DECAY) * attn_grad
    ffn_state = MOMENT_DECAY * ffn_moment + (1.0 - MOMENT_DECAY) * ffn_grad
    gain_grad = gain_sum(grad_gain)
    attn_new = attn_master - LR_MUON * attn_orth
    ffn_new = ffn_master - LR_MUON * math.sqrt(FF / D) * ffn_orth
    first_new = BETA_ONE * gain_first + (1.0 - BETA_ONE) * gain_grad
    second_new = BETA_TWO * gain_second + (1.0 - BETA_TWO) * gain_grad * gain_grad
    gains_new = gains - LR_GAIN * first_new / (jnp.sqrt(second_new) + ADAM_EPS)
    return (
        out,
        x_grad,
        attn_grad,
        ffn_grad,
        gain_grad,
        attn_state,
        ffn_state,
        attn_new,
        ffn_new,
        attn_new.astype(B16),
        ffn_new.astype(B16),
        gains_new,
        first_new,
        second_new,
    )


def solution(mesh):
    return jax.shard_map(
        on_device,
        mesh=mesh,
        in_specs=(
            P(("dp", "fsdp"), None),
            P(("dp", "fsdp"), None),
            P(),
            P(("dp", "fsdp"), None),
            P(None, ("dp", "fsdp"), None),
            P(None, ("dp", "fsdp"), None),
            P(None, ("dp", "fsdp")),
            P(None, ("dp", "fsdp"), None),
            P(None, ("dp", "fsdp"), None),
            P(None, ("dp", "fsdp")),
            P(None, ("dp", "fsdp")),
        ),
        out_specs=(
            P(("dp", "fsdp"), None),
            P(("dp", "fsdp"), None),
            P(None, ("dp", "fsdp"), None),
            P(None, ("dp", "fsdp"), None),
            P(None, ("dp", "fsdp")),
            P(None, ("dp", "fsdp"), None),
            P(None, ("dp", "fsdp"), None),
            P(None, ("dp", "fsdp"), None),
            P(None, ("dp", "fsdp"), None),
            P(None, ("dp", "fsdp"), None),
            P(None, ("dp", "fsdp"), None),
            P(None, ("dp", "fsdp")),
            P(None, ("dp", "fsdp")),
            P(None, ("dp", "fsdp")),
        ),
        check_vma=False,
    )
```

```python
import itertools
import math

import jax
import jax.numpy as jnp
from jax import lax
from jax.experimental import pallas as pl
from jax.experimental.pallas import tpu as pltpu
from jax.sharding import PartitionSpec as P

D = 1024
FF = 2816
NS_STEPS = 5


EPS = 1e-06
NS_EPS = 1e-07
NS_A = 3.4445
NS_B = -4.775
NS_C = 2.0315
LR_MUON = 0.3
LR_GAIN = 0.1
MOMENT_DECAY = 0.5
BETA_ONE = 0.9
BETA_TWO = 0.95
ADAM_EPS = 1e-08
F32 = jnp.float32
B16 = jnp.bfloat16
ROWS_BY_ROWS = (((1,), (1,)), ((), ()))
TOKENS_OUT = (((0,), (0,)), ((), ()))


def rms_scale(series):
    return lax.rsqrt(jnp.mean(series * series, axis=-1, keepdims=True) + EPS)


def rms_back(series, factor, upstream):
    return factor * upstream - series * (factor * factor * factor) * jnp.mean(
        upstream * series, axis=-1, keepdims=True
    )


def decay_mask(segments, decay_rate):
    length = segments.shape[0]
    places = jnp.arange(length, dtype=jnp.int32)
    distance = places[:, None] - places[None, :]
    allowed = (segments[:, None] == segments[None, :]) & (distance >= 0)
    fading = jnp.exp(-decay_rate[:, None, None] * jnp.maximum(distance, 0).astype(F32)[None])
    return jnp.where(allowed[None], fading, 0.0)


def forward(tokens, segments, decay_rate, attn_full, up_gathers, down_line, gain_low, moments):
    length, model_width = tokens.shape
    head_count = decay_rate.shape[0]
    head_size = model_width // head_count
    gain_full = gain_low.astype(F32)
    inputs = tokens.astype(F32)
    first_scale = rms_scale(inputs)
    normed = (inputs * first_scale * gain_full[0]).astype(B16)
    projected = lax.dot_general(
        normed,
        attn_full.reshape(5 * model_width, model_width),
        ROWS_BY_ROWS,
        preferred_element_type=F32,
    )
    query_act = jax.nn.relu(projected[:, :model_width]).astype(B16)
    key_act = jax.nn.relu(projected[:, model_width : 2 * model_width]).astype(B16)
    value_act = projected[:, 2 * model_width : 3 * model_width].astype(B16)
    gate_pre = projected[:, 3 * model_width : 4 * model_width]
    fading_mask = decay_mask(segments, decay_rate)
    query_heads = query_act.reshape(length, head_count, head_size)
    key_heads = key_act.reshape(length, head_count, head_size)
    value_heads = value_act.reshape(length, head_count, head_size)
    scores = jnp.einsum("the,she->hts", query_heads, key_heads, preferred_element_type=F32)
    weights_low = (scores * fading_mask).astype(B16)
    attended = jnp.einsum(
        "hts,she->the", weights_low, value_heads, preferred_element_type=F32
    ).reshape(length, model_width)
    out_scale = rms_scale(attended)
    normal_out = attended * out_scale * gain_full[2]
    gate_sig = jax.nn.sigmoid(gate_pre)
    gated_out = (normal_out * gate_sig).astype(B16)
    one_gather, two_gather = up_gathers
    one_gather.came, two_gather.came, moments, down_line, gated_out = tied(
        [one_gather.came, two_gather.came, moments], down_line, gated_out
    )
    one_gather.cores()
    two_gather.cores()
    down_gather = Gather(down_line)
    moments = exchange(*moments)
    branch = lax.dot_general(gated_out, attn_full[4], ROWS_BY_ROWS, preferred_element_type=F32)
    middle = inputs + branch
    second_scale = rms_scale(middle)
    normed_two = (middle * second_scale * gain_full[1]).astype(B16)
    one_gather.pieces, two_gather.pieces, down_gather.held, normed_two = tied(
        [one_gather.pieces, two_gather.pieces, down_gather.held], normed_two
    )
    ffn_up = one_gather.join() + two_gather.join()
    down_gather.cross()
    down_gather.cores()
    up_one, up_two = (
        lax.dot_general(normed_two, matrix, ROWS_BY_ROWS, preferred_element_type=F32) for matrix in ffn_up
    )
    product = (up_one * up_two).astype(B16)
    stored = (
        inputs,
        first_scale,
        normed,
        query_act,
        key_act,
        value_act,
        gate_pre,
        fading_mask,
        weights_low,
        attended,
        out_scale,
        normal_out,
        gate_sig,
        gated_out,
        middle,
        second_scale,
        normed_two,
        up_one,
        up_two,
        product,
    )
    return stored, down_gather, moments, ffn_up


def backward(stored, cotangent, attn_full, ffn_up, down_gather, moments, gain_low):
    (
        inputs,
        first_scale,
        normed,
        query_act,
        key_act,
        value_act,
        gate_pre,
        fading_mask,
        weights_low,
        attended,
        out_scale,
        normal_out,
        gate_sig,
        gated_out,
        middle,
        second_scale,
        normed_two,
        up_one,
        up_two,
        product,
    ) = stored
    length, model_width = inputs.shape
    head_count = fading_mask.shape[0]
    head_size = model_width // head_count
    hidden = product.shape[1]
    gain_full = gain_low.astype(F32)
    grad_out = cotangent.astype(F32)
    half = hidden // 2
    down = Halving(
        weight_grad(product[:, :half], cotangent), weight_grad(product[:, half:], cotangent)
    )
    down_out, down_gather.pieces, moments, cotangent = tied(
        [down.payloads(), down_gather.pieces, moments], cotangent
    )
    down_in = down.swap(down_out)
    (ffn_down,) = down_gather.join()
    grad_product = lax.dot_general(cotangent, ffn_down, ROWS_BY_ROWS, preferred_element_type=F32)
    grad_one = (grad_product * up_two).astype(B16)
    grad_two = (grad_product * up_one).astype(B16)
    send_one, send_two = weight_grad(grad_one[:, half:], normed_two), weight_grad(grad_two[:, half:], normed_two)
    down_in, sends, grad_one, grad_two = tied([down_in, [send_one, send_two]], grad_one, grad_two)
    down.accept(down_in)
    one = Halving(weight_grad(grad_one[:, :half], normed_two), sends[0])
    two = Halving(weight_grad(grad_two[:, :half], normed_two), sends[1])
    one_in, two_in = one.swap(one.payloads()), two.swap(two.payloads())
    down_out, grad_one, grad_two = tied([down.payloads()], grad_one, grad_two)
    down_in = down.swap(down_out)
    grad_normed_two = jnp.dot(grad_one, ffn_up[0], preferred_element_type=F32) + jnp.dot(
        grad_two, ffn_up[1], preferred_element_type=F32
    )
    gain_two = jnp.sum(grad_normed_two * middle * second_scale, axis=0)
    grad_middle = grad_out + rms_back(middle, second_scale, grad_normed_two * gain_full[1])
    middle_low = grad_middle.astype(B16)
    down_in, one_in, two_in, middle_low = tied([down_in, one_in, two_in], middle_low)
    down.accept(down_in)
    one.accept(one_in)
    two.accept(two_in)
    down_out, one_out, two_out, middle_low = tied(
        [down.payloads(), one.payloads(), two.payloads()], middle_low
    )
    down_in, one_in, two_in = down.swap(down_out), one.swap(one_out), two.swap(two_out)
    grad_outproj = lax.dot_general(middle_low, gated_out, TOKENS_OUT, preferred_element_type=F32).astype(B16)
    proj = Halving(grad_outproj[None])
    proj_out, middle_low = tied([proj.payloads()], middle_low)
    proj_in = proj.swap(proj_out)
    grad_gated = jnp.dot(middle_low, attn_full[4], preferred_element_type=F32)
    grad_normal = grad_gated * gate_sig
    grad_gate = grad_gated * normal_out * gate_sig * (1.0 - gate_sig)
    gain_three = jnp.sum(grad_normal * attended * out_scale, axis=0)
    grad_attended = (
        rms_back(attended, out_scale, grad_normal * gain_full[2])
        .astype(B16)
    )
    down_in, proj_in, grad_attended = tied([down_in, proj_in], grad_attended)
    down.accept(down_in)
    proj.accept(proj_in)
    proj_out, grad_attended = tied([proj.payloads()], grad_attended)
    proj_in = proj.swap(proj_out)
    grad_attended = grad_attended.reshape(length, head_count, head_size)
    query_heads = query_act.reshape(length, head_count, head_size)
    key_heads = key_act.reshape(length, head_count, head_size)
    value_heads = value_act.reshape(length, head_count, head_size)
    grad_weights = jnp.einsum(
        "the,she->hts", grad_attended, value_heads, preferred_element_type=F32
    )
    grad_values = jnp.einsum(
        "hts,the->she", weights_low, grad_attended, preferred_element_type=F32
    ).reshape(length, model_width)
    grad_scores = (grad_weights * fading_mask).astype(B16)
    grad_queries = jnp.einsum(
        "hts,she->the", grad_scores, key_heads, preferred_element_type=F32
    ).reshape(length, model_width)
    grad_keys = jnp.einsum(
        "hts,the->she", grad_scores, query_heads, preferred_element_type=F32
    ).reshape(length, model_width)
    grad_mixed = jnp.concatenate(
        [
            jnp.where(query_act > 0, grad_queries, 0.0),
            jnp.where(key_act > 0, grad_keys, 0.0),
            grad_values,
            grad_gate,
        ],
        axis=1,
    ).astype(B16)
    inner = Halving(weight_grad(grad_mixed, normed).reshape(4, model_width, model_width))
    inner_out, grad_mixed = tied([inner.payloads()], grad_mixed)
    inner_in = inner.swap(inner_out)
    one_in, two_in, proj_in, inner_in, grad_mixed = tied([one_in, two_in, proj_in, inner_in], grad_mixed)
    one.accept(one_in)
    two.accept(two_in)
    proj.accept(proj_in)
    inner.accept(inner_in)
    one_out, two_out, proj_out, inner_out, grad_mixed = tied(
        [one.payloads(), two.payloads(), proj.payloads(), inner.payloads()], grad_mixed
    )
    one_in, two_in, proj_in = one.swap(one_out), two.swap(two_out), proj.swap(proj_out)
    inner_in = inner.swap(inner_out)
    grad_normed = jnp.dot(
        jnp.pad(grad_mixed, ((0, 0), (0, model_width))),
        attn_full.reshape(5 * model_width, model_width),
        preferred_element_type=F32,
    )
    gain_one = jnp.sum(grad_normed * inputs * first_scale, axis=0)
    grad_inputs = grad_middle + rms_back(inputs, first_scale, grad_normed * gain_full[0])
    grad_gain = jnp.stack([gain_one, gain_two, gain_three])
    one_in, two_in, proj_in, grad_inputs = tied([one_in, two_in, proj_in], grad_inputs)
    one.accept(one_in)
    two.accept(two_in)
    proj.accept(proj_in)
    inner.accept(inner_in)
    return (grad_inputs, (one, two, down, proj, inner), grad_gain, ffn_down, moments)


def ordered(*values):
    return lax.optimization_barrier(values)


def plane_bits():
    return lax.axis_size("dp").bit_length() - 1


def swap_bit(value, bit):
    count = lax.axis_size("dp")
    return lax.ppermute(value, "dp", [(i, i ^ (1 << bit)) for i in range(count)])


def weight_grad(features, series):
    return lax.dot_general(features, series, TOKENS_OUT, preferred_element_type=F32).astype(B16)


class Halving:
    def __init__(self, grad, sent=None):
        bits = plane_bits()
        self.fixed = sent is not None
        if self.fixed:
            rows, columns = grad.shape
            self.chunk = 2 * rows // lax.axis_size("dp")
            shape = (1,) + (2,) * (bits - 1) + (self.chunk, columns)
            self.first = [sent.reshape(shape)]
            self.parts = [[(grad.reshape(shape), list(range(1, bits))[::-1])]]
        else:
            count, rows, columns = grad.shape
            self.chunk = rows // lax.axis_size("dp")
            self.first = None
            blocks = grad.reshape((count,) + (2,) * bits + (self.chunk, columns))
            self.parts = [[(blocks, list(range(bits))[::-1])]]
        self.orders = [[0]]

    def choose(self, term, dims, bit, other):
        if bit not in dims:
            return term
        if self.fixed:
            index = 1 if other else 0
        else:
            place = (lax.axis_index("dp") >> bit) & 1
            index = 1 - place if other else place
        return lax.dynamic_index_in_dim(term, index, 1 + dims.index(bit), keepdims=False)

    def payloads(self):
        if self.orders == [[]]:
            rest = list(range(1, plane_bits()))
            half = self.chunk // 2
            self.parts = [
                [(t[..., color * half : (color + 1) * half, :], dims) for t, dims in self.parts[0]]
                for color in range(2)
            ]
            self.orders = [rest, rest[::-1]]
        self.bits = [order[0] for order in self.orders]
        if self.first is not None:
            first, self.first = self.first, None
            return first
        return [
            sum(self.choose(t, dims, bit, True).astype(F32) for t, dims in part).astype(B16)
            for part, bit in zip(self.parts, self.bits)
        ]

    def swap(self, payloads):
        return [swap_bit(value, bit) for value, bit in zip(payloads, self.bits)]

    def accept(self, arrived):
        for color, (part, bit) in enumerate(zip(self.parts, self.bits)):
            left = [b for b in part[0][1] if b != bit]
            self.parts[color] = [(self.choose(t, dims, bit, False), left) for t, dims in part]
            self.parts[color].append((arrived[color], left))
            self.orders[color] = self.orders[color][1:]

    def finish(self):
        while len(self.parts) == 1 or self.orders[0]:
            self.accept(self.swap(self.payloads()))
        return jnp.concatenate([sum(t.astype(F32) for t, _ in part).astype(B16) for part in self.parts], axis=1)


def tied(lists, *values):
    flat = ordered(*[v for part in lists for v in part], *values)
    out, at = [], 0
    for part in lists:
        out.append(list(flat[at : at + len(part)]))
        at += len(part)
    return (*out, *flat[at:])


def line_gather(value):
    copies = jnp.broadcast_to(value[None], (lax.axis_size("fsdp"), *value.shape))
    return jnp.swapaxes(lax.all_to_all(copies, "fsdp", 0, 0, tiled=True), 0, 1)


class Gather:
    def __init__(self, line):
        self.count, lines, _, self.columns = line.shape
        rest = list(range(1, plane_bits()))
        self.orders = (rest, rest[::-1])
        self.held, self.axes = [], []
        for color, order in enumerate(self.orders):
            held = line[:, : lines // 2] if color == 0 else line[:, lines // 2 :]
            for step, bit in enumerate(order):
                axis = sorted(order[: step + 1], reverse=True).index(bit)
                if step + 1 < len(order):
                    held = jnp.stack([held, swap_bit(held, bit)], axis=1 + axis)
            self.held.append(held)
            self.axes.append(axis)

    def cross(self):
        self.came = [swap_bit(held, order[-1]) for held, order in zip(self.held, self.orders)]

    def cores(self):
        self.pieces = []
        for held, came in zip(self.held, self.came):
            self.pieces += [held, came, swap_bit(held, 0), swap_bit(came, 0)]

    def natural(self):
        half, own, _ = self.held[0].shape[-3:]
        planes = lax.axis_size("dp")
        whole = jnp.zeros((self.count, planes, 2 * half, own, self.columns), self.held[0].dtype)
        for number in range(4):
            for color, order in enumerate(self.orders):
                piece = self.pieces[4 * color + number]
                bits = sorted(order[:-1], reverse=True)
                base = (1 << order[-1]) * (number % 2) + number // 2
                for index in itertools.product(range(2), repeat=len(bits)):
                    place = base + sum(value << bit for value, bit in zip(index, bits))
                    block = piece[(slice(None), *index)][:, None]
                    where = (0, lax.axis_index("dp") ^ place, color * half, 0, 0)
                    whole = lax.dynamic_update_slice(whole, block, where)
        return whole.reshape(self.count, -1, self.columns)

    def join(self):
        out = []
        for matrix in range(self.count):
            sides = []
            for side in range(2):
                halves = []
                for color, axis in enumerate(self.axes):
                    first = 4 * color + 2 * side
                    pair = [p[matrix] for p in self.pieces[first : first + 2]]
                    halves.append(jnp.stack(pair, axis=axis))
                sides.append(jnp.concatenate(halves, axis=len(self.orders[0])))
            out.append(jnp.stack(sides).reshape(-1, self.columns))
        return out


def gain_gather(value):
    rows, own = value.shape
    total = lax.axis_size("dp") * lax.axis_size("fsdp")
    copies = jnp.broadcast_to(value[None], (total, rows, own))
    every = lax.all_to_all(copies, ("dp", "fsdp"), 0, 0, tiled=True)
    return jnp.transpose(every, (1, 0, 2)).reshape(rows, total * own)


def gain_sum(grad):
    rows, columns = grad.shape
    total = lax.axis_size("dp") * lax.axis_size("fsdp")
    blocks = jnp.transpose(grad.reshape(rows, total, columns // total), (1, 0, 2))
    return jnp.sum(lax.all_to_all(blocks, ("dp", "fsdp"), 0, 0, tiled=True), axis=0)


NS_ROWS = 256


def polynomial_kernel(gram_ref, rows_ref, out_ref, gram, rest_low, poly, poly_low, current):
    size = gram_ref.shape[0]
    count = rows_ref.shape[0]
    blocks = size // NS_ROWS
    parts = count // 2

    def block(i):
        return pl.ds(pl.multiple_of(i * NS_ROWS, NS_ROWS), NS_ROWS)

    def on_diagonal(i):
        row = lax.broadcasted_iota(jnp.int32, (NS_ROWS, size), 0) + i * NS_ROWS
        return row == lax.broadcasted_iota(jnp.int32, (NS_ROWS, size), 1)

    def trace_of(ref):
        def add(i, total):
            return total + jnp.sum(jnp.where(on_diagonal(i), ref[block(i), :], 0.0))

        return lax.fori_loop(0, blocks, add, jnp.float32(0.0))

    square = jnp.full((1, 1), trace_of(gram_ref), F32)
    norm = jnp.sqrt(square) + NS_EPS
    scale = 1.0 / norm

    def start(i, carry):
        gram[block(i), :] = gram_ref[block(i), :] * (scale * scale)
        return carry

    lax.fori_loop(0, blocks, start, 0)
    current[...] = rows_ref[...].astype(F32) * scale

    def step(iteration, trace):
        shift = trace / size
        factor = NS_A + NS_B * shift + NS_C * shift * shift

        def low_rest(i, carry):
            rest_low[block(i), :] = (gram[block(i), :] - jnp.where(on_diagonal(i), shift, 0.0)).astype(B16)
            return carry

        lax.fori_loop(0, blocks, low_rest, 0)

        def polynomial(i, carry):
            eye = on_diagonal(i)
            own = gram[block(i), :]
            rest = own - jnp.where(eye, shift, 0.0)
            squared = jnp.dot(rest_low[block(i), :], rest_low[...], preferred_element_type=F32)
            squared = squared + 2.0 * shift * rest + jnp.where(eye, shift * shift, 0.0)
            value = NS_B * own + NS_C * squared + jnp.where(eye, NS_A - factor, 0.0)
            poly[block(i), :] = value
            poly_low[block(i), :] = value.astype(B16)
            return carry

        lax.fori_loop(0, blocks, polynomial, 0)

        def apply(i, carry):
            where = pl.ds(pl.multiple_of(i * parts, parts), parts)
            value = current[where, :]
            current[where, :] = factor * value + jnp.dot(
                value.astype(B16), poly_low[...], preferred_element_type=F32
            )
            return carry

        lax.fori_loop(0, 2, apply, 0)

        def next_gram(i, total):
            eye = on_diagonal(i)
            rest = gram[block(i), :] - jnp.where(eye, shift, 0.0)
            own = poly[block(i), :]
            half_way = jnp.dot(rest_low[block(i), :], poly_low[...], preferred_element_type=F32)
            half_way = half_way + shift * own + factor * rest
            value = jnp.dot(half_way.astype(B16), poly_low[...], preferred_element_type=F32)
            value = value + (shift * factor) * own + factor * half_way
            value = value + jnp.where(eye, shift * factor * factor, 0.0)
            gram[block(i), :] = value
            return total + jnp.sum(jnp.where(eye, value, 0.0))

        steps = jnp.where(iteration + 1 < NS_STEPS, blocks, 0)
        return lax.fori_loop(0, steps, next_gram, jnp.float32(0.0))

    lax.fori_loop(0, NS_STEPS, step, trace_of(gram))
    out_ref[...] = current[...].astype(B16)


def gram_orthogonalize(rows, gram):
    size = gram.shape[0]
    whole = pltpu.VMEM((size, size), F32)
    low = pltpu.VMEM((size, size), B16)
    return pl.pallas_call(
        polynomial_kernel,
        out_shape=jax.ShapeDtypeStruct(rows.shape, B16),
        in_specs=[pl.BlockSpec(memory_space=pltpu.VMEM)] * 2,
        out_specs=pl.BlockSpec(memory_space=pltpu.VMEM),
        scratch_shapes=[whole, low, whole, low, pltpu.VMEM(rows.shape, F32)],
        compiler_params=pltpu.CompilerParams(vmem_limit_bytes=48 * 1024 * 1024),
        cost_estimate=pl.CostEstimate(flops=30 * size**3, transcendentals=0, bytes_accessed=8 * size * size),
    )(gram, rows)


def one_way(value, bit, lower):
    count = lax.axis_size("dp")
    start = 1 if lower else 0
    return lax.ppermute(
        value, "dp", [(i, i ^ (1 << bit)) for i in range(count) if (i & 1) == start]
    )


def swap_core(value, bit, core):
    count = lax.axis_size("dp")
    return lax.ppermute(value, "dp", [(i, i ^ (1 << bit)) for i in range(count) if (i & 1) == core])


def gather_plane(own, other, core, late=None):
    rest = list(range(1, plane_bits()))
    held = [own[None], other[None]]
    for step in range(len(rest)):
        if late is not None and step + 1 == len(rest):
            held, late = tied([held], late)
        for color in range(2):
            bit = rest[step] if color == 0 else rest[::-1][step]
            held[color] = jnp.concatenate([held[color], swap_core(held[color], bit, core)])
    return held, late


def gram_of(held):
    return sum(
        lax.dot_general(
            part.reshape(-1, part.shape[-1]),
            part.reshape(-1, part.shape[-1]),
            TOKENS_OUT,
            preferred_element_type=F32,
        )
        for part in held
    )


def to_owners(attn, ffn):
    lines = lax.axis_size("fsdp")
    attn_count, small, columns = attn.shape
    ffn_count, large, _ = ffn.shape
    at_one = min(lines, attn_count)
    spare = attn_count - at_one
    top = [ffn]
    if spare:
        top.append(jnp.pad(attn[at_one:], ((0, 0), (0, large - small), (0, 0))))
    if lines > ffn_count + spare:
        top.append(jnp.zeros((lines - ffn_count - spare, large, columns), ffn.dtype))
    low = attn[:at_one]
    if lines > at_one:
        low = jnp.pad(low, ((0, lines - at_one), (0, 0), (0, 0)))
    return jnp.concatenate(top), low


def exchange(top, low):
    large = top.shape[1]
    both = lax.all_to_all(
        jnp.concatenate([top, low], axis=1), "fsdp", split_axis=0, concat_axis=0, tiled=True
    )
    return both[:, :large], both[:, large:]


def from_owners(top, low, ffn_count, attn_count):
    at_one = min(top.shape[0], attn_count)
    spare = attn_count - at_one
    attn = low[:at_one]
    if spare:
        attn = jnp.concatenate([attn, top[ffn_count : ffn_count + spare, : low.shape[1]]])
    return attn, top[:ffn_count]


def owner_momentum(moment, grad):
    return (MOMENT_DECAY * moment.astype(F32) + (1.0 - MOMENT_DECAY) * grad.astype(F32)).astype(B16)


def on_device(
    tokens,
    segment_ids,
    decay_rate,
    cotangent,
    attn_master,
    ffn_master,
    gains,
    attn_moment,
    ffn_moment,
    gain_first,
    gain_second,
):
    attn_low = attn_master.astype(B16)
    ffn_low = ffn_master.astype(B16)
    gain_low = gains.astype(B16)
    attn_line, gain_low = ordered(line_gather(attn_low), gain_low)
    gain_whole = gain_gather(gain_low)
    attn_gather = Gather(attn_line)
    attn_gather.held, up_low = tied([attn_gather.held], ffn_low[:2])
    attn_gather.cross()
    attn_gather.cores()
    up_line = line_gather(up_low)
    one_gather, two_gather = Gather(up_line[:1]), Gather(up_line[1:])
    attn_full = attn_gather.natural()
    moments = to_owners(attn_moment.astype(B16), ffn_moment.astype(B16))
    one_gather.held, two_gather.held, moments, down_low, attn_full = tied(
        [one_gather.held, two_gather.held, moments], ffn_low[2:], attn_full
    )
    one_gather.cross()
    two_gather.cross()
    stored, down_gather, moments, ffn_up = forward(
        tokens,
        segment_ids[0],
        decay_rate,
        attn_full,
        (one_gather, two_gather),
        line_gather(down_low),
        gain_whole,
        moments,
    )
    x_grad, grads, grad_gain, ffn_down, (top_moment, low_moment) = backward(
        stored, cotangent, attn_full, ffn_up, down_gather, moments, gain_whole
    )
    one, two, down, proj, inner = grads
    lines = lax.axis_size("fsdp")
    attn_count, small, columns = attn_master.shape
    ffn_count, large, _ = ffn_master.shape
    block, little = lines * large, lines * small
    middle, product = stored[-6], stored[-1]
    ffn_sums = [value.finish() for value in (one, two, down)]
    proj_sum = proj.finish()
    out = (middle + jnp.dot(product, ffn_down, preferred_element_type=F32)).astype(B16)
    at_one = min(lines, attn_count)
    top_grad = ffn_sums
    if attn_count > at_one:
        spread = jnp.pad(proj_sum.reshape(1, lines, small, columns), ((0, 0), (0, 0), (0, large - small), (0, 0)))
        top_grad.append(spread.reshape(1, block, columns))
    top_grad = jnp.concatenate(top_grad)
    if lines > top_grad.shape[0]:
        top_grad = jnp.pad(top_grad, ((0, lines - top_grad.shape[0]), (0, 0), (0, 0)))
    top_grad = lax.psum_scatter(top_grad, "fsdp", scatter_dimension=0, tiled=True)[0]
    low_grad = inner.finish()
    if attn_count == at_one:
        low_grad = jnp.concatenate([low_grad, proj_sum])
    if lines > low_grad.shape[0]:
        low_grad = jnp.pad(low_grad, ((0, lines - low_grad.shape[0]), (0, 0), (0, 0)))
    top_grad, low_grad = ordered(top_grad, low_grad)
    low_grad = lax.psum_scatter(low_grad, "fsdp", scatter_dimension=0, tiled=True)[0]
    at_core = lax.axis_index("dp") & 1
    big = owner_momentum(top_moment.reshape(block, columns), top_grad)
    big_other = one_way(big, 0, True)
    top_held, low_grad = gather_plane(big, big_other, 0, low_grad)
    top_gram = gram_of(top_held)
    low = owner_momentum(low_moment.reshape(little, columns), low_grad)
    low_other = one_way(low, 0, False)
    low_gram = gram_of(gather_plane(low, low_other, 1)[0])
    gram = jnp.where(at_core == 0, top_gram, low_gram)
    fill = ((0, block - little), (0, 0))
    mine = jnp.concatenate(
        [
            jnp.where(at_core == 0, big, jnp.pad(low, fill)),
            jnp.where(at_core == 0, big_other, jnp.pad(low_other, fill)),
        ]
    )
    result = gram_orthogonalize(mine, gram)
    own, other = result[:block], result[block:]
    back_top = one_way(other, 0, False)
    back_low = one_way(other[:little], 0, True)
    top_orth = jnp.where(at_core == 0, own, back_top).reshape(lines, large, columns)
    low_orth = jnp.where(at_core == 0, back_low, own[:little]).reshape(lines, small, columns)
    attn_orth, ffn_orth = from_owners(*exchange(top_orth, low_orth), ffn_count, attn_count)
    attn_orth, ffn_orth = attn_orth.astype(F32), ffn_orth.astype(F32)
    attn_grad, ffn_grad = from_owners(
        *exchange(top_grad.reshape(lines, large, columns), low_grad.reshape(lines, small, columns)),
        ffn_count,
        attn_count,
    )
    attn_grad, ffn_grad = attn_grad.astype(F32), ffn_grad.astype(F32)
    attn_state = MOMENT_DECAY * attn_moment + (1.0 - MOMENT_DECAY) * attn_grad
    ffn_state = MOMENT_DECAY * ffn_moment + (1.0 - MOMENT_DECAY) * ffn_grad
    gain_grad = gain_sum(grad_gain)
    attn_new = attn_master - LR_MUON * attn_orth
    ffn_new = ffn_master - LR_MUON * math.sqrt(FF / D) * ffn_orth
    first_new = BETA_ONE * gain_first + (1.0 - BETA_ONE) * gain_grad
    second_new = BETA_TWO * gain_second + (1.0 - BETA_TWO) * gain_grad * gain_grad
    gains_new = gains - LR_GAIN * first_new / (jnp.sqrt(second_new) + ADAM_EPS)
    return (
        out,
        x_grad,
        attn_grad,
        ffn_grad,
        gain_grad,
        attn_state,
        ffn_state,
        attn_new,
        ffn_new,
        attn_new.astype(B16),
        ffn_new.astype(B16),
        gains_new,
        first_new,
        second_new,
    )


def solution(mesh):
    return jax.shard_map(
        on_device,
        mesh=mesh,
        in_specs=(
            P(("dp", "fsdp"), None),
            P(("dp", "fsdp"), None),
            P(),
            P(("dp", "fsdp"), None),
            P(None, ("dp", "fsdp"), None),
            P(None, ("dp", "fsdp"), None),
            P(None, ("dp", "fsdp")),
            P(None, ("dp", "fsdp"), None),
            P(None, ("dp", "fsdp"), None),
            P(None, ("dp", "fsdp")),
            P(None, ("dp", "fsdp")),
        ),
        out_specs=(
            P(("dp", "fsdp"), None),
            P(("dp", "fsdp"), None),
            P(None, ("dp", "fsdp"), None),
            P(None, ("dp", "fsdp"), None),
            P(None, ("dp", "fsdp")),
            P(None, ("dp", "fsdp"), None),
            P(None, ("dp", "fsdp"), None),
            P(None, ("dp", "fsdp"), None),
            P(None, ("dp", "fsdp"), None),
            P(None, ("dp", "fsdp"), None),
            P(None, ("dp", "fsdp"), None),
            P(None, ("dp", "fsdp")),
            P(None, ("dp", "fsdp")),
            P(None, ("dp", "fsdp")),
        ),
        check_vma=False,
    )
```

```python
import itertools
import math

import jax
import jax.numpy as jnp
from jax import lax
from jax.experimental import pallas as pl
from jax.experimental.pallas import tpu as pltpu
from jax.sharding import PartitionSpec as P

D = 1024
FF = 2816
NS_STEPS = 5


EPS = 1e-06
NS_EPS = 1e-07
NS_A = 3.4445
NS_B = -4.775
NS_C = 2.0315
LR_MUON = 0.3
LR_GAIN = 0.1
MOMENT_DECAY = 0.5
BETA_ONE = 0.9
BETA_TWO = 0.95
ADAM_EPS = 1e-08
F32 = jnp.float32
B16 = jnp.bfloat16
ROWS_BY_ROWS = (((1,), (1,)), ((), ()))
TOKENS_OUT = (((0,), (0,)), ((), ()))


def rms_scale(series):
    return lax.rsqrt(jnp.mean(series * series, axis=-1, keepdims=True) + EPS)


def rms_back(series, factor, upstream):
    return factor * upstream - series * (factor * factor * factor) * jnp.mean(
        upstream * series, axis=-1, keepdims=True
    )


def decay_mask(segments, decay_rate):
    length = segments.shape[0]
    places = jnp.arange(length, dtype=jnp.int32)
    distance = places[:, None] - places[None, :]
    allowed = (segments[:, None] == segments[None, :]) & (distance >= 0)
    fading = jnp.exp(-decay_rate[:, None, None] * jnp.maximum(distance, 0).astype(F32)[None])
    return jnp.where(allowed[None], fading, 0.0)


def forward(tokens, segments, decay_rate, attn_full, up_gathers, down_low, gain_low, moments):
    length, model_width = tokens.shape
    head_count = decay_rate.shape[0]
    head_size = model_width // head_count
    gain_full = gain_low.astype(F32)
    inputs = tokens.astype(F32)
    first_scale = rms_scale(inputs)
    normed = (inputs * first_scale * gain_full[0]).astype(B16)
    projected = lax.dot_general(
        normed,
        attn_full.reshape(5 * model_width, model_width),
        ROWS_BY_ROWS,
        preferred_element_type=F32,
    )
    query_act = jax.nn.relu(projected[:, :model_width]).astype(B16)
    key_act = jax.nn.relu(projected[:, model_width : 2 * model_width]).astype(B16)
    value_act = projected[:, 2 * model_width : 3 * model_width].astype(B16)
    gate_pre = projected[:, 3 * model_width : 4 * model_width]
    one_gather, two_gather = up_gathers
    one_gather.held, two_gather.held, moments, down_low, query_act, key_act = tied(
        [one_gather.held, two_gather.held, moments], down_low, query_act, key_act
    )
    one_gather.cross()
    two_gather.cross()
    down_line = line_gather(down_low)
    fading_mask = decay_mask(segments, decay_rate)
    query_heads = query_act.reshape(length, head_count, head_size)
    key_heads = key_act.reshape(length, head_count, head_size)
    value_heads = value_act.reshape(length, head_count, head_size)
    scores = jnp.einsum("the,she->hts", query_heads, key_heads, preferred_element_type=F32)
    weights_low = (scores * fading_mask).astype(B16)
    attended = jnp.einsum(
        "hts,she->the", weights_low, value_heads, preferred_element_type=F32
    ).reshape(length, model_width)
    out_scale = rms_scale(attended)
    normal_out = attended * out_scale * gain_full[2]
    gate_sig = jax.nn.sigmoid(gate_pre)
    gated_out = (normal_out * gate_sig).astype(B16)
    one_gather.came, two_gather.came, moments, down_line, gated_out = tied(
        [one_gather.came, two_gather.came, moments], down_line, gated_out
    )
    one_gather.cores()
    two_gather.cores()
    down_gather = Gather(down_line)
    moments = exchange(*moments)
    branch = lax.dot_general(gated_out, attn_full[4], ROWS_BY_ROWS, preferred_element_type=F32)
    middle = inputs + branch
    second_scale = rms_scale(middle)
    normed_two = (middle * second_scale * gain_full[1]).astype(B16)
    one_gather.pieces, two_gather.pieces, down_gather.held, normed_two = tied(
        [one_gather.pieces, two_gather.pieces, down_gather.held], normed_two
    )
    ffn_up = one_gather.join() + two_gather.join()
    down_gather.cross()
    down_gather.cores()
    up_one, up_two = (
        lax.dot_general(normed_two, matrix, ROWS_BY_ROWS, preferred_element_type=F32) for matrix in ffn_up
    )
    product = (up_one * up_two).astype(B16)
    stored = (
        inputs,
        first_scale,
        normed,
        query_act,
        key_act,
        value_act,
        gate_pre,
        fading_mask,
        weights_low,
        attended,
        out_scale,
        normal_out,
        gate_sig,
        gated_out,
        middle,
        second_scale,
        normed_two,
        up_one,
        up_two,
        product,
    )
    return stored, down_gather, moments, ffn_up


def backward(stored, cotangent, attn_full, ffn_up, down_gather, moments, gain_low):
    (
        inputs,
        first_scale,
        normed,
        query_act,
        key_act,
        value_act,
        gate_pre,
        fading_mask,
        weights_low,
        attended,
        out_scale,
        normal_out,
        gate_sig,
        gated_out,
        middle,
        second_scale,
        normed_two,
        up_one,
        up_two,
        product,
    ) = stored
    length, model_width = inputs.shape
    head_count = fading_mask.shape[0]
    head_size = model_width // head_count
    hidden = product.shape[1]
    gain_full = gain_low.astype(F32)
    grad_out = cotangent.astype(F32)
    half = hidden // 2
    down = Halving(
        weight_grad(product[:, :half], cotangent), weight_grad(product[:, half:], cotangent)
    )
    down_out, down_gather.pieces, moments, cotangent = tied(
        [down.payloads(), down_gather.pieces, moments], cotangent
    )
    down_in = down.swap(down_out)
    (ffn_down,) = down_gather.join()
    grad_product = lax.dot_general(cotangent, ffn_down, ROWS_BY_ROWS, preferred_element_type=F32)
    grad_one = (grad_product * up_two).astype(B16)
    grad_two = (grad_product * up_one).astype(B16)
    send_one, send_two = weight_grad(grad_one[:, half:], normed_two), weight_grad(grad_two[:, half:], normed_two)
    down_in, sends, grad_one, grad_two = tied([down_in, [send_one, send_two]], grad_one, grad_two)
    down.accept(down_in)
    one = Halving(weight_grad(grad_one[:, :half], normed_two), sends[0])
    two = Halving(weight_grad(grad_two[:, :half], normed_two), sends[1])
    one_in, two_in = one.swap(one.payloads()), two.swap(two.payloads())
    down_out, grad_one, grad_two = tied([down.payloads()], grad_one, grad_two)
    down_in = down.swap(down_out)
    grad_normed_two = jnp.dot(grad_one, ffn_up[0], preferred_element_type=F32) + jnp.dot(
        grad_two, ffn_up[1], preferred_element_type=F32
    )
    gain_two = jnp.sum(grad_normed_two * middle * second_scale, axis=0)
    grad_middle = grad_out + rms_back(middle, second_scale, grad_normed_two * gain_full[1])
    middle_low = grad_middle.astype(B16)
    down_in, one_in, two_in, middle_low = tied([down_in, one_in, two_in], middle_low)
    down.accept(down_in)
    one.accept(one_in)
    two.accept(two_in)
    down_out, one_out, two_out, middle_low = tied(
        [down.payloads(), one.payloads(), two.payloads()], middle_low
    )
    down_in, one_in, two_in = down.swap(down_out), one.swap(one_out), two.swap(two_out)
    grad_outproj = lax.dot_general(middle_low, gated_out, TOKENS_OUT, preferred_element_type=F32).astype(B16)
    proj = Halving(grad_outproj[None])
    proj_out, middle_low = tied([proj.payloads()], middle_low)
    proj_in = proj.swap(proj_out)
    grad_gated = jnp.dot(middle_low, attn_full[4], preferred_element_type=F32)
    grad_normal = grad_gated * gate_sig
    grad_gate = grad_gated * normal_out * gate_sig * (1.0 - gate_sig)
    gain_three = jnp.sum(grad_normal * attended * out_scale, axis=0)
    grad_attended = (
        rms_back(attended, out_scale, grad_normal * gain_full[2])
        .astype(B16)
    )
    down_in, proj_in, grad_attended = tied([down_in, proj_in], grad_attended)
    down.accept(down_in)
    proj.accept(proj_in)
    proj_out, grad_attended = tied([proj.payloads()], grad_attended)
    proj_in = proj.swap(proj_out)
    grad_attended = grad_attended.reshape(length, head_count, head_size)
    query_heads = query_act.reshape(length, head_count, head_size)
    key_heads = key_act.reshape(length, head_count, head_size)
    value_heads = value_act.reshape(length, head_count, head_size)
    grad_weights = jnp.einsum(
        "the,she->hts", grad_attended, value_heads, preferred_element_type=F32
    )
    grad_values = jnp.einsum(
        "hts,the->she", weights_low, grad_attended, preferred_element_type=F32
    ).reshape(length, model_width)
    grad_scores = (grad_weights * fading_mask).astype(B16)
    grad_queries = jnp.einsum(
        "hts,she->the", grad_scores, key_heads, preferred_element_type=F32
    ).reshape(length, model_width)
    grad_keys = jnp.einsum(
        "hts,the->she", grad_scores, query_heads, preferred_element_type=F32
    ).reshape(length, model_width)
    grad_mixed = jnp.concatenate(
        [
            jnp.where(query_act > 0, grad_queries, 0.0),
            jnp.where(key_act > 0, grad_keys, 0.0),
            grad_values,
            grad_gate,
        ],
        axis=1,
    ).astype(B16)
    inner = Halving(weight_grad(grad_mixed, normed).reshape(4, model_width, model_width))
    inner_out, grad_mixed = tied([inner.payloads()], grad_mixed)
    inner_in = inner.swap(inner_out)
    one_in, two_in, proj_in, inner_in, grad_mixed = tied([one_in, two_in, proj_in, inner_in], grad_mixed)
    one.accept(one_in)
    two.accept(two_in)
    proj.accept(proj_in)
    inner.accept(inner_in)
    one_out, two_out, proj_out, inner_out, grad_mixed = tied(
        [one.payloads(), two.payloads(), proj.payloads(), inner.payloads()], grad_mixed
    )
    one_in, two_in, proj_in = one.swap(one_out), two.swap(two_out), proj.swap(proj_out)
    inner_in = inner.swap(inner_out)
    grad_normed = jnp.dot(
        jnp.pad(grad_mixed, ((0, 0), (0, model_width))),
        attn_full.reshape(5 * model_width, model_width),
        preferred_element_type=F32,
    )
    gain_one = jnp.sum(grad_normed * inputs * first_scale, axis=0)
    grad_inputs = grad_middle + rms_back(inputs, first_scale, grad_normed * gain_full[0])
    grad_gain = jnp.stack([gain_one, gain_two, gain_three])
    one_in, two_in, proj_in, grad_inputs = tied([one_in, two_in, proj_in], grad_inputs)
    one.accept(one_in)
    two.accept(two_in)
    proj.accept(proj_in)
    inner.accept(inner_in)
    return (grad_inputs, (one, two, down, proj, inner), grad_gain, ffn_down, moments)


def ordered(*values):
    return lax.optimization_barrier(values)


def plane_bits():
    return lax.axis_size("dp").bit_length() - 1


def swap_bit(value, bit):
    count = lax.axis_size("dp")
    return lax.ppermute(value, "dp", [(i, i ^ (1 << bit)) for i in range(count)])


def weight_grad(features, series):
    return lax.dot_general(features, series, TOKENS_OUT, preferred_element_type=F32).astype(B16)


class Halving:
    def __init__(self, grad, sent=None):
        bits = plane_bits()
        self.fixed = sent is not None
        if self.fixed:
            rows, columns = grad.shape
            self.chunk = 2 * rows // lax.axis_size("dp")
            shape = (1,) + (2,) * (bits - 1) + (self.chunk, columns)
            self.first = [sent.reshape(shape)]
            self.parts = [[(grad.reshape(shape), list(range(1, bits))[::-1])]]
        else:
            count, rows, columns = grad.shape
            self.chunk = rows // lax.axis_size("dp")
            self.first = None
            blocks = grad.reshape((count,) + (2,) * bits + (self.chunk, columns))
            self.parts = [[(blocks, list(range(bits))[::-1])]]
        self.orders = [[0]]

    def choose(self, term, dims, bit, other):
        if bit not in dims:
            return term
        if self.fixed:
            index = 1 if other else 0
        else:
            place = (lax.axis_index("dp") >> bit) & 1
            index = 1 - place if other else place
        return lax.dynamic_index_in_dim(term, index, 1 + dims.index(bit), keepdims=False)

    def payloads(self):
        if self.orders == [[]]:
            rest = list(range(1, plane_bits()))
            half = self.chunk // 2
            self.parts = [
                [(t[..., color * half : (color + 1) * half, :], dims) for t, dims in self.parts[0]]
                for color in range(2)
            ]
            self.orders = [rest, rest[::-1]]
        self.bits = [order[0] for order in self.orders]
        if self.first is not None:
            first, self.first = self.first, None
            return first
        return [
            sum(self.choose(t, dims, bit, True).astype(F32) for t, dims in part).astype(B16)
            for part, bit in zip(self.parts, self.bits)
        ]

    def swap(self, payloads):
        return [swap_bit(value, bit) for value, bit in zip(payloads, self.bits)]

    def accept(self, arrived):
        for color, (part, bit) in enumerate(zip(self.parts, self.bits)):
            left = [b for b in part[0][1] if b != bit]
            self.parts[color] = [(self.choose(t, dims, bit, False), left) for t, dims in part]
            self.parts[color].append((arrived[color], left))
            self.orders[color] = self.orders[color][1:]

    def finish(self):
        while len(self.parts) == 1 or self.orders[0]:
            self.accept(self.swap(self.payloads()))
        return jnp.concatenate([sum(t.astype(F32) for t, _ in part).astype(B16) for part in self.parts], axis=1)


def tied(lists, *values):
    flat = ordered(*[v for part in lists for v in part], *values)
    out, at = [], 0
    for part in lists:
        out.append(list(flat[at : at + len(part)]))
        at += len(part)
    return (*out, *flat[at:])


def line_gather(value):
    copies = jnp.broadcast_to(value[None], (lax.axis_size("fsdp"), *value.shape))
    return jnp.swapaxes(lax.all_to_all(copies, "fsdp", 0, 0, tiled=True), 0, 1)


class Gather:
    def __init__(self, line):
        self.count, lines, _, self.columns = line.shape
        rest = list(range(1, plane_bits()))
        self.orders = (rest, rest[::-1])
        self.held, self.axes = [], []
        for color, order in enumerate(self.orders):
            held = line[:, : lines // 2] if color == 0 else line[:, lines // 2 :]
            for step, bit in enumerate(order):
                axis = sorted(order[: step + 1], reverse=True).index(bit)
                if step + 1 < len(order):
                    held = jnp.stack([held, swap_bit(held, bit)], axis=1 + axis)
            self.held.append(held)
            self.axes.append(axis)

    def cross(self):
        self.came = [swap_bit(held, order[-1]) for held, order in zip(self.held, self.orders)]

    def cores(self):
        self.pieces = []
        for held, came in zip(self.held, self.came):
            self.pieces += [held, came, swap_bit(held, 0), swap_bit(came, 0)]

    def natural(self):
        half, own, _ = self.held[0].shape[-3:]
        planes = lax.axis_size("dp")
        whole = jnp.zeros((self.count, planes, 2 * half, own, self.columns), self.held[0].dtype)
        for number in range(4):
            for color, order in enumerate(self.orders):
                piece = self.pieces[4 * color + number]
                bits = sorted(order[:-1], reverse=True)
                base = (1 << order[-1]) * (number % 2) + number // 2
                for index in itertools.product(range(2), repeat=len(bits)):
                    place = base + sum(value << bit for value, bit in zip(index, bits))
                    block = piece[(slice(None), *index)][:, None]
                    where = (0, lax.axis_index("dp") ^ place, color * half, 0, 0)
                    whole = lax.dynamic_update_slice(whole, block, where)
        return whole.reshape(self.count, -1, self.columns)

    def join(self):
        out = []
        for matrix in range(self.count):
            sides = []
            for side in range(2):
                halves = []
                for color, axis in enumerate(self.axes):
                    first = 4 * color + 2 * side
                    pair = [p[matrix] for p in self.pieces[first : first + 2]]
                    halves.append(jnp.stack(pair, axis=axis))
                sides.append(jnp.concatenate(halves, axis=len(self.orders[0])))
            out.append(jnp.stack(sides).reshape(-1, self.columns))
        return out


def gain_gather(value):
    rows, own = value.shape
    total = lax.axis_size("dp") * lax.axis_size("fsdp")
    copies = jnp.broadcast_to(value[None], (total, rows, own))
    every = lax.all_to_all(copies, ("dp", "fsdp"), 0, 0, tiled=True)
    return jnp.transpose(every, (1, 0, 2)).reshape(rows, total * own)


def gain_sum(grad):
    rows, columns = grad.shape
    total = lax.axis_size("dp") * lax.axis_size("fsdp")
    blocks = jnp.transpose(grad.reshape(rows, total, columns // total), (1, 0, 2))
    return jnp.sum(lax.all_to_all(blocks, ("dp", "fsdp"), 0, 0, tiled=True), axis=0)


NS_ROWS = 1024


def polynomial_kernel(gram_ref, rows_ref, out_ref, gram, rest_low, poly, poly_low, current):
    size = gram_ref.shape[0]
    blocks = size // NS_ROWS

    def block(i):
        return pl.ds(pl.multiple_of(i * NS_ROWS, NS_ROWS), NS_ROWS)

    def on_diagonal(i):
        row = lax.broadcasted_iota(jnp.int32, (NS_ROWS, size), 0) + i * NS_ROWS
        return row == lax.broadcasted_iota(jnp.int32, (NS_ROWS, size), 1)

    def trace_of(ref):
        def add(i, total):
            return total + jnp.sum(jnp.where(on_diagonal(i), ref[block(i), :], 0.0))

        return lax.fori_loop(0, blocks, add, jnp.float32(0.0))

    square = jnp.full((1, 1), trace_of(gram_ref), F32)
    norm = jnp.sqrt(square) + NS_EPS
    scale = 1.0 / norm

    def start(i, carry):
        gram[block(i), :] = gram_ref[block(i), :] * (scale * scale)
        return carry

    lax.fori_loop(0, blocks, start, 0)
    current[...] = rows_ref[...].astype(F32) * scale

    def step(iteration, trace):
        shift = trace / size
        factor = NS_A + NS_B * shift + NS_C * shift * shift

        def low_rest(i, carry):
            rest_low[block(i), :] = (gram[block(i), :] - jnp.where(on_diagonal(i), shift, 0.0)).astype(B16)
            return carry

        lax.fori_loop(0, blocks, low_rest, 0)

        def polynomial(i, carry):
            eye = on_diagonal(i)
            own = gram[block(i), :]
            rest = own - jnp.where(eye, shift, 0.0)
            squared = jnp.dot(rest_low[block(i), :], rest_low[...], preferred_element_type=F32)
            squared = squared + 2.0 * shift * rest + jnp.where(eye, shift * shift, 0.0)
            value = NS_B * own + NS_C * squared + jnp.where(eye, NS_A - factor, 0.0)
            poly[block(i), :] = value
            poly_low[block(i), :] = value.astype(B16)
            return carry

        lax.fori_loop(0, blocks, polynomial, 0)

        value = current[...]
        current[...] = factor * value + jnp.dot(value.astype(B16), poly_low[...], preferred_element_type=F32)

        def next_gram(i, total):
            eye = on_diagonal(i)
            rest = gram[block(i), :] - jnp.where(eye, shift, 0.0)
            own = poly[block(i), :]
            half_way = jnp.dot(rest_low[block(i), :], poly_low[...], preferred_element_type=F32)
            half_way = half_way + shift * own + factor * rest
            value = jnp.dot(half_way.astype(B16), poly_low[...], preferred_element_type=F32)
            value = value + (shift * factor) * own + factor * half_way
            value = value + jnp.where(eye, shift * factor * factor, 0.0)
            gram[block(i), :] = value
            return total + jnp.sum(jnp.where(eye, value, 0.0))

        steps = jnp.where(iteration + 1 < NS_STEPS, blocks, 0)
        return lax.fori_loop(0, steps, next_gram, jnp.float32(0.0))

    lax.fori_loop(0, NS_STEPS, step, trace_of(gram))
    out_ref[...] = current[...].astype(B16)


def gram_orthogonalize(rows, gram):
    size = gram.shape[0]
    whole = pltpu.VMEM((size, size), F32)
    low = pltpu.VMEM((size, size), B16)
    return pl.pallas_call(
        polynomial_kernel,
        out_shape=jax.ShapeDtypeStruct(rows.shape, B16),
        in_specs=[pl.BlockSpec(memory_space=pltpu.VMEM)] * 2,
        out_specs=pl.BlockSpec(memory_space=pltpu.VMEM),
        scratch_shapes=[whole, low, whole, low, pltpu.VMEM(rows.shape, F32)],
        compiler_params=pltpu.CompilerParams(vmem_limit_bytes=48 * 1024 * 1024),
        cost_estimate=pl.CostEstimate(flops=30 * size**3, transcendentals=0, bytes_accessed=8 * size * size),
    )(gram, rows)


def one_way(value, bit, lower):
    count = lax.axis_size("dp")
    start = 1 if lower else 0
    return lax.ppermute(
        value, "dp", [(i, i ^ (1 << bit)) for i in range(count) if (i & 1) == start]
    )


def swap_core(value, bit, core):
    count = lax.axis_size("dp")
    return lax.ppermute(value, "dp", [(i, i ^ (1 << bit)) for i in range(count) if (i & 1) == core])


def gather_plane(own, other, core, late=None):
    rest = list(range(1, plane_bits()))
    held = [own[None], other[None]]
    for step in range(len(rest)):
        if late is not None and step + 1 == len(rest):
            held, late = tied([held], late)
        for color in range(2):
            bit = rest[step] if color == 0 else rest[::-1][step]
            held[color] = jnp.concatenate([held[color], swap_core(held[color], bit, core)])
    return held, late


def gram_of(held):
    return sum(
        lax.dot_general(
            part.reshape(-1, part.shape[-1]),
            part.reshape(-1, part.shape[-1]),
            TOKENS_OUT,
            preferred_element_type=F32,
        )
        for part in held
    )


def to_owners(attn, ffn):
    lines = lax.axis_size("fsdp")
    attn_count, small, columns = attn.shape
    ffn_count, large, _ = ffn.shape
    at_one = min(lines, attn_count)
    spare = attn_count - at_one
    top = [ffn]
    if spare:
        top.append(jnp.pad(attn[at_one:], ((0, 0), (0, large - small), (0, 0))))
    if lines > ffn_count + spare:
        top.append(jnp.zeros((lines - ffn_count - spare, large, columns), ffn.dtype))
    low = attn[:at_one]
    if lines > at_one:
        low = jnp.pad(low, ((0, lines - at_one), (0, 0), (0, 0)))
    return jnp.concatenate(top), low


def exchange(top, low):
    large = top.shape[1]
    both = lax.all_to_all(
        jnp.concatenate([top, low], axis=1), "fsdp", split_axis=0, concat_axis=0, tiled=True
    )
    return both[:, :large], both[:, large:]


def from_owners(top, low, ffn_count, attn_count):
    at_one = min(top.shape[0], attn_count)
    spare = attn_count - at_one
    attn = low[:at_one]
    if spare:
        attn = jnp.concatenate([attn, top[ffn_count : ffn_count + spare, : low.shape[1]]])
    return attn, top[:ffn_count]


def owner_momentum(moment, grad):
    return (MOMENT_DECAY * moment.astype(F32) + (1.0 - MOMENT_DECAY) * grad.astype(F32)).astype(B16)


def on_device(
    tokens,
    segment_ids,
    decay_rate,
    cotangent,
    attn_master,
    ffn_master,
    gains,
    attn_moment,
    ffn_moment,
    gain_first,
    gain_second,
):
    attn_low = attn_master.astype(B16)
    ffn_low = ffn_master.astype(B16)
    gain_low = gains.astype(B16)
    attn_line, gain_low = ordered(line_gather(attn_low), gain_low)
    gain_whole = gain_gather(gain_low)
    attn_gather = Gather(attn_line)
    attn_gather.held, up_low = tied([attn_gather.held], ffn_low[:2])
    attn_gather.cross()
    attn_gather.cores()
    up_line = line_gather(up_low)
    last, up_line = tied([attn_gather.pieces[3::4]], up_line)
    attn_gather.pieces[3::4] = last
    one_gather, two_gather = Gather(up_line[:1]), Gather(up_line[1:])
    attn_full = attn_gather.natural()
    moments = to_owners(attn_moment.astype(B16), ffn_moment.astype(B16))
    stored, down_gather, moments, ffn_up = forward(
        tokens,
        segment_ids[0],
        decay_rate,
        attn_full,
        (one_gather, two_gather),
        ffn_low[2:],
        gain_whole,
        moments,
    )
    x_grad, grads, grad_gain, ffn_down, (top_moment, low_moment) = backward(
        stored, cotangent, attn_full, ffn_up, down_gather, moments, gain_whole
    )
    one, two, down, proj, inner = grads
    lines = lax.axis_size("fsdp")
    attn_count, small, columns = attn_master.shape
    ffn_count, large, _ = ffn_master.shape
    block, little = lines * large, lines * small
    middle, product = stored[-6], stored[-1]
    ffn_sums = [value.finish() for value in (one, two, down)]
    proj_sum = proj.finish()
    out = (middle + jnp.dot(product, ffn_down, preferred_element_type=F32)).astype(B16)
    at_one = min(lines, attn_count)
    top_grad = ffn_sums
    if attn_count > at_one:
        spread = jnp.pad(proj_sum.reshape(1, lines, small, columns), ((0, 0), (0, 0), (0, large - small), (0, 0)))
        top_grad.append(spread.reshape(1, block, columns))
    top_grad = jnp.concatenate(top_grad)
    if lines > top_grad.shape[0]:
        top_grad = jnp.pad(top_grad, ((0, lines - top_grad.shape[0]), (0, 0), (0, 0)))
    top_grad = lax.psum_scatter(top_grad, "fsdp", scatter_dimension=0, tiled=True)[0]
    low_grad = inner.finish()
    if attn_count == at_one:
        low_grad = jnp.concatenate([low_grad, proj_sum])
    if lines > low_grad.shape[0]:
        low_grad = jnp.pad(low_grad, ((0, lines - low_grad.shape[0]), (0, 0), (0, 0)))
    low_parts = lax.all_to_all(low_grad, "fsdp", split_axis=0, concat_axis=0, tiled=True)
    low_grad = jnp.sum(low_parts.astype(F32), axis=0).astype(B16)
    at_core = lax.axis_index("dp") & 1
    big = owner_momentum(top_moment.reshape(block, columns), top_grad)
    big_other = one_way(big, 0, True)
    top_held, low_grad = gather_plane(big, big_other, 0, low_grad)
    top_gram = gram_of(top_held)
    low = owner_momentum(low_moment.reshape(little, columns), low_grad)
    low_other = one_way(low, 0, False)
    low_gram = gram_of(gather_plane(low, low_other, 1)[0])
    gram = jnp.where(at_core == 0, top_gram, low_gram)
    fill = ((0, block - little), (0, 0))
    mine = jnp.concatenate(
        [
            jnp.where(at_core == 0, big, jnp.pad(low, fill)),
            jnp.where(at_core == 0, big_other, jnp.pad(low_other, fill)),
        ]
    )
    result = gram_orthogonalize(mine, gram)
    own, other = result[:block], result[block:]
    back_top = one_way(other, 0, False)
    back_low = one_way(other[:little], 0, True)
    top_orth = jnp.where(at_core == 0, own, back_top).reshape(lines, large, columns)
    low_orth = jnp.where(at_core == 0, back_low, own[:little]).reshape(lines, small, columns)
    attn_orth, ffn_orth = from_owners(*exchange(top_orth, low_orth), ffn_count, attn_count)
    attn_orth, ffn_orth = attn_orth.astype(F32), ffn_orth.astype(F32)
    attn_grad, ffn_grad = from_owners(
        *exchange(top_grad.reshape(lines, large, columns), low_grad.reshape(lines, small, columns)),
        ffn_count,
        attn_count,
    )
    attn_grad, ffn_grad = attn_grad.astype(F32), ffn_grad.astype(F32)
    attn_state = MOMENT_DECAY * attn_moment + (1.0 - MOMENT_DECAY) * attn_grad
    ffn_state = MOMENT_DECAY * ffn_moment + (1.0 - MOMENT_DECAY) * ffn_grad
    gain_grad = gain_sum(grad_gain)
    attn_new = attn_master - LR_MUON * attn_orth
    ffn_new = ffn_master - LR_MUON * math.sqrt(FF / D) * ffn_orth
    first_new = BETA_ONE * gain_first + (1.0 - BETA_ONE) * gain_grad
    second_new = BETA_TWO * gain_second + (1.0 - BETA_TWO) * gain_grad * gain_grad
    gains_new = gains - LR_GAIN * first_new / (jnp.sqrt(second_new) + ADAM_EPS)
    return (
        out,
        x_grad,
        attn_grad,
        ffn_grad,
        gain_grad,
        attn_state,
        ffn_state,
        attn_new,
        ffn_new,
        attn_new.astype(B16),
        ffn_new.astype(B16),
        gains_new,
        first_new,
        second_new,
    )


def solution(mesh):
    return jax.shard_map(
        on_device,
        mesh=mesh,
        in_specs=(
            P(("dp", "fsdp"), None),
            P(("dp", "fsdp"), None),
            P(),
            P(("dp", "fsdp"), None),
            P(None, ("dp", "fsdp"), None),
            P(None, ("dp", "fsdp"), None),
            P(None, ("dp", "fsdp")),
            P(None, ("dp", "fsdp"), None),
            P(None, ("dp", "fsdp"), None),
            P(None, ("dp", "fsdp")),
            P(None, ("dp", "fsdp")),
        ),
        out_specs=(
            P(("dp", "fsdp"), None),
            P(("dp", "fsdp"), None),
            P(None, ("dp", "fsdp"), None),
            P(None, ("dp", "fsdp"), None),
            P(None, ("dp", "fsdp")),
            P(None, ("dp", "fsdp"), None),
            P(None, ("dp", "fsdp"), None),
            P(None, ("dp", "fsdp"), None),
            P(None, ("dp", "fsdp"), None),
            P(None, ("dp", "fsdp"), None),
            P(None, ("dp", "fsdp"), None),
            P(None, ("dp", "fsdp")),
            P(None, ("dp", "fsdp")),
            P(None, ("dp", "fsdp")),
        ),
        check_vma=False,
    )
```

```python
import itertools
import math

import jax
import jax.numpy as jnp
from jax import lax
from jax.experimental import pallas as pl
from jax.experimental.pallas import tpu as pltpu
from jax.sharding import PartitionSpec as P

D = 1024
FF = 2816
NS_STEPS = 5


EPS = 1e-06
NS_EPS = 1e-07
NS_A = 3.4445
NS_B = -4.775
NS_C = 2.0315
LR_MUON = 0.3
LR_GAIN = 0.1
MOMENT_DECAY = 0.5
BETA_ONE = 0.9
BETA_TWO = 0.95
ADAM_EPS = 1e-08
F32 = jnp.float32
B16 = jnp.bfloat16
ROWS_BY_ROWS = (((1,), (1,)), ((), ()))
TOKENS_OUT = (((0,), (0,)), ((), ()))


def rms_scale(series):
    return lax.rsqrt(jnp.mean(series * series, axis=-1, keepdims=True) + EPS)


def rms_back(series, factor, upstream):
    return factor * upstream - series * (factor * factor * factor) * jnp.mean(
        upstream * series, axis=-1, keepdims=True
    )


def decay_mask(segments, decay_rate):
    length = segments.shape[0]
    places = jnp.arange(length, dtype=jnp.int32)
    distance = places[:, None] - places[None, :]
    allowed = (segments[:, None] == segments[None, :]) & (distance >= 0)
    fading = jnp.exp(-decay_rate[:, None, None] * jnp.maximum(distance, 0).astype(F32)[None])
    return jnp.where(allowed[None], fading, 0.0)


def forward(tokens, segments, decay_rate, attn_full, up_gathers, down_low, gain_low, moments):
    length, model_width = tokens.shape
    head_count = decay_rate.shape[0]
    head_size = model_width // head_count
    gain_full = gain_low.astype(F32)
    inputs = tokens.astype(F32)
    first_scale = rms_scale(inputs)
    normed = (inputs * first_scale * gain_full[0]).astype(B16)
    projected = lax.dot_general(
        normed,
        attn_full.reshape(5 * model_width, model_width),
        ROWS_BY_ROWS,
        preferred_element_type=F32,
    )
    query_act = jax.nn.relu(projected[:, :model_width]).astype(B16)
    key_act = jax.nn.relu(projected[:, model_width : 2 * model_width]).astype(B16)
    value_act = projected[:, 2 * model_width : 3 * model_width].astype(B16)
    gate_pre = projected[:, 3 * model_width : 4 * model_width]
    one_gather, two_gather = up_gathers
    one_gather.held, two_gather.held, moments, down_low, query_act, key_act = tied(
        [one_gather.held, two_gather.held, moments], down_low, query_act, key_act
    )
    one_gather.cross()
    two_gather.cross()
    down_line = line_gather(down_low)
    fading_mask = decay_mask(segments, decay_rate)
    query_heads = query_act.reshape(length, head_count, head_size)
    key_heads = key_act.reshape(length, head_count, head_size)
    value_heads = value_act.reshape(length, head_count, head_size)
    scores = jnp.einsum("the,she->hts", query_heads, key_heads, preferred_element_type=F32)
    weights_low = (scores * fading_mask).astype(B16)
    attended = jnp.einsum(
        "hts,she->the", weights_low, value_heads, preferred_element_type=F32
    ).reshape(length, model_width)
    out_scale = rms_scale(attended)
    normal_out = attended * out_scale * gain_full[2]
    gate_sig = jax.nn.sigmoid(gate_pre)
    gated_out = (normal_out * gate_sig).astype(B16)
    one_gather.came, two_gather.came, moments, down_line, gated_out = tied(
        [one_gather.came, two_gather.came, moments], down_line, gated_out
    )
    one_gather.cores()
    two_gather.cores()
    down_gather = Gather(down_line)
    moments = exchange(*moments)
    branch = lax.dot_general(gated_out, attn_full[4], ROWS_BY_ROWS, preferred_element_type=F32)
    middle = inputs + branch
    second_scale = rms_scale(middle)
    normed_two = (middle * second_scale * gain_full[1]).astype(B16)
    one_gather.pieces, two_gather.pieces, down_gather.held, normed_two = tied(
        [one_gather.pieces, two_gather.pieces, down_gather.held], normed_two
    )
    ffn_up = one_gather.join() + two_gather.join()
    down_gather.cross()
    down_gather.cores()
    up_one, up_two = (
        lax.dot_general(normed_two, matrix, ROWS_BY_ROWS, preferred_element_type=F32) for matrix in ffn_up
    )
    product = (up_one * up_two).astype(B16)
    stored = (
        inputs,
        first_scale,
        normed,
        query_act,
        key_act,
        value_act,
        gate_pre,
        fading_mask,
        weights_low,
        attended,
        out_scale,
        normal_out,
        gate_sig,
        gated_out,
        middle,
        second_scale,
        normed_two,
        up_one,
        up_two,
        product,
    )
    return stored, down_gather, moments, ffn_up


def backward(stored, cotangent, attn_full, ffn_up, down_gather, moments, gain_low):
    (
        inputs,
        first_scale,
        normed,
        query_act,
        key_act,
        value_act,
        gate_pre,
        fading_mask,
        weights_low,
        attended,
        out_scale,
        normal_out,
        gate_sig,
        gated_out,
        middle,
        second_scale,
        normed_two,
        up_one,
        up_two,
        product,
    ) = stored
    length, model_width = inputs.shape
    head_count = fading_mask.shape[0]
    head_size = model_width // head_count
    hidden = product.shape[1]
    gain_full = gain_low.astype(F32)
    grad_out = cotangent.astype(F32)
    half = hidden // 2
    down = Halving(
        weight_grad(product[:, :half], cotangent), weight_grad(product[:, half:], cotangent)
    )
    down_out, down_gather.pieces, moments, cotangent = tied(
        [down.payloads(), down_gather.pieces, moments], cotangent
    )
    down_in = down.swap(down_out)
    (ffn_down,) = down_gather.join()
    grad_product = lax.dot_general(cotangent, ffn_down, ROWS_BY_ROWS, preferred_element_type=F32)
    grad_one = (grad_product * up_two).astype(B16)
    grad_two = (grad_product * up_one).astype(B16)
    send_one, send_two = weight_grad(grad_one[:, half:], normed_two), weight_grad(grad_two[:, half:], normed_two)
    down_in, sends, grad_one, grad_two = tied([down_in, [send_one, send_two]], grad_one, grad_two)
    down.accept(down_in)
    one = Halving(weight_grad(grad_one[:, :half], normed_two), sends[0])
    two = Halving(weight_grad(grad_two[:, :half], normed_two), sends[1])
    one_in, two_in = one.swap(one.payloads()), two.swap(two.payloads())
    down_out, grad_one, grad_two = tied([down.payloads()], grad_one, grad_two)
    down_in = down.swap(down_out)
    grad_normed_two = jnp.dot(grad_one, ffn_up[0], preferred_element_type=F32) + jnp.dot(
        grad_two, ffn_up[1], preferred_element_type=F32
    )
    gain_two = jnp.sum(grad_normed_two * middle * second_scale, axis=0)
    grad_middle = grad_out + rms_back(middle, second_scale, grad_normed_two * gain_full[1])
    middle_low = grad_middle.astype(B16)
    down_in, one_in, two_in, middle_low = tied([down_in, one_in, two_in], middle_low)
    down.accept(down_in)
    one.accept(one_in)
    two.accept(two_in)
    down_out, one_out, two_out, middle_low = tied(
        [down.payloads(), one.payloads(), two.payloads()], middle_low
    )
    down_in, one_in, two_in = down.swap(down_out), one.swap(one_out), two.swap(two_out)
    grad_outproj = lax.dot_general(middle_low, gated_out, TOKENS_OUT, preferred_element_type=F32).astype(B16)
    proj = Halving(grad_outproj[None])
    proj_out, middle_low = tied([proj.payloads()], middle_low)
    proj_in = proj.swap(proj_out)
    grad_gated = jnp.dot(middle_low, attn_full[4], preferred_element_type=F32)
    grad_normal = grad_gated * gate_sig
    grad_gate = grad_gated * normal_out * gate_sig * (1.0 - gate_sig)
    gain_three = jnp.sum(grad_normal * attended * out_scale, axis=0)
    grad_attended = (
        rms_back(attended, out_scale, grad_normal * gain_full[2])
        .astype(B16)
    )
    down_in, one_in, two_in, proj_in, grad_attended = tied([down_in, one_in, two_in, proj_in], grad_attended)
    down.accept(down_in)
    one.accept(one_in)
    two.accept(two_in)
    proj.accept(proj_in)
    one_out, two_out, proj_out, grad_attended = tied(
        [one.payloads(), two.payloads(), proj.payloads()], grad_attended
    )
    one_in, two_in, proj_in = one.swap(one_out), two.swap(two_out), proj.swap(proj_out)
    grad_attended = grad_attended.reshape(length, head_count, head_size)
    query_heads = query_act.reshape(length, head_count, head_size)
    key_heads = key_act.reshape(length, head_count, head_size)
    value_heads = value_act.reshape(length, head_count, head_size)
    grad_weights = jnp.einsum(
        "the,she->hts", grad_attended, value_heads, preferred_element_type=F32
    )
    grad_values = jnp.einsum(
        "hts,the->she", weights_low, grad_attended, preferred_element_type=F32
    ).reshape(length, model_width)
    grad_scores = (grad_weights * fading_mask).astype(B16)
    grad_queries = jnp.einsum(
        "hts,she->the", grad_scores, key_heads, preferred_element_type=F32
    ).reshape(length, model_width)
    grad_keys = jnp.einsum(
        "hts,the->she", grad_scores, query_heads, preferred_element_type=F32
    ).reshape(length, model_width)
    grad_mixed = jnp.concatenate(
        [
            jnp.where(query_act > 0, grad_queries, 0.0),
            jnp.where(key_act > 0, grad_keys, 0.0),
            grad_values,
            grad_gate,
        ],
        axis=1,
    ).astype(B16)
    one_in, two_in, proj_in, grad_mixed = tied([one_in, two_in, proj_in], grad_mixed)
    one.accept(one_in)
    two.accept(two_in)
    proj.accept(proj_in)
    proj_out, grad_mixed = tied([proj.payloads()], grad_mixed)
    proj_in = proj.swap(proj_out)
    inner = Halving(weight_grad(grad_mixed, normed).reshape(4, model_width, model_width))
    inner_out, grad_mixed = tied([inner.payloads()], grad_mixed)
    inner_in = inner.swap(inner_out)
    proj_in, inner_in, grad_mixed = tied([proj_in, inner_in], grad_mixed)
    proj.accept(proj_in)
    inner.accept(inner_in)
    inner_out, grad_mixed = tied([inner.payloads()], grad_mixed)
    inner_in = inner.swap(inner_out)
    grad_normed = jnp.dot(
        jnp.pad(grad_mixed, ((0, 0), (0, model_width))),
        attn_full.reshape(5 * model_width, model_width),
        preferred_element_type=F32,
    )
    gain_one = jnp.sum(grad_normed * inputs * first_scale, axis=0)
    grad_inputs = grad_middle + rms_back(inputs, first_scale, grad_normed * gain_full[0])
    grad_gain = jnp.stack([gain_one, gain_two, gain_three])
    inner.accept(inner_in)
    return (grad_inputs, (one, two, down, proj, inner), grad_gain, ffn_down, moments)


def ordered(*values):
    return lax.optimization_barrier(values)


def plane_bits():
    return lax.axis_size("dp").bit_length() - 1


def swap_bit(value, bit):
    count = lax.axis_size("dp")
    return lax.ppermute(value, "dp", [(i, i ^ (1 << bit)) for i in range(count)])


def weight_grad(features, series):
    return lax.dot_general(features, series, TOKENS_OUT, preferred_element_type=F32).astype(B16)


class Halving:
    def __init__(self, grad, sent=None):
        bits = plane_bits()
        self.fixed = sent is not None
        if self.fixed:
            rows, columns = grad.shape
            self.chunk = 2 * rows // lax.axis_size("dp")
            shape = (1,) + (2,) * (bits - 1) + (self.chunk, columns)
            self.first = [sent.reshape(shape)]
            self.parts = [[(grad.reshape(shape), list(range(1, bits))[::-1])]]
        else:
            count, rows, columns = grad.shape
            self.chunk = rows // lax.axis_size("dp")
            self.first = None
            blocks = grad.reshape((count,) + (2,) * bits + (self.chunk, columns))
            self.parts = [[(blocks, list(range(bits))[::-1])]]
        self.orders = [[0]]

    def choose(self, term, dims, bit, other):
        if bit not in dims:
            return term
        if self.fixed:
            index = 1 if other else 0
        else:
            place = (lax.axis_index("dp") >> bit) & 1
            index = 1 - place if other else place
        return lax.dynamic_index_in_dim(term, index, 1 + dims.index(bit), keepdims=False)

    def payloads(self):
        if self.orders == [[]]:
            rest = list(range(1, plane_bits()))
            half = self.chunk // 2
            self.parts = [
                [(t[..., color * half : (color + 1) * half, :], dims) for t, dims in self.parts[0]]
                for color in range(2)
            ]
            self.orders = [rest, rest[::-1]]
        self.bits = [order[0] for order in self.orders]
        if self.first is not None:
            first, self.first = self.first, None
            return first
        return [
            sum(self.choose(t, dims, bit, True).astype(F32) for t, dims in part).astype(B16)
            for part, bit in zip(self.parts, self.bits)
        ]

    def swap(self, payloads):
        return [swap_bit(value, bit) for value, bit in zip(payloads, self.bits)]

    def accept(self, arrived):
        for color, (part, bit) in enumerate(zip(self.parts, self.bits)):
            left = [b for b in part[0][1] if b != bit]
            self.parts[color] = [(self.choose(t, dims, bit, False), left) for t, dims in part]
            self.parts[color].append((arrived[color], left))
            self.orders[color] = self.orders[color][1:]

    def finish(self):
        while len(self.parts) == 1 or self.orders[0]:
            self.accept(self.swap(self.payloads()))
        return jnp.concatenate([sum(t.astype(F32) for t, _ in part).astype(B16) for part in self.parts], axis=1)


def tied(lists, *values):
    flat = ordered(*[v for part in lists for v in part], *values)
    out, at = [], 0
    for part in lists:
        out.append(list(flat[at : at + len(part)]))
        at += len(part)
    return (*out, *flat[at:])


def line_gather(value):
    copies = jnp.broadcast_to(value[None], (lax.axis_size("fsdp"), *value.shape))
    return jnp.swapaxes(lax.all_to_all(copies, "fsdp", 0, 0, tiled=True), 0, 1)


class Gather:
    def __init__(self, line):
        self.count, lines, _, self.columns = line.shape
        rest = list(range(1, plane_bits()))
        self.orders = (rest, rest[::-1])
        self.held, self.axes = [], []
        for color, order in enumerate(self.orders):
            held = line[:, : lines // 2] if color == 0 else line[:, lines // 2 :]
            for step, bit in enumerate(order):
                axis = sorted(order[: step + 1], reverse=True).index(bit)
                if step + 1 < len(order):
                    held = jnp.stack([held, swap_bit(held, bit)], axis=1 + axis)
            self.held.append(held)
            self.axes.append(axis)

    def cross(self):
        self.came = [swap_bit(held, order[-1]) for held, order in zip(self.held, self.orders)]

    def cores(self):
        self.pieces = []
        for held, came in zip(self.held, self.came):
            self.pieces += [held, came, swap_bit(held, 0), swap_bit(came, 0)]

    def natural(self):
        half, own, _ = self.held[0].shape[-3:]
        planes = lax.axis_size("dp")
        whole = jnp.zeros((self.count, planes, 2 * half, own, self.columns), self.held[0].dtype)
        for number in range(4):
            for color, order in enumerate(self.orders):
                piece = self.pieces[4 * color + number]
                bits = sorted(order[:-1], reverse=True)
                base = (1 << order[-1]) * (number % 2) + number // 2
                for index in itertools.product(range(2), repeat=len(bits)):
                    place = base + sum(value << bit for value, bit in zip(index, bits))
                    block = piece[(slice(None), *index)][:, None]
                    where = (0, lax.axis_index("dp") ^ place, color * half, 0, 0)
                    whole = lax.dynamic_update_slice(whole, block, where)
        return whole.reshape(self.count, -1, self.columns)

    def join(self):
        out = []
        for matrix in range(self.count):
            sides = []
            for side in range(2):
                halves = []
                for color, axis in enumerate(self.axes):
                    first = 4 * color + 2 * side
                    pair = [p[matrix] for p in self.pieces[first : first + 2]]
                    halves.append(jnp.stack(pair, axis=axis))
                sides.append(jnp.concatenate(halves, axis=len(self.orders[0])))
            out.append(jnp.stack(sides).reshape(-1, self.columns))
        return out


def gain_gather(value):
    rows, own = value.shape
    total = lax.axis_size("dp") * lax.axis_size("fsdp")
    copies = jnp.broadcast_to(value[None], (total, rows, own))
    every = lax.all_to_all(copies, ("dp", "fsdp"), 0, 0, tiled=True)
    return jnp.transpose(every, (1, 0, 2)).reshape(rows, total * own)


def gain_sum(grad):
    rows, columns = grad.shape
    total = lax.axis_size("dp") * lax.axis_size("fsdp")
    blocks = jnp.transpose(grad.reshape(rows, total, columns // total), (1, 0, 2))
    return jnp.sum(lax.all_to_all(blocks, ("dp", "fsdp"), 0, 0, tiled=True), axis=0)


NS_ROWS = 1024


def polynomial_kernel(gram_ref, rows_ref, out_ref, gram, rest_low, poly, poly_low, current):
    size = gram_ref.shape[0]
    blocks = size // NS_ROWS

    def block(i):
        return pl.ds(pl.multiple_of(i * NS_ROWS, NS_ROWS), NS_ROWS)

    def on_diagonal(i):
        row = lax.broadcasted_iota(jnp.int32, (NS_ROWS, size), 0) + i * NS_ROWS
        return row == lax.broadcasted_iota(jnp.int32, (NS_ROWS, size), 1)

    def trace_of(ref):
        def add(i, total):
            return total + jnp.sum(jnp.where(on_diagonal(i), ref[block(i), :], 0.0))

        return lax.fori_loop(0, blocks, add, jnp.float32(0.0))

    square = jnp.full((1, 1), trace_of(gram_ref), F32)
    norm = jnp.sqrt(square) + NS_EPS
    scale = 1.0 / norm

    def start(i, carry):
        gram[block(i), :] = gram_ref[block(i), :] * (scale * scale)
        return carry

    lax.fori_loop(0, blocks, start, 0)
    current[...] = rows_ref[...].astype(F32) * scale

    def step(iteration, trace):
        shift = trace / size
        factor = NS_A + NS_B * shift + NS_C * shift * shift

        def low_rest(i, carry):
            rest_low[block(i), :] = (gram[block(i), :] - jnp.where(on_diagonal(i), shift, 0.0)).astype(B16)
            return carry

        lax.fori_loop(0, blocks, low_rest, 0)

        def polynomial(i, carry):
            eye = on_diagonal(i)
            own = gram[block(i), :]
            rest = own - jnp.where(eye, shift, 0.0)
            squared = jnp.dot(rest_low[block(i), :], rest_low[...], preferred_element_type=F32)
            squared = squared + 2.0 * shift * rest + jnp.where(eye, shift * shift, 0.0)
            value = NS_B * own + NS_C * squared + jnp.where(eye, NS_A - factor, 0.0)
            poly[block(i), :] = value
            poly_low[block(i), :] = value.astype(B16)
            return carry

        lax.fori_loop(0, blocks, polynomial, 0)

        value = current[...]
        current[...] = factor * value + jnp.dot(value.astype(B16), poly_low[...], preferred_element_type=F32)

        def next_gram(i, total):
            eye = on_diagonal(i)
            rest = gram[block(i), :] - jnp.where(eye, shift, 0.0)
            own = poly[block(i), :]
            half_way = jnp.dot(rest_low[block(i), :], poly_low[...], preferred_element_type=F32)
            half_way = half_way + shift * own + factor * rest
            value = jnp.dot(half_way.astype(B16), poly_low[...], preferred_element_type=F32)
            value = value + (shift * factor) * own + factor * half_way
            value = value + jnp.where(eye, shift * factor * factor, 0.0)
            gram[block(i), :] = value
            return total + jnp.sum(jnp.where(eye, value, 0.0))

        steps = jnp.where(iteration + 1 < NS_STEPS, blocks, 0)
        return lax.fori_loop(0, steps, next_gram, jnp.float32(0.0))

    lax.fori_loop(0, NS_STEPS, step, trace_of(gram))
    out_ref[...] = current[...].astype(B16)


def gram_orthogonalize(rows, gram):
    size = gram.shape[0]
    whole = pltpu.VMEM((size, size), F32)
    low = pltpu.VMEM((size, size), B16)
    return pl.pallas_call(
        polynomial_kernel,
        out_shape=jax.ShapeDtypeStruct(rows.shape, B16),
        in_specs=[pl.BlockSpec(memory_space=pltpu.VMEM)] * 2,
        out_specs=pl.BlockSpec(memory_space=pltpu.VMEM),
        scratch_shapes=[whole, low, whole, low, pltpu.VMEM(rows.shape, F32)],
        compiler_params=pltpu.CompilerParams(vmem_limit_bytes=48 * 1024 * 1024),
        cost_estimate=pl.CostEstimate(flops=30 * size**3, transcendentals=0, bytes_accessed=8 * size * size),
    )(gram, rows)


def one_way(value, bit, lower):
    count = lax.axis_size("dp")
    start = 1 if lower else 0
    return lax.ppermute(
        value, "dp", [(i, i ^ (1 << bit)) for i in range(count) if (i & 1) == start]
    )


def swap_core(value, bit, core):
    count = lax.axis_size("dp")
    return lax.ppermute(value, "dp", [(i, i ^ (1 << bit)) for i in range(count) if (i & 1) == core])


def gather_plane(own, other, core, late=None):
    rest = list(range(1, plane_bits()))
    held = [own[None], other[None]]
    for step in range(len(rest)):
        if late is not None and step + 1 == len(rest):
            held, late = tied([held], late)
        for color in range(2):
            bit = rest[step] if color == 0 else rest[::-1][step]
            held[color] = jnp.concatenate([held[color], swap_core(held[color], bit, core)])
    return held, late


def gram_of(held):
    return sum(
        lax.dot_general(
            part.reshape(-1, part.shape[-1]),
            part.reshape(-1, part.shape[-1]),
            TOKENS_OUT,
            preferred_element_type=F32,
        )
        for part in held
    )


def to_owners(attn, ffn):
    lines = lax.axis_size("fsdp")
    attn_count, small, columns = attn.shape
    ffn_count, large, _ = ffn.shape
    at_one = min(lines, attn_count)
    spare = attn_count - at_one
    top = [ffn]
    if spare:
        top.append(jnp.pad(attn[at_one:], ((0, 0), (0, large - small), (0, 0))))
    if lines > ffn_count + spare:
        top.append(jnp.zeros((lines - ffn_count - spare, large, columns), ffn.dtype))
    low = attn[:at_one]
    if lines > at_one:
        low = jnp.pad(low, ((0, lines - at_one), (0, 0), (0, 0)))
    return jnp.concatenate(top), low


def exchange(top, low):
    large = top.shape[1]
    both = lax.all_to_all(
        jnp.concatenate([top, low], axis=1), "fsdp", split_axis=0, concat_axis=0, tiled=True
    )
    return both[:, :large], both[:, large:]


def from_owners(top, low, ffn_count, attn_count):
    at_one = min(top.shape[0], attn_count)
    spare = attn_count - at_one
    attn = low[:at_one]
    if spare:
        attn = jnp.concatenate([attn, top[ffn_count : ffn_count + spare, : low.shape[1]]])
    return attn, top[:ffn_count]


def owner_momentum(moment, grad):
    return (MOMENT_DECAY * moment.astype(F32) + (1.0 - MOMENT_DECAY) * grad.astype(F32)).astype(B16)


def on_device(
    tokens,
    segment_ids,
    decay_rate,
    cotangent,
    attn_master,
    ffn_master,
    gains,
    attn_moment,
    ffn_moment,
    gain_first,
    gain_second,
):
    attn_low = attn_master.astype(B16)
    ffn_low = ffn_master.astype(B16)
    gain_low = gains.astype(B16)
    attn_line, gain_low = ordered(line_gather(attn_low), gain_low)
    gain_whole = gain_gather(gain_low)
    attn_gather = Gather(attn_line)
    attn_gather.held, up_low = tied([attn_gather.held], ffn_low[:2])
    attn_gather.cross()
    attn_gather.cores()
    up_line = line_gather(up_low)
    last, up_line = tied([attn_gather.pieces[3::4]], up_line)
    attn_gather.pieces[3::4] = last
    one_gather, two_gather = Gather(up_line[:1]), Gather(up_line[1:])
    attn_full = attn_gather.natural()
    moments = to_owners(attn_moment.astype(B16), ffn_moment.astype(B16))
    stored, down_gather, moments, ffn_up = forward(
        tokens,
        segment_ids[0],
        decay_rate,
        attn_full,
        (one_gather, two_gather),
        ffn_low[2:],
        gain_whole,
        moments,
    )
    x_grad, grads, grad_gain, ffn_down, (top_moment, low_moment) = backward(
        stored, cotangent, attn_full, ffn_up, down_gather, moments, gain_whole
    )
    one, two, down, proj, inner = grads
    lines = lax.axis_size("fsdp")
    attn_count, small, columns = attn_master.shape
    ffn_count, large, _ = ffn_master.shape
    block, little = lines * large, lines * small
    middle, product = stored[-6], stored[-1]
    ffn_sums = [value.finish() for value in (one, two, down)]
    proj_sum = proj.finish()
    out = (middle + jnp.dot(product, ffn_down, preferred_element_type=F32)).astype(B16)
    at_one = min(lines, attn_count)
    top_grad = ffn_sums
    if attn_count > at_one:
        spread = jnp.pad(proj_sum.reshape(1, lines, small, columns), ((0, 0), (0, 0), (0, large - small), (0, 0)))
        top_grad.append(spread.reshape(1, block, columns))
    top_grad = jnp.concatenate(top_grad)
    if lines > top_grad.shape[0]:
        top_grad = jnp.pad(top_grad, ((0, lines - top_grad.shape[0]), (0, 0), (0, 0)))
    top_grad = lax.psum_scatter(top_grad, "fsdp", scatter_dimension=0, tiled=True)[0]
    low_grad = inner.finish()
    if attn_count == at_one:
        low_grad = jnp.concatenate([low_grad, proj_sum])
    if lines > low_grad.shape[0]:
        low_grad = jnp.pad(low_grad, ((0, lines - low_grad.shape[0]), (0, 0), (0, 0)))
    low_parts = lax.all_to_all(low_grad, "fsdp", split_axis=0, concat_axis=0, tiled=True)
    low_grad = jnp.sum(low_parts.astype(F32), axis=0).astype(B16)
    at_core = lax.axis_index("dp") & 1
    big = owner_momentum(top_moment.reshape(block, columns), top_grad)
    big_other = one_way(big, 0, True)
    top_held, low_grad = gather_plane(big, big_other, 0, low_grad)
    top_gram = gram_of(top_held)
    low = owner_momentum(low_moment.reshape(little, columns), low_grad)
    low_other = one_way(low, 0, False)
    low_gram = gram_of(gather_plane(low, low_other, 1)[0])
    gram = jnp.where(at_core == 0, top_gram, low_gram)
    fill = ((0, block - little), (0, 0))
    mine = jnp.concatenate(
        [
            jnp.where(at_core == 0, big, jnp.pad(low, fill)),
            jnp.where(at_core == 0, big_other, jnp.pad(low_other, fill)),
        ]
    )
    result = gram_orthogonalize(mine, gram)
    own, other = result[:block], result[block:]
    back_top = one_way(other, 0, False)
    back_low = one_way(other[:little], 0, True)
    top_orth = jnp.where(at_core == 0, own, back_top).reshape(lines, large, columns)
    low_orth = jnp.where(at_core == 0, back_low, own[:little]).reshape(lines, small, columns)
    attn_orth, ffn_orth = from_owners(*exchange(top_orth, low_orth), ffn_count, attn_count)
    attn_orth, ffn_orth = attn_orth.astype(F32), ffn_orth.astype(F32)
    attn_grad, ffn_grad = from_owners(
        *exchange(top_grad.reshape(lines, large, columns), low_grad.reshape(lines, small, columns)),
        ffn_count,
        attn_count,
    )
    attn_grad, ffn_grad = attn_grad.astype(F32), ffn_grad.astype(F32)
    attn_state = MOMENT_DECAY * attn_moment + (1.0 - MOMENT_DECAY) * attn_grad
    ffn_state = MOMENT_DECAY * ffn_moment + (1.0 - MOMENT_DECAY) * ffn_grad
    gain_grad = gain_sum(grad_gain)
    attn_new = attn_master - LR_MUON * attn_orth
    ffn_new = ffn_master - LR_MUON * math.sqrt(FF / D) * ffn_orth
    first_new = BETA_ONE * gain_first + (1.0 - BETA_ONE) * gain_grad
    second_new = BETA_TWO * gain_second + (1.0 - BETA_TWO) * gain_grad * gain_grad
    gains_new = gains - LR_GAIN * first_new / (jnp.sqrt(second_new) + ADAM_EPS)
    return (
        out,
        x_grad,
        attn_grad,
        ffn_grad,
        gain_grad,
        attn_state,
        ffn_state,
        attn_new,
        ffn_new,
        attn_new.astype(B16),
        ffn_new.astype(B16),
        gains_new,
        first_new,
        second_new,
    )


def solution(mesh):
    return jax.shard_map(
        on_device,
        mesh=mesh,
        in_specs=(
            P(("dp", "fsdp"), None),
            P(("dp", "fsdp"), None),
            P(),
            P(("dp", "fsdp"), None),
            P(None, ("dp", "fsdp"), None),
            P(None, ("dp", "fsdp"), None),
            P(None, ("dp", "fsdp")),
            P(None, ("dp", "fsdp"), None),
            P(None, ("dp", "fsdp"), None),
            P(None, ("dp", "fsdp")),
            P(None, ("dp", "fsdp")),
        ),
        out_specs=(
            P(("dp", "fsdp"), None),
            P(("dp", "fsdp"), None),
            P(None, ("dp", "fsdp"), None),
            P(None, ("dp", "fsdp"), None),
            P(None, ("dp", "fsdp")),
            P(None, ("dp", "fsdp"), None),
            P(None, ("dp", "fsdp"), None),
            P(None, ("dp", "fsdp"), None),
            P(None, ("dp", "fsdp"), None),
            P(None, ("dp", "fsdp"), None),
            P(None, ("dp", "fsdp"), None),
            P(None, ("dp", "fsdp")),
            P(None, ("dp", "fsdp")),
            P(None, ("dp", "fsdp")),
        ),
        check_vma=False,
    )
```

```python
import itertools
import math

import jax
import jax.numpy as jnp
from jax import lax
from jax.experimental import pallas as pl
from jax.experimental.pallas import tpu as pltpu
from jax.sharding import PartitionSpec as P

D = 1024
FF = 2816
NS_STEPS = 5


EPS = 1e-06
NS_EPS = 1e-07
NS_A = 3.4445
NS_B = -4.775
NS_C = 2.0315
LR_MUON = 0.3
LR_GAIN = 0.1
MOMENT_DECAY = 0.5
BETA_ONE = 0.9
BETA_TWO = 0.95
ADAM_EPS = 1e-08
F32 = jnp.float32
B16 = jnp.bfloat16
ROWS_BY_ROWS = (((1,), (1,)), ((), ()))
TOKENS_OUT = (((0,), (0,)), ((), ()))


def rms_scale(series):
    return lax.rsqrt(jnp.mean(series * series, axis=-1, keepdims=True) + EPS)


def rms_back(series, factor, upstream):
    return factor * upstream - series * (factor * factor * factor) * jnp.mean(
        upstream * series, axis=-1, keepdims=True
    )


def decay_mask(segments, decay_rate):
    length = segments.shape[0]
    places = jnp.arange(length, dtype=jnp.int32)
    distance = places[:, None] - places[None, :]
    allowed = (segments[:, None] == segments[None, :]) & (distance >= 0)
    fading = jnp.exp(-decay_rate[:, None, None] * jnp.maximum(distance, 0).astype(F32)[None])
    return jnp.where(allowed[None], fading, 0.0)


def forward(tokens, segments, decay_rate, attn_full, up_gathers, down_low, gain_low, moments):
    length, model_width = tokens.shape
    head_count = decay_rate.shape[0]
    head_size = model_width // head_count
    gain_full = gain_low.astype(F32)
    inputs = tokens.astype(F32)
    first_scale = rms_scale(inputs)
    normed = (inputs * first_scale * gain_full[0]).astype(B16)
    projected = lax.dot_general(
        normed,
        attn_full.reshape(5 * model_width, model_width),
        ROWS_BY_ROWS,
        preferred_element_type=F32,
    )
    query_act = jax.nn.relu(projected[:, :model_width]).astype(B16)
    key_act = jax.nn.relu(projected[:, model_width : 2 * model_width]).astype(B16)
    value_act = projected[:, 2 * model_width : 3 * model_width].astype(B16)
    gate_pre = projected[:, 3 * model_width : 4 * model_width]
    one_gather, two_gather = up_gathers
    one_gather.held, two_gather.held, moments, down_low, query_act, key_act = tied(
        [one_gather.held, two_gather.held, moments], down_low, query_act, key_act
    )
    one_gather.cross()
    two_gather.cross()
    down_line = line_gather(down_low)
    fading_mask = decay_mask(segments, decay_rate)
    query_heads = query_act.reshape(length, head_count, head_size)
    key_heads = key_act.reshape(length, head_count, head_size)
    value_heads = value_act.reshape(length, head_count, head_size)
    scores = jnp.einsum("the,she->hts", query_heads, key_heads, preferred_element_type=F32)
    weights_low = (scores * fading_mask).astype(B16)
    attended = jnp.einsum(
        "hts,she->the", weights_low, value_heads, preferred_element_type=F32
    ).reshape(length, model_width)
    out_scale = rms_scale(attended)
    normal_out = attended * out_scale * gain_full[2]
    gate_sig = jax.nn.sigmoid(gate_pre)
    gated_out = (normal_out * gate_sig).astype(B16)
    one_gather.came, two_gather.came, moments, down_line, gated_out = tied(
        [one_gather.came, two_gather.came, moments], down_line, gated_out
    )
    one_gather.cores()
    two_gather.cores()
    down_gather = Gather(down_line)
    moments = exchange(*moments)
    branch = lax.dot_general(gated_out, attn_full[4], ROWS_BY_ROWS, preferred_element_type=F32)
    middle = inputs + branch
    second_scale = rms_scale(middle)
    normed_two = (middle * second_scale * gain_full[1]).astype(B16)
    one_gather.pieces, two_gather.pieces, down_gather.held, normed_two = tied(
        [one_gather.pieces, two_gather.pieces, down_gather.held], normed_two
    )
    ffn_up = one_gather.join() + two_gather.join()
    down_gather.cross()
    down_gather.cores()
    up_one, up_two = (
        lax.dot_general(normed_two, matrix, ROWS_BY_ROWS, preferred_element_type=F32) for matrix in ffn_up
    )
    product = (up_one * up_two).astype(B16)
    stored = (
        inputs,
        first_scale,
        normed,
        query_act,
        key_act,
        value_act,
        gate_pre,
        fading_mask,
        weights_low,
        attended,
        out_scale,
        normal_out,
        gate_sig,
        gated_out,
        middle,
        second_scale,
        normed_two,
        up_one,
        up_two,
        product,
    )
    return stored, down_gather, moments, ffn_up


def backward(stored, cotangent, attn_full, ffn_up, down_gather, moments, gain_low):
    (
        inputs,
        first_scale,
        normed,
        query_act,
        key_act,
        value_act,
        gate_pre,
        fading_mask,
        weights_low,
        attended,
        out_scale,
        normal_out,
        gate_sig,
        gated_out,
        middle,
        second_scale,
        normed_two,
        up_one,
        up_two,
        product,
    ) = stored
    length, model_width = inputs.shape
    head_count = fading_mask.shape[0]
    head_size = model_width // head_count
    hidden = product.shape[1]
    gain_full = gain_low.astype(F32)
    grad_out = cotangent.astype(F32)
    half = hidden // 2
    down = Halving(
        weight_grad(product[:, :half], cotangent), weight_grad(product[:, half:], cotangent)
    )
    down_out, down_gather.pieces, moments, cotangent = tied(
        [down.payloads(), down_gather.pieces, moments], cotangent
    )
    down_in = down.swap(down_out)
    (ffn_down,) = down_gather.join()
    grad_product = lax.dot_general(cotangent, ffn_down, ROWS_BY_ROWS, preferred_element_type=F32)
    grad_one = (grad_product * up_two).astype(B16)
    grad_two = (grad_product * up_one).astype(B16)
    send_one, send_two = weight_grad(grad_one[:, half:], normed_two), weight_grad(grad_two[:, half:], normed_two)
    down_in, sends, grad_one, grad_two = tied([down_in, [send_one, send_two]], grad_one, grad_two)
    down.accept(down_in)
    one = Halving(weight_grad(grad_one[:, :half], normed_two), sends[0])
    two = Halving(weight_grad(grad_two[:, :half], normed_two), sends[1])
    one_in, two_in = one.swap(one.payloads()), two.swap(two.payloads())
    down_out, grad_one, grad_two = tied([down.payloads()], grad_one, grad_two)
    down_in = down.swap(down_out)
    grad_normed_two = jnp.dot(grad_one, ffn_up[0], preferred_element_type=F32) + jnp.dot(
        grad_two, ffn_up[1], preferred_element_type=F32
    )
    gain_two = jnp.sum(grad_normed_two * middle * second_scale, axis=0)
    grad_middle = grad_out + rms_back(middle, second_scale, grad_normed_two * gain_full[1])
    middle_low = grad_middle.astype(B16)
    down_in, one_in, two_in, middle_low = tied([down_in, one_in, two_in], middle_low)
    down.accept(down_in)
    one.accept(one_in)
    two.accept(two_in)
    down_out, one_out, two_out, middle_low = tied(
        [down.payloads(), one.payloads(), two.payloads()], middle_low
    )
    down_in, one_in, two_in = down.swap(down_out), one.swap(one_out), two.swap(two_out)
    grad_outproj = lax.dot_general(middle_low, gated_out, TOKENS_OUT, preferred_element_type=F32).astype(B16)
    proj = Halving(grad_outproj[None])
    proj_out, middle_low = tied([proj.payloads()], middle_low)
    proj_in = proj.swap(proj_out)
    grad_gated = jnp.dot(middle_low, attn_full[4], preferred_element_type=F32)
    grad_normal = grad_gated * gate_sig
    grad_gate = grad_gated * normal_out * gate_sig * (1.0 - gate_sig)
    gain_three = jnp.sum(grad_normal * attended * out_scale, axis=0)
    grad_attended = (
        rms_back(attended, out_scale, grad_normal * gain_full[2])
        .astype(B16)
    )
    down_in, one_in, two_in, proj_in, grad_attended = tied([down_in, one_in, two_in, proj_in], grad_attended)
    down.accept(down_in)
    one.accept(one_in)
    two.accept(two_in)
    proj.accept(proj_in)
    one_out, two_out, proj_out, grad_attended = tied(
        [one.payloads(), two.payloads(), proj.payloads()], grad_attended
    )
    one_in, two_in, proj_in = one.swap(one_out), two.swap(two_out), proj.swap(proj_out)
    grad_attended = grad_attended.reshape(length, head_count, head_size)
    query_heads = query_act.reshape(length, head_count, head_size)
    key_heads = key_act.reshape(length, head_count, head_size)
    value_heads = value_act.reshape(length, head_count, head_size)
    grad_weights = jnp.einsum(
        "the,she->hts", grad_attended, value_heads, preferred_element_type=F32
    )
    grad_values = jnp.einsum(
        "hts,the->she", weights_low, grad_attended, preferred_element_type=F32
    ).reshape(length, model_width)
    grad_scores = (grad_weights * fading_mask).astype(B16)
    grad_queries = jnp.einsum(
        "hts,she->the", grad_scores, key_heads, preferred_element_type=F32
    ).reshape(length, model_width)
    grad_keys = jnp.einsum(
        "hts,the->she", grad_scores, query_heads, preferred_element_type=F32
    ).reshape(length, model_width)
    grad_mixed = jnp.concatenate(
        [
            jnp.where(query_act > 0, grad_queries, 0.0),
            jnp.where(key_act > 0, grad_keys, 0.0),
            grad_values,
            grad_gate,
        ],
        axis=1,
    ).astype(B16)
    one_in, two_in, proj_in, grad_mixed = tied([one_in, two_in, proj_in], grad_mixed)
    one.accept(one_in)
    two.accept(two_in)
    proj.accept(proj_in)
    proj_out, grad_mixed = tied([proj.payloads()], grad_mixed)
    proj_in = proj.swap(proj_out)
    inner = Halving(weight_grad(grad_mixed, normed).reshape(4, model_width, model_width))
    inner_out, grad_mixed = tied([inner.payloads()], grad_mixed)
    inner_in = inner.swap(inner_out)
    proj_in, inner_in, grad_mixed = tied([proj_in, inner_in], grad_mixed)
    proj.accept(proj_in)
    inner.accept(inner_in)
    inner_out, grad_mixed = tied([inner.payloads()], grad_mixed)
    inner_in = inner.swap(inner_out)
    grad_normed = jnp.dot(
        jnp.pad(grad_mixed, ((0, 0), (0, model_width))),
        attn_full.reshape(5 * model_width, model_width),
        preferred_element_type=F32,
    )
    gain_one = jnp.sum(grad_normed * inputs * first_scale, axis=0)
    grad_inputs = grad_middle + rms_back(inputs, first_scale, grad_normed * gain_full[0])
    grad_gain = jnp.stack([gain_one, gain_two, gain_three])
    inner.accept(inner_in)
    return (grad_inputs, (one, two, down, proj, inner), grad_gain, ffn_down, moments)


def ordered(*values):
    return lax.optimization_barrier(values)


def plane_bits():
    return lax.axis_size("dp").bit_length() - 1


def swap_bit(value, bit):
    count = lax.axis_size("dp")
    return lax.ppermute(value, "dp", [(i, i ^ (1 << bit)) for i in range(count)])


def weight_grad(features, series):
    return lax.dot_general(features, series, TOKENS_OUT, preferred_element_type=F32).astype(B16)


class Halving:
    def __init__(self, grad, sent=None):
        bits = plane_bits()
        self.fixed = sent is not None
        if self.fixed:
            rows, columns = grad.shape
            self.chunk = 2 * rows // lax.axis_size("dp")
            shape = (1,) + (2,) * (bits - 1) + (self.chunk, columns)
            self.first = [sent.reshape(shape)]
            self.parts = [[(grad.reshape(shape), list(range(1, bits))[::-1])]]
        else:
            count, rows, columns = grad.shape
            self.chunk = rows // lax.axis_size("dp")
            self.first = None
            blocks = grad.reshape((count,) + (2,) * bits + (self.chunk, columns))
            self.parts = [[(blocks, list(range(bits))[::-1])]]
        self.orders = [[0]]

    def choose(self, term, dims, bit, other):
        if bit not in dims:
            return term
        if self.fixed:
            index = 1 if other else 0
        else:
            place = (lax.axis_index("dp") >> bit) & 1
            index = 1 - place if other else place
        return lax.dynamic_index_in_dim(term, index, 1 + dims.index(bit), keepdims=False)

    def payloads(self):
        if self.orders == [[]]:
            rest = list(range(1, plane_bits()))
            half = self.chunk // 2
            self.parts = [
                [(t[..., color * half : (color + 1) * half, :], dims) for t, dims in self.parts[0]]
                for color in range(2)
            ]
            self.orders = [rest, rest[::-1]]
        self.bits = [order[0] for order in self.orders]
        if self.first is not None:
            first, self.first = self.first, None
            return first
        return [
            sum(self.choose(t, dims, bit, True).astype(F32) for t, dims in part).astype(B16)
            for part, bit in zip(self.parts, self.bits)
        ]

    def swap(self, payloads):
        return [swap_bit(value, bit) for value, bit in zip(payloads, self.bits)]

    def accept(self, arrived):
        for color, (part, bit) in enumerate(zip(self.parts, self.bits)):
            left = [b for b in part[0][1] if b != bit]
            self.parts[color] = [(self.choose(t, dims, bit, False), left) for t, dims in part]
            self.parts[color].append((arrived[color], left))
            self.orders[color] = self.orders[color][1:]

    def finish(self):
        while len(self.parts) == 1 or self.orders[0]:
            self.accept(self.swap(self.payloads()))
        return jnp.concatenate([sum(t.astype(F32) for t, _ in part).astype(B16) for part in self.parts], axis=1)


def tied(lists, *values):
    flat = ordered(*[v for part in lists for v in part], *values)
    out, at = [], 0
    for part in lists:
        out.append(list(flat[at : at + len(part)]))
        at += len(part)
    return (*out, *flat[at:])


def line_gather(value):
    copies = jnp.broadcast_to(value[None], (lax.axis_size("fsdp"), *value.shape))
    return jnp.swapaxes(lax.all_to_all(copies, "fsdp", 0, 0, tiled=True), 0, 1)


class Gather:
    def __init__(self, line):
        self.count, lines, _, self.columns = line.shape
        rest = list(range(1, plane_bits()))
        self.orders = (rest, rest[::-1])
        self.held, self.axes = [], []
        for color, order in enumerate(self.orders):
            held = line[:, : lines // 2] if color == 0 else line[:, lines // 2 :]
            for step, bit in enumerate(order):
                axis = sorted(order[: step + 1], reverse=True).index(bit)
                if step + 1 < len(order):
                    held = jnp.stack([held, swap_bit(held, bit)], axis=1 + axis)
            self.held.append(held)
            self.axes.append(axis)

    def cross(self):
        self.came = [swap_bit(held, order[-1]) for held, order in zip(self.held, self.orders)]

    def cores(self):
        self.pieces = []
        for held, came in zip(self.held, self.came):
            self.pieces += [held, came, swap_bit(held, 0), swap_bit(came, 0)]

    def natural(self):
        half, own, _ = self.held[0].shape[-3:]
        planes = lax.axis_size("dp")
        whole = jnp.zeros((self.count, planes, 2 * half, own, self.columns), self.held[0].dtype)
        for number in range(4):
            for color, order in enumerate(self.orders):
                piece = self.pieces[4 * color + number]
                bits = sorted(order[:-1], reverse=True)
                base = (1 << order[-1]) * (number % 2) + number // 2
                for index in itertools.product(range(2), repeat=len(bits)):
                    place = base + sum(value << bit for value, bit in zip(index, bits))
                    block = piece[(slice(None), *index)][:, None]
                    where = (0, lax.axis_index("dp") ^ place, color * half, 0, 0)
                    whole = lax.dynamic_update_slice(whole, block, where)
        return whole.reshape(self.count, -1, self.columns)

    def join(self):
        out = []
        for matrix in range(self.count):
            sides = []
            for side in range(2):
                halves = []
                for color, axis in enumerate(self.axes):
                    first = 4 * color + 2 * side
                    pair = [p[matrix] for p in self.pieces[first : first + 2]]
                    halves.append(jnp.stack(pair, axis=axis))
                sides.append(jnp.concatenate(halves, axis=len(self.orders[0])))
            out.append(jnp.stack(sides).reshape(-1, self.columns))
        return out


def gain_gather(value):
    rows, own = value.shape
    total = lax.axis_size("dp") * lax.axis_size("fsdp")
    copies = jnp.broadcast_to(value[None], (total, rows, own))
    every = lax.all_to_all(copies, ("dp", "fsdp"), 0, 0, tiled=True)
    return jnp.transpose(every, (1, 0, 2)).reshape(rows, total * own)


def gain_sum(grad):
    rows, columns = grad.shape
    total = lax.axis_size("dp") * lax.axis_size("fsdp")
    blocks = jnp.transpose(grad.reshape(rows, total, columns // total), (1, 0, 2))
    return jnp.sum(lax.all_to_all(blocks, ("dp", "fsdp"), 0, 0, tiled=True), axis=0)


NS_ROWS = 1024


def polynomial_kernel(gram_ref, rows_ref, out_ref, gram, rest_low, poly, poly_low, current):
    size = gram_ref.shape[0]
    blocks = size // NS_ROWS

    def block(i):
        return pl.ds(pl.multiple_of(i * NS_ROWS, NS_ROWS), NS_ROWS)

    def on_diagonal(i):
        row = lax.broadcasted_iota(jnp.int32, (NS_ROWS, size), 0) + i * NS_ROWS
        return row == lax.broadcasted_iota(jnp.int32, (NS_ROWS, size), 1)

    def trace_of(ref):
        def add(i, total):
            return total + jnp.sum(jnp.where(on_diagonal(i), ref[block(i), :], 0.0))

        return lax.fori_loop(0, blocks, add, jnp.float32(0.0))

    square = jnp.full((1, 1), trace_of(gram_ref), F32)
    norm = jnp.sqrt(square) + NS_EPS
    scale = 1.0 / norm

    def start(i, carry):
        gram[block(i), :] = gram_ref[block(i), :] * (scale * scale)
        return carry

    lax.fori_loop(0, blocks, start, 0)
    current[...] = rows_ref[...].astype(F32) * scale

    def step(iteration, trace):
        shift = trace / size
        factor = NS_A + NS_B * shift + NS_C * shift * shift

        def low_rest(i, carry):
            rest_low[block(i), :] = (gram[block(i), :] - jnp.where(on_diagonal(i), shift, 0.0)).astype(B16)
            return carry

        lax.fori_loop(0, blocks, low_rest, 0)

        def polynomial(i, carry):
            eye = on_diagonal(i)
            own = gram[block(i), :]
            rest = own - jnp.where(eye, shift, 0.0)
            squared = jnp.dot(rest_low[block(i), :], rest_low[...], preferred_element_type=F32)
            squared = squared + 2.0 * shift * rest + jnp.where(eye, shift * shift, 0.0)
            value = NS_B * own + NS_C * squared + jnp.where(eye, NS_A - factor, 0.0)
            poly[block(i), :] = value
            poly_low[block(i), :] = value.astype(B16)
            return carry

        lax.fori_loop(0, blocks, polynomial, 0)

        value = current[...]
        current[...] = factor * value + jnp.dot(value.astype(B16), poly_low[...], preferred_element_type=F32)

        def next_gram(i, total):
            eye = on_diagonal(i)
            rest = gram[block(i), :] - jnp.where(eye, shift, 0.0)
            own = poly[block(i), :]
            half_way = jnp.dot(rest_low[block(i), :], poly_low[...], preferred_element_type=F32)
            half_way = half_way + shift * own + factor * rest
            value = jnp.dot(half_way.astype(B16), poly_low[...], preferred_element_type=F32)
            value = value + (shift * factor) * own + factor * half_way
            value = value + jnp.where(eye, shift * factor * factor, 0.0)
            gram[block(i), :] = value
            return total + jnp.sum(jnp.where(eye, value, 0.0))

        steps = jnp.where(iteration + 1 < NS_STEPS, blocks, 0)
        return lax.fori_loop(0, steps, next_gram, jnp.float32(0.0))

    lax.fori_loop(0, NS_STEPS, step, trace_of(gram))
    out_ref[...] = current[...].astype(B16)


def gram_orthogonalize(rows, gram):
    size = gram.shape[0]
    whole = pltpu.VMEM((size, size), F32)
    low = pltpu.VMEM((size, size), B16)
    return pl.pallas_call(
        polynomial_kernel,
        out_shape=jax.ShapeDtypeStruct(rows.shape, B16),
        in_specs=[pl.BlockSpec(memory_space=pltpu.VMEM)] * 2,
        out_specs=pl.BlockSpec(memory_space=pltpu.VMEM),
        scratch_shapes=[whole, low, whole, low, pltpu.VMEM(rows.shape, F32)],
        compiler_params=pltpu.CompilerParams(vmem_limit_bytes=48 * 1024 * 1024),
        cost_estimate=pl.CostEstimate(flops=30 * size**3, transcendentals=0, bytes_accessed=8 * size * size),
    )(gram, rows)


def one_way(value, bit, lower):
    count = lax.axis_size("dp")
    start = 1 if lower else 0
    return lax.ppermute(
        value, "dp", [(i, i ^ (1 << bit)) for i in range(count) if (i & 1) == start]
    )


def swap_core(value, bit, core):
    count = lax.axis_size("dp")
    return lax.ppermute(value, "dp", [(i, i ^ (1 << bit)) for i in range(count) if (i & 1) == core])


def gather_plane(own, other, core, late=None):
    rest = list(range(1, plane_bits()))
    held = [own[None], other[None]]
    for step in range(len(rest)):
        if late is not None and step + 1 == len(rest):
            held, late = tied([held], late)
        for color in range(2):
            bit = rest[step] if color == 0 else rest[::-1][step]
            held[color] = jnp.concatenate([held[color], swap_core(held[color], bit, core)])
    return held, late


def gram_of(held):
    return sum(
        lax.dot_general(
            part.reshape(-1, part.shape[-1]),
            part.reshape(-1, part.shape[-1]),
            TOKENS_OUT,
            preferred_element_type=F32,
        )
        for part in held
    )


def to_owners(attn, ffn):
    lines = lax.axis_size("fsdp")
    attn_count, small, columns = attn.shape
    ffn_count, large, _ = ffn.shape
    at_one = min(lines, attn_count)
    spare = attn_count - at_one
    top = [ffn]
    if spare:
        top.append(jnp.pad(attn[at_one:], ((0, 0), (0, large - small), (0, 0))))
    if lines > ffn_count + spare:
        top.append(jnp.zeros((lines - ffn_count - spare, large, columns), ffn.dtype))
    low = attn[:at_one]
    if lines > at_one:
        low = jnp.pad(low, ((0, lines - at_one), (0, 0), (0, 0)))
    return jnp.concatenate(top), low


def exchange(top, low):
    large = top.shape[1]
    both = lax.all_to_all(
        jnp.concatenate([top, low], axis=1), "fsdp", split_axis=0, concat_axis=0, tiled=True
    )
    return both[:, :large], both[:, large:]


def from_owners(top, low, ffn_count, attn_count):
    at_one = min(top.shape[0], attn_count)
    spare = attn_count - at_one
    attn = low[:at_one]
    if spare:
        attn = jnp.concatenate([attn, top[ffn_count : ffn_count + spare, : low.shape[1]]])
    return attn, top[:ffn_count]


def owner_momentum(moment, grad):
    return (MOMENT_DECAY * moment.astype(F32) + (1.0 - MOMENT_DECAY) * grad.astype(F32)).astype(B16)


def on_device(
    tokens,
    segment_ids,
    decay_rate,
    cotangent,
    attn_master,
    ffn_master,
    gains,
    attn_moment,
    ffn_moment,
    gain_first,
    gain_second,
):
    attn_low = attn_master.astype(B16)
    ffn_low = ffn_master.astype(B16)
    gain_low = gains.astype(B16)
    attn_line, gain_low = ordered(line_gather(attn_low), gain_low)
    gain_whole = gain_gather(gain_low)
    attn_gather = Gather(attn_line)
    attn_gather.held, up_low = tied([attn_gather.held], ffn_low[:2])
    attn_gather.cross()
    attn_gather.cores()
    up_line = line_gather(up_low)
    last, up_line = tied([attn_gather.pieces[3::4]], up_line)
    attn_gather.pieces[3::4] = last
    one_gather, two_gather = Gather(up_line[:1]), Gather(up_line[1:])
    attn_full = attn_gather.natural()
    moments = to_owners(attn_moment.astype(B16), ffn_moment.astype(B16))
    stored, down_gather, moments, ffn_up = forward(
        tokens,
        segment_ids[0],
        decay_rate,
        attn_full,
        (one_gather, two_gather),
        ffn_low[2:],
        gain_whole,
        moments,
    )
    x_grad, grads, grad_gain, ffn_down, (top_moment, low_moment) = backward(
        stored, cotangent, attn_full, ffn_up, down_gather, moments, gain_whole
    )
    one, two, down, proj, inner = grads
    lines = lax.axis_size("fsdp")
    attn_count, small, columns = attn_master.shape
    ffn_count, large, _ = ffn_master.shape
    block, little = lines * large, lines * small
    middle, product = stored[-6], stored[-1]
    ffn_sums = [value.finish() for value in (one, two, down)]
    proj_sum = proj.finish()
    out = (middle + jnp.dot(product, ffn_down, preferred_element_type=F32)).astype(B16)
    at_one = min(lines, attn_count)
    top_grad = ffn_sums
    if attn_count > at_one:
        spread = jnp.pad(proj_sum.reshape(1, lines, small, columns), ((0, 0), (0, 0), (0, large - small), (0, 0)))
        top_grad.append(spread.reshape(1, block, columns))
    top_grad = jnp.concatenate(top_grad)
    if lines > top_grad.shape[0]:
        top_grad = jnp.pad(top_grad, ((0, lines - top_grad.shape[0]), (0, 0), (0, 0)))
    top_grad = lax.psum_scatter(top_grad, "fsdp", scatter_dimension=0, tiled=True)[0]
    low_grad = inner.finish()
    if attn_count == at_one:
        low_grad = jnp.concatenate([low_grad, proj_sum])
    if lines > low_grad.shape[0]:
        low_grad = jnp.pad(low_grad, ((0, lines - low_grad.shape[0]), (0, 0), (0, 0)))
    low_parts = lax.all_to_all(low_grad, "fsdp", split_axis=0, concat_axis=0, tiled=True)
    low_grad = jnp.sum(low_parts.astype(F32), axis=0).astype(B16)
    at_core = lax.axis_index("dp") & 1
    big = owner_momentum(top_moment.reshape(block, columns), top_grad)
    big_other = one_way(big, 0, True)
    top_held, _ = gather_plane(big, big_other, 0)
    top_gram = gram_of(top_held)
    low = owner_momentum(low_moment.reshape(little, columns), low_grad)
    low_other = one_way(low, 0, False)
    low_gram = gram_of(gather_plane(low, low_other, 1)[0])
    gram = jnp.where(at_core == 0, top_gram, low_gram)
    fill = ((0, block - little), (0, 0))
    mine = jnp.concatenate(
        [
            jnp.where(at_core == 0, big, jnp.pad(low, fill)),
            jnp.where(at_core == 0, big_other, jnp.pad(low_other, fill)),
        ]
    )
    result = gram_orthogonalize(mine, gram)
    own, other = result[:block], result[block:]
    back_top = one_way(other, 0, False)
    back_low = one_way(other[:little], 0, True)
    top_orth = jnp.where(at_core == 0, own, back_top).reshape(lines, large, columns)
    low_orth = jnp.where(at_core == 0, back_low, own[:little]).reshape(lines, small, columns)
    attn_orth, ffn_orth = from_owners(*exchange(top_orth, low_orth), ffn_count, attn_count)
    attn_orth, ffn_orth = attn_orth.astype(F32), ffn_orth.astype(F32)
    attn_grad, ffn_grad = from_owners(
        *exchange(top_grad.reshape(lines, large, columns), low_grad.reshape(lines, small, columns)),
        ffn_count,
        attn_count,
    )
    attn_grad, ffn_grad = attn_grad.astype(F32), ffn_grad.astype(F32)
    attn_state = MOMENT_DECAY * attn_moment + (1.0 - MOMENT_DECAY) * attn_grad
    ffn_state = MOMENT_DECAY * ffn_moment + (1.0 - MOMENT_DECAY) * ffn_grad
    gain_grad = gain_sum(grad_gain)
    attn_new = attn_master - LR_MUON * attn_orth
    ffn_new = ffn_master - LR_MUON * math.sqrt(FF / D) * ffn_orth
    first_new = BETA_ONE * gain_first + (1.0 - BETA_ONE) * gain_grad
    second_new = BETA_TWO * gain_second + (1.0 - BETA_TWO) * gain_grad * gain_grad
    gains_new = gains - LR_GAIN * first_new / (jnp.sqrt(second_new) + ADAM_EPS)
    return (
        out,
        x_grad,
        attn_grad,
        ffn_grad,
        gain_grad,
        attn_state,
        ffn_state,
        attn_new,
        ffn_new,
        attn_new.astype(B16),
        ffn_new.astype(B16),
        gains_new,
        first_new,
        second_new,
    )


def solution(mesh):
    return jax.shard_map(
        on_device,
        mesh=mesh,
        in_specs=(
            P(("dp", "fsdp"), None),
            P(("dp", "fsdp"), None),
            P(),
            P(("dp", "fsdp"), None),
            P(None, ("dp", "fsdp"), None),
            P(None, ("dp", "fsdp"), None),
            P(None, ("dp", "fsdp")),
            P(None, ("dp", "fsdp"), None),
            P(None, ("dp", "fsdp"), None),
            P(None, ("dp", "fsdp")),
            P(None, ("dp", "fsdp")),
        ),
        out_specs=(
            P(("dp", "fsdp"), None),
            P(("dp", "fsdp"), None),
            P(None, ("dp", "fsdp"), None),
            P(None, ("dp", "fsdp"), None),
            P(None, ("dp", "fsdp")),
            P(None, ("dp", "fsdp"), None),
            P(None, ("dp", "fsdp"), None),
            P(None, ("dp", "fsdp"), None),
            P(None, ("dp", "fsdp"), None),
            P(None, ("dp", "fsdp"), None),
            P(None, ("dp", "fsdp"), None),
            P(None, ("dp", "fsdp")),
            P(None, ("dp", "fsdp")),
            P(None, ("dp", "fsdp")),
        ),
        check_vma=False,
    )
```
